32 devices in a mesh: facet: 8 (over y, x, core), slab: 4 (over z).
Axes of the slice: x: 2, y: 2, z: 4, core: 2. Of those that a mesh axis runs over, the one named last changes fastest.
Arguments:
- slab: bfloat16 [2, 8, 4096, 256], P(None, 'facet', 'slab'), may hold values from -6 to 6
- facet_offset: int32 [8], P('facet'), may hold values from 0 to 28672
- subgrid_offset: int32 [8], replicated, may hold values from 0 to 28672
- vis_cell: int32 [4, 8, 32768], P('slab', 'facet'), may hold values from 0 to 16383
- vis_value: float32 [2, 4, 8, 32768], P(None, 'slab', 'facet'), may hold values from -6 to 6
- vis_weight: float32 [4, 8, 32768], P('slab', 'facet'), may hold values from 0.1 to 1
Outputs:
- residual: float32 [2, 4, 512, 256], P(None, 'slab', 'facet')
- facet_update: float32 [2, 8, 4096, 256], P(None, 'facet', 'slab')
The draws below stay inside these ranges and needn't reach their ends.
All inputs are finite; a program needn't handle non-finite values.
Results may differ from the reference program's by a relative error of at most 0.0041.
Values may be sent and summed in bfloat16 or wider, within the bound.
A program may use at most 64 MiB of HBM per device.

```python
import math
import jax
import jax.numpy as jnp
from jax import lax

IMAGE = 32768
FY = 4096
XW = 256
SG = 256
UVSTEP = 16
SUBGRIDS = 8
FACETS = 8
SLABS = 4
SGR = 64
OWN = 64
VIS_DEV = 32768
N_FACET = 8
N_SLAB = 4


def touch_ends(drawn, stream_key, smallest, high):
    place = [jax.random.randint(jax.random.fold_in(stream_key, axis), (), 0, length) for axis, length in enumerate(drawn.shape)]
    longest = drawn.shape.index(max(drawn.shape))
    neighbour = place[:longest] + [(place[longest] + 1) % drawn.shape[longest]] + place[longest + 1:]
    return drawn.at[tuple(place)].set(smallest).at[tuple(neighbour)].set(high)


def shard_levels(key, dims, cuts, smallest, high):
    gain, own = 1.0, jax.random.fold_in(key, 6)
    for axis_at, blocks in cuts:
        draws = jnp.exp(jax.random.uniform(jax.random.fold_in(own, axis_at), (blocks,), jnp.float32, smallest / len(cuts), high / len(cuts)))
        gain = gain * jnp.repeat(draws, dims[axis_at] // blocks).reshape([-1 if axis == axis_at else 1 for axis in range(len(dims))])
    return gain


def scatter_about(rng, shape, scale, most, split=(), kind=jnp.bfloat16):
    drawn = scale * jax.random.normal(rng, shape, jnp.float32)
    if split:
        drawn = drawn * shard_levels(rng, shape, split, -0.22, 0.18)
    return jnp.clip(drawn, -most, most).astype(kind)


def setup_inputs(seed: int = 0) -> dict:
    keys = jax.random.split(jax.random.key(seed), 7)
    return {
        "slab": scatter_about(keys[0], (2, FACETS, FY, XW), 1.0, 6.0, ((1, 8), (2, 4))),
        "facet_offset": touch_ends(jax.random.randint(keys[1], (FACETS,), 0, IMAGE - FY + 1), jax.random.fold_in(keys[1], 1), 0, IMAGE - FY).astype(jnp.int32),
        "subgrid_offset": touch_ends(jax.random.randint(keys[2], (SUBGRIDS,), 0, IMAGE - UVSTEP * SG + 1), jax.random.fold_in(keys[2], 1), 0, IMAGE - UVSTEP * SG).astype(jnp.int32),
        "vis_cell": touch_ends(jax.random.randint(keys[3], (SLABS, FACETS, VIS_DEV), 0, OWN * XW), jax.random.fold_in(keys[3], 1), 0, (OWN * XW) - 1).astype(jnp.int32),
        "vis_value": scatter_about(keys[4], (2, SLABS, FACETS, VIS_DEV), 1.0, 6.0, ((1, 4), (2, 8)), jnp.float32),
        "vis_weight": jnp.clip(jnp.exp(math.log(1.0) - 2.3025851 * jax.random.uniform(keys[5], (SLABS, FACETS, VIS_DEV), jnp.float32) ** shard_levels(keys[5], (SLABS, FACETS, VIS_DEV), ((0, 4), (1, 8)), -0.2, 0.2)), 0.1, 1.0),
    }


def phase_tables(first_row, local_rows, subgrid_offset):
    freq = subgrid_offset[:, None] + UVSTEP * jnp.arange(SG, dtype=jnp.int32)[None, :]
    places = first_row + jnp.arange(local_rows, dtype=jnp.int32)
    turns = (freq % IMAGE)[:, :, None] * (places % IMAGE)[None, None, :] % IMAGE
    angle = turns.astype(jnp.float32) * (2.0 * math.pi / IMAGE)
    return (jnp.cos(angle).astype(jnp.bfloat16), (-jnp.sin(angle)).astype(jnp.bfloat16))

def reference(slab, facet_offset, subgrid_offset, vis_cell, vis_value, vis_weight):
    scale_fwd = 1.0 / math.sqrt(FY * FACETS)
    scale_back = 1.0 / math.sqrt(SUBGRIDS * SG)

    def forward_step(total, inputs):
        offset, piece = inputs
        tab_real, tab_imag = phase_tables(offset, FY, subgrid_offset)
        tab_real = tab_real.astype(jnp.float32)
        tab_imag = tab_imag.astype(jnp.float32)
        part_real = piece[0].astype(jnp.float32)
        part_imag = piece[1].astype(jnp.float32)
        real = jnp.einsum('skl,lx->skx', tab_real, part_real) - jnp.einsum('skl,lx->skx', tab_imag, part_imag)
        imag = jnp.einsum('skl,lx->skx', tab_real, part_imag) + jnp.einsum('skl,lx->skx', tab_imag, part_real)
        return (total + jnp.stack([real, imag]), None)
    start = jnp.zeros((2, SUBGRIDS, SG, XW), jnp.float32)
    model, _ = lax.scan(forward_step, start, (facet_offset, jnp.moveaxis(slab, 1, 0)))
    model = model * scale_fwd
    model_flat = model.reshape(2, SUBGRIDS, N_SLAB, SGR, XW).transpose(0, 2, 1, 3, 4).reshape(2, -1)
    cells_block = OWN * XW
    base = (jnp.arange(N_SLAB, dtype=jnp.int32)[:, None] * N_FACET + jnp.arange(N_FACET, dtype=jnp.int32)[None, :]) * cells_block
    index = (base[:, :, None] + vis_cell).reshape(-1)
    weighted = (vis_weight[None] * vis_value).reshape(2, -1)
    gridded = jnp.zeros((2, N_SLAB * N_FACET * cells_block), jnp.float32).at[:, index].add(weighted)
    weight_sum = jnp.zeros((N_SLAB * N_FACET * cells_block,), jnp.float32).at[index].add(vis_weight.reshape(-1))
    residual = (gridded - weight_sum[None, :] * model_flat).reshape(2, N_SLAB, SUBGRIDS * SGR, XW)
    sent = residual.astype(jnp.bfloat16)
    whole = sent.reshape(2, N_SLAB, SUBGRIDS, SGR, XW).transpose(0, 2, 1, 3, 4).reshape(2, SUBGRIDS, SG, XW)
    whole = whole.astype(jnp.float32)

    def adjoint_step(offset):
        tab_real, tab_imag = phase_tables(offset, FY, subgrid_offset)
        tab_real = tab_real.astype(jnp.float32)
        tab_imag = tab_imag.astype(jnp.float32)
        real = jnp.einsum('skl,skx->lx', tab_real, whole[0]) + jnp.einsum('skl,skx->lx', tab_imag, whole[1])
        imag = jnp.einsum('skl,skx->lx', tab_real, whole[1]) - jnp.einsum('skl,skx->lx', tab_imag, whole[0])
        return jnp.stack([real, imag]) * scale_back
    updates = lax.map(adjoint_step, facet_offset)
    facet_update = jnp.moveaxis(updates, 0, 1)
    return (residual, facet_update)
```

```python
import functools
import math

import jax
import jax.numpy as jnp
from jax import lax
from jax.experimental import pallas as pl
from jax.experimental.pallas import tpu as pltpu
from jax.sharding import PartitionSpec as P

IMAGE = 32768
SG = 256
UVSTEP = 16
F32 = jnp.float32
BF16 = jnp.bfloat16


def cis(turns):
    turns = turns & (IMAGE - 1)
    quarter = IMAGE // 4
    quad = (turns + quarter // 2) // quarter if quarter & (quarter - 1) else lax.shift_right_logical(
        turns + quarter // 2, quarter.bit_length() - 1
    )
    t = (turns - quad * quarter).astype(F32) * (2.0 * math.pi / IMAGE)
    z = t * t
    s = ((-1.9515295891e-4 * z + 8.3321608736e-3) * z - 1.6666654611e-1) * z * t + t
    c = ((2.443315711809948e-5 * z - 1.388731625493765e-3) * z + 4.166664568298827e-2) * z * z - 0.5 * z + 1.0
    odd = (quad & 1) == 1
    cos = jnp.where(odd, s, c)
    sin = jnp.where(odd, c, s)
    cos = jnp.where(((quad + 1) & 2) == 2, -cos, cos)
    sin = jnp.where((quad & 2) == 2, -sin, sin)
    return cos, sin


def grid_kernel(width, rows, cell_ref, value_ref, weight_ref, out_ref):
    @pl.when(pl.program_id(0) == 0)
    def _():
        out_ref[...] = jnp.zeros_like(out_ref)

    cell = cell_ref[...]
    weight = weight_ref[...]
    chunk = cell.shape[1]
    row = lax.shift_right_logical(cell, width.bit_length() - 1)
    col = cell & (width - 1)
    hot = jnp.where(lax.broadcasted_iota(jnp.int32, (width, chunk), 0) == col, 1.0, 0.0).astype(BF16)
    mine = lax.broadcasted_iota(jnp.int32, (rows, chunk), 0) == row
    terms = [weight * value_ref[0:1, :], weight * value_ref[1:2, :], weight]
    left = jnp.concatenate([jnp.where(mine, t, 0.0).astype(BF16) for t in terms], axis=0)
    out_ref[...] += lax.dot_general(left, hot, (((1,), (1,)), ((), ())), preferred_element_type=F32)


def grid_visibilities(cells, values, weights, owned, width):
    count = cells.shape[1]
    rows = -(-owned // 16) * 16
    chunk = min(count, 2048)
    out = pl.pallas_call(
        functools.partial(grid_kernel, width, rows),
        grid=(count // chunk,),
        in_specs=[
            pl.BlockSpec((1, chunk), lambda i: (0, i)),
            pl.BlockSpec((2, chunk), lambda i: (0, i)),
            pl.BlockSpec((1, chunk), lambda i: (0, i)),
        ],
        out_specs=pl.BlockSpec((3 * rows, width), lambda i: (0, 0)),
        out_shape=jax.ShapeDtypeStruct((3 * rows, width), F32),
        cost_estimate=pl.CostEstimate(flops=6 * rows * width * count, bytes_accessed=16 * count, transcendentals=0),
        name="gridding",
    )(cells, values, weights)
    return out.reshape(3, rows, width)[:, :owned]


def forward_kernel(first_ref, subs_ref, slab_ref, out_ref, cos_ref, sin_ref):
    s = pl.program_id(0)
    rows, local = cos_ref.shape
    first = first_ref[0]

    @pl.when(s == 0)
    def _():
        k = lax.broadcasted_iota(jnp.int32, (rows, local), 0)
        y = lax.broadcasted_iota(jnp.int32, (rows, local), 1) + first
        c, n = cis((UVSTEP * k) * y)
        cos_ref[...] = c
        sin_ref[...] = n

    y = lax.broadcasted_iota(jnp.int32, (8, local), 1) + first
    c1, s1 = cis(subs_ref[s] * y)
    c1, s1 = c1[0:1], s1[0:1]
    c2, s2 = cos_ref[...], sin_ref[...]
    tab_real = (c1 * c2 - s1 * s2).astype(BF16)
    tab_imag = (-(s1 * c2 + c1 * s2)).astype(BF16)
    re, im = slab_ref[0], slab_ref[1]
    dot = functools.partial(jnp.dot, preferred_element_type=F32)
    real = dot(tab_real, re) - dot(tab_imag, im)
    imag = dot(tab_real, im) + dot(tab_imag, re)
    slabs, band = out_ref.shape[1], out_ref.shape[3]
    for p in range(slabs):
        out_ref[0, p, 0] = real[p * band:(p + 1) * band].astype(out_ref.dtype)
        out_ref[1, p, 0] = imag[p * band:(p + 1) * band].astype(out_ref.dtype)


def forward(first, subs, slab, slabs):
    _, local, width = slab.shape
    count = subs.shape[0]
    band = SG // slabs
    return pl.pallas_call(
        forward_kernel,
        grid=(count,),
        in_specs=[
            pl.BlockSpec(memory_space=pltpu.SMEM),
            pl.BlockSpec(memory_space=pltpu.SMEM),
            pl.BlockSpec((2, local, width), lambda s: (0, 0, 0)),
        ],
        out_specs=pl.BlockSpec((2, slabs, 1, band, width), lambda s: (0, 0, s, 0, 0)),
        out_shape=jax.ShapeDtypeStruct((2, slabs, count, band, width), BF16),
        scratch_shapes=[pltpu.VMEM((SG, local), F32), pltpu.VMEM((SG, local), F32)],
        name="forward",
    )(first, subs, slab)


def adjoint_kernel(scale, slabs, first_ref, subs_ref, sent_ref, out_ref):
    tile = out_ref.shape[1]
    count = subs_ref.shape[1]
    band = SG // slabs
    start = first_ref[0] + pl.program_id(0) * tile
    yk = lax.broadcasted_iota(jnp.int32, (tile, SG), 0) + start
    c2, s2 = cis((UVSTEP * lax.broadcasted_iota(jnp.int32, (tile, SG), 1)) * yk)
    ys = lax.broadcasted_iota(jnp.int32, (tile, count), 0) + start
    c1, s1 = cis(ys * subs_ref[...])
    real = jnp.zeros(out_ref.shape[1:], F32)
    imag = jnp.zeros(out_ref.shape[1:], F32)
    dot = functools.partial(jnp.dot, preferred_element_type=F32)
    for s in range(count):
        a, b = c1[:, s:s + 1], s1[:, s:s + 1]
        tab_real = (a * c2 - b * s2).astype(BF16)
        tab_imag = (-(b * c2 + a * s2)).astype(BF16)
        re = jnp.concatenate([sent_ref[0, p, s] for p in range(slabs)], axis=0)
        im = jnp.concatenate([sent_ref[1, p, s] for p in range(slabs)], axis=0)
        real += dot(tab_real, re) + dot(tab_imag, im)
        imag += dot(tab_real, im) - dot(tab_imag, re)
    out_ref[0] = real * scale
    out_ref[1] = imag * scale


def adjoint(first, subs, sent, local):
    _, slabs, count, band, width = sent.shape
    tile = min(local, 256)
    return pl.pallas_call(
        functools.partial(adjoint_kernel, 1.0 / math.sqrt(count * SG), slabs),
        grid=(local // tile,),
        in_specs=[
            pl.BlockSpec(memory_space=pltpu.SMEM),
            pl.BlockSpec((1, count), lambda i: (0, 0)),
            pl.BlockSpec((2, slabs, count, band, width), lambda i: (0, 0, 0, 0, 0)),
        ],
        out_specs=pl.BlockSpec((2, tile, width), lambda i: (0, i, 0)),
        out_shape=jax.ShapeDtypeStruct((2, local, width), F32),
        name="adjoint",
    )(first, subs[None, :], sent)


def fused_kernel(
    scale, back, subs_ref, offset_ref, offv_ref, slab_hbm, cell_hbm, value_hbm, weight_hbm,
    residual_ref, update_ref,
    slab_ref, pslab, cell_ref, value_ref, weight_ref, poff, low, high, acc, cb, rx, zf, zb, rz, sums, full,
    table, turn, load,
    sw_send, sw_recv, x_send, x_recv, z_send, z_recv, gz_send, gz_recv, gx_send, gx_recv, gc_send, gc_recv,
):
    facets, slabs = lax.axis_size("facet"), lax.axis_size("slab")
    q, z = lax.axis_index("facet"), lax.axis_index("slab")
    core, chip = q % 2, q // 2
    chips = facets // 2
    partner = q + 1 - 2 * core
    _, local, width = slab_ref.shape
    band = SG // slabs
    groups = band // 16
    dot = functools.partial(jnp.dot, preferred_element_type=F32)

    def at_chip(d):
        return 2 * (chip ^ d) + core

    def remote(src, dst, send, recv, **where):
        return pltpu.make_async_remote_copy(
            src_ref=src, dst_ref=dst, send_sem=send, recv_sem=recv,
            device_id=where, device_id_type=pl.DeviceIdType.MESH,
        )

    barrier = pltpu.get_barrier_semaphore()
    for e in range(1, slabs):
        pl.semaphore_signal(barrier, inc=1, device_id={"slab": z ^ e}, device_id_type=pl.DeviceIdType.MESH)
    for d in range(1, chips):
        pl.semaphore_signal(barrier, inc=1, device_id={"facet": at_chip(d)}, device_id_type=pl.DeviceIdType.MESH)
    pl.semaphore_signal(barrier, inc=1, device_id={"facet": partner}, device_id_type=pl.DeviceIdType.MESH)
    loads = [
        pltpu.make_async_copy(src, dst, load.at[i])
        for i, (src, dst) in enumerate(
            [(slab_hbm, slab_ref), (cell_hbm, cell_ref), (value_hbm, value_ref), (weight_hbm, weight_ref)]
        )
    ]
    for copy in loads:
        copy.start()

    first = offset_ref[0] + z * local
    line = lax.broadcasted_iota(jnp.int32, (16, local), 1)

    def build_low(places, slot):
        c, n = cis(UVSTEP * lax.broadcasted_iota(jnp.int32, (16, local), 0) * places)
        low[slot, 0] = c
        low[slot, 1] = n

    def partial_sum(p, places, slot, data_ref):
        row = lax.broadcasted_iota(jnp.int32, (chips * groups, local), 0)
        freq = UVSTEP * (band * p + 16 * (row % groups))
        for d in range(chips):
            freq += jnp.where(row // groups == d, subs_ref[at_chip(d)], 0)
        c, n = cis(freq * places[0:1])
        high[0] = c
        high[1] = n
        c2, s2 = low[slot, 0], low[slot, 1]
        cos, sin = [], []
        for g in range(chips * groups):
            c1, s1 = high[0, g:g + 1], high[1, g:g + 1]
            cos.append((c1 * c2 - s1 * s2).astype(BF16))
            sin.append((s1 * c2 + c1 * s2).astype(BF16))
        cos = jnp.concatenate(cos, axis=0)
        sin = jnp.concatenate(sin, axis=0)
        data = data_ref[...].reshape(2 * local, width)
        real = dot(jnp.concatenate([cos, sin], axis=1), data)
        imag = dot(jnp.concatenate([-sin, cos], axis=1), data)
        return real, imag

    places = line + first
    build_low(places, 0)
    loads[0].wait()
    pl.semaphore_wait(barrier, chips + slabs - 1)
    swap_offset = remote(offv_ref, poff, sw_send.at[0], sw_recv.at[0], facet=partner)
    swap_slab = remote(slab_ref, pslab, sw_send.at[1], sw_recv.at[1], facet=partner)
    swap_offset.start()
    swap_slab.start()

    def own_part(i, carry):
        real, imag = partial_sum(z ^ (slabs - 1 - i), places, 0, slab_ref)
        acc[i, 0] = real
        acc[i, 1] = imag
        return carry

    lax.fori_loop(0, slabs, own_part, 0)
    swap_offset.wait()
    pplaces = line + (poff[0:1, 0:1] + z * local)
    build_low(pplaces, 1)
    swap_slab.wait()

    def x_copy(i, d):
        return remote(
            cb.at[i, d - 1], rx.at[i, d - 1], x_send.at[i, d - 1], x_recv.at[i, d - 1], facet=at_chip(d)
        )

    def partner_part(i, carry):
        real, imag = partial_sum(z ^ (slabs - 1 - i), pplaces, 1, pslab)
        for c, part in enumerate((real, imag)):
            for d in range(1, chips):
                at = slice(d * band, (d + 1) * band)
                cb[i, d - 1, c] = (acc[i, c, at] + part[at]).astype(BF16)
            zf[i, c] = acc[i, c, 0:band] + part[0:band]
        for d in range(chips - 1, 0, -1):
            x_copy(i, d).start()
        return carry

    lax.fori_loop(0, slabs, partner_part, 0)

    rows = sums.shape[0] // 3
    count = cell_ref.shape[1]
    chunk = min(count, 2048)
    for copy in loads[1:]:
        copy.wait()
    sums[...] = jnp.zeros_like(sums)

    def grid_step(i, carry):
        at = pl.ds(pl.multiple_of(i * chunk, chunk), chunk)
        cell = cell_ref[:, at]
        weight = weight_ref[:, at]
        row = lax.shift_right_logical(cell, width.bit_length() - 1).astype(F32)
        col = (cell & (width - 1)).astype(F32)
        lines = lax.broadcasted_iota(jnp.int32, (16, chunk), 0).astype(F32).astype(BF16)
        row = jnp.broadcast_to(row, (16, chunk)).astype(BF16)
        col = jnp.broadcast_to(col, (16, chunk)).astype(BF16)
        one, zero = jnp.ones((16, chunk), BF16), jnp.zeros((16, chunk), BF16)
        hot = jnp.concatenate(
            [jnp.where(col == lines + jnp.asarray(g, BF16), one, zero) for g in range(0, width, 16)], axis=0
        )
        terms = [weight * value_ref[0, :, at], weight * value_ref[1, :, at], weight]
        terms = [jnp.broadcast_to(t, (16, chunk)).astype(BF16) for t in terms]
        left = jnp.concatenate(
            [jnp.where(row == lines + jnp.asarray(g, BF16), t, zero) for t in terms for g in range(0, rows, 16)],
            axis=0,
        )
        sums[...] += lax.dot_general(left, hot, (((1,), (1,)), ((), ())), preferred_element_type=F32)
        return carry

    span = facets * band

    def table_band(p, carry):
        lane = lax.broadcasted_iota(jnp.int32, (16, span), 1)
        freq = UVSTEP * (band * p + lane % band)
        for s in range(facets):
            freq += jnp.where(lane // band == s, subs_ref[s], 0)
        c2, s2 = cis(freq * lax.broadcasted_iota(jnp.int32, (16, span), 0))
        far = first + 16 * lax.broadcasted_iota(jnp.int32, (local // 16, span), 0)
        c, n = cis(freq[0:1] * far)
        turn[0] = c
        turn[1] = n

        def step(g, inner):
            c1, s1 = turn[0, pl.ds(g, 1)], turn[1, pl.ds(g, 1)]
            sin = (s1 * c2 + c1 * s2).astype(BF16)
            at = pl.ds(pl.multiple_of(g * 16, 16), 16)
            table[p, at, 0:span] = sin
            table[p, at, span:2 * span] = (c1 * c2 - s1 * s2).astype(BF16)
            table[p, at, 2 * span:3 * span] = -sin
            return inner

        lax.fori_loop(0, local // 16, step, 0)
        return carry

    chunks = count // chunk
    cuts = [0, (6 * chunks) // 16, (9 * chunks) // 16, (13 * chunks) // 16, chunks]
    cuts = [cuts[min(i, 4)] for i in range(slabs)] + [chunks]

    def z_copy(i):
        return remote(zb.at[i], rz.at[i], z_send.at[i], z_recv.at[i], slab=z ^ (slabs - 1 - i))

    model = []
    for i in range(slabs):
        lax.fori_loop(cuts[i], cuts[i + 1], grid_step, 0)
        for d in range(chips - 1, 0, -1):
            x_copy(i, d).wait()
        for c in range(2):
            total = zf[i, c]
            for d in range(1, chips):
                total += rx[i, d - 1, c].astype(F32)
            if i < slabs - 1:
                zb[i, c] = total.astype(BF16)
            else:
                zf[i, c] = total
        if i < slabs - 1:
            z_copy(i).start()
    for i in range(slabs - 1):
        z_copy(i).wait()
    for c in range(2):
        model = zf[slabs - 1, c]
        for i in range(slabs - 1):
            model += rz[i, c].astype(F32)
        piece = sums[c * rows:c * rows + band] - sums[2 * rows:2 * rows + band] * (model * scale)
        residual_ref[c] = piece
        full[z, c, q] = piece.astype(BF16)

    def up_copy(e):
        ref = full.at[z, :, q]
        return remote(ref, ref, gz_send.at[e - 1], gz_recv.at[e - 1], slab=z ^ e)

    def across_copy(e, d):
        ref = full.at[z ^ e, :, q]
        return remote(ref, ref, gx_send.at[e, d - 1], gx_recv.at[e, d - 1], facet=at_chip(d))

    def spread_copy(e, d):
        ref = full.at[z ^ e, :, at_chip(d)]
        return remote(ref, ref, gc_send.at[e, d], gc_recv.at[e, d], facet=partner)

    def hand_on(e):
        for d in range(chips - 1, 0, -1):
            across_copy(e, d).start()
        spread_copy(e, 0).start()

    def relay(e):
        for d in range(1, chips):
            across_copy(e, d).wait_recv()
            spread_copy(e, d).start()

    tile = min(local, 256)

    def update_pass(e, begin, end):
        p = z ^ e
        for d in range(chips):
            spread_copy(e, d).wait_recv()

        def step(i, carry):
            at = pl.ds(pl.multiple_of(i * tile, tile), tile)
            data = full[p].reshape(2 * span, width)
            imag = dot(table[p, at, 0:2 * span], data)
            real = dot(table[p, at, span:3 * span], data)
            if not begin:
                real += update_ref[0, at]
                imag += update_ref[1, at]
            update_ref[0, at] = real * back if end else real
            update_ref[1, at] = imag * back if end else imag
            return carry

        lax.fori_loop(0, local // tile, step, 0)

    for e in range(1, slabs):
        up_copy(e).start()
    hand_on(0)
    lax.fori_loop(0, slabs, table_band, 0)
    order = list(range(1, slabs))
    order = order[0:1] + order[:0:-1]
    for e in order[0:1]:
        up_copy(e).wait_recv()
        hand_on(e)
    relay(0)
    for e in order[1:]:
        up_copy(e).wait_recv()
        hand_on(e)
    order = [0] + order
    for k, e in enumerate(order):
        if k + 1 < slabs:
            relay(order[k + 1])
        update_pass(e, k == 0, k == slabs - 1)
    for e in range(slabs):
        if e:
            up_copy(e).wait_send()
        for d in range(chips):
            if d:
                across_copy(e, d).wait_send()
            spread_copy(e, d).wait_send()


def fused(offset, subs, slab, cells, values, weights, slabs, facets):
    _, local, width = slab.shape
    band = SG // slabs
    chips = facets // 2
    rows = -(-band // 16) * 16
    vmem = pl.BlockSpec(memory_space=pltpu.VMEM)
    dma = pltpu.SemaphoreType.DMA
    return pl.pallas_call(
        functools.partial(
            fused_kernel, 1.0 / math.sqrt(local * slabs * facets), 1.0 / math.sqrt(subs.shape[0] * SG)
        ),
        in_specs=[pl.BlockSpec(memory_space=pltpu.SMEM)] * 2 + [vmem] + [pl.BlockSpec(memory_space=pltpu.HBM)] * 4,
        out_specs=[vmem, vmem],
        out_shape=[
            jax.ShapeDtypeStruct((2, band, width), F32),
            jax.ShapeDtypeStruct((2, local, width), F32),
        ],
        scratch_shapes=[
            pltpu.VMEM((2, local, width), BF16),
            pltpu.VMEM((2, local, width), BF16),
            pltpu.VMEM(cells.shape, jnp.int32),
            pltpu.VMEM(values.shape, F32),
            pltpu.VMEM(weights.shape, F32),
            pltpu.VMEM((8, 128), jnp.int32),
            pltpu.VMEM((2, 2, 16, local), F32),
            pltpu.VMEM((2, chips * (band // 16), local), F32),
            pltpu.VMEM((slabs, 2, chips * band, width), F32),
            pltpu.VMEM((slabs, chips - 1, 2, band, width), BF16),
            pltpu.VMEM((slabs, chips - 1, 2, band, width), BF16),
            pltpu.VMEM((slabs, 2, band, width), F32),
            pltpu.VMEM((slabs - 1, 2, band, width), BF16),
            pltpu.VMEM((slabs - 1, 2, band, width), BF16),
            pltpu.VMEM((3 * rows, width), F32),
            pltpu.VMEM((slabs, 2, facets, band, width), BF16),
            pltpu.VMEM((slabs, local, 3 * facets * band), BF16),
            pltpu.VMEM((2, local // 16, facets * band), F32),
            dma((4,)),
            dma((2,)), dma((2,)),
            dma((slabs, chips - 1)), dma((slabs, chips - 1)),
            dma((slabs - 1,)), dma((slabs - 1,)),
            dma((slabs - 1,)), dma((slabs - 1,)),
            dma((slabs, chips - 1)), dma((slabs, chips - 1)),
            dma((slabs, chips)), dma((slabs, chips)),
        ],
        compiler_params=pltpu.CompilerParams(collective_id=0, has_side_effects=True, vmem_limit_bytes=48 * 1024 * 1024),
        name="fused",
    )(subs, offset, jnp.broadcast_to(offset, (8, 128)), slab, cells, values, weights)


def body(slab, facet_offset, subgrid_offset, vis_cell, vis_value, vis_weight):
    slabs = lax.axis_size("slab")
    facets = lax.axis_size("facet")
    local_rows = slab.shape[2]
    width = slab.shape[3]
    count_sub = subgrid_offset.shape[0]
    band = SG // slabs
    owned = count_sub * band // facets
    first = (facet_offset + lax.axis_index("slab") * local_rows).astype(jnp.int32)
    chips = facets // 2
    paired = facets == 2 * chips and chips > 1 and chips & (chips - 1) == 0 and slabs > 1 and slabs & (slabs - 1) == 0
    if owned == band and count_sub == facets and paired and band % 16 == 0 and local_rows % 256 == 0:
        residual, update = fused(
            facet_offset, subgrid_offset, slab[:, 0], vis_cell[0], vis_value[:, 0], vis_weight[0], slabs, facets
        )
        return (residual.reshape(2, 1, owned, width), update.reshape(2, 1, local_rows, width))
    sums = grid_visibilities(vis_cell[0], vis_value[:, 0, 0], vis_weight[0], owned, width)
    contrib = forward(first, subgrid_offset, slab[:, 0], slabs)
    contrib = contrib.reshape(2, slabs, facets, owned, width)
    parts = lax.all_to_all(contrib, "facet", 2, 2, tiled=True)
    parts = jnp.sum(parts, axis=2, dtype=F32).astype(BF16)
    parts = lax.all_to_all(parts, "slab", 1, 1, tiled=True)
    scale = 1.0 / math.sqrt(local_rows * slabs * facets)
    model = jnp.sum(parts, axis=1, dtype=F32) * scale
    residual = sums[:2] - sums[2:] * model
    sent = residual.astype(BF16).reshape(2, 1, 1, owned, width)
    piece = lax.all_gather(sent, "slab", axis=1, tiled=True)
    piece = lax.all_gather(piece, "facet", axis=2, tiled=True)
    piece = piece.reshape(2, slabs, count_sub, band, width)
    update = adjoint(first, subgrid_offset, piece, local_rows)
    return (residual.reshape(2, 1, owned, width), update.reshape(2, 1, local_rows, width))


def solution(mesh):
    placed = (
        P(None, "facet", "slab", None),
        P("facet"),
        P(),
        P("slab", "facet", None),
        P(None, "slab", "facet", None),
        P("slab", "facet", None),
    )
    return jax.shard_map(
        body,
        mesh=mesh,
        in_specs=placed,
        out_specs=(P(None, "slab", "facet", None), P(None, "facet", "slab", None)),
        check_vma=False,
    )
```

```python
import functools
import math

import jax
import jax.numpy as jnp
from jax import lax
from jax.experimental import pallas as pl
from jax.experimental.pallas import tpu as pltpu
from jax.sharding import PartitionSpec as P

IMAGE = 32768
SG = 256
UVSTEP = 16
F32 = jnp.float32
BF16 = jnp.bfloat16
EARLY = 1


def cis(turns):
    turns = turns & (IMAGE - 1)
    quarter = IMAGE // 4
    quad = (turns + quarter // 2) // quarter if quarter & (quarter - 1) else lax.shift_right_logical(
        turns + quarter // 2, quarter.bit_length() - 1
    )
    t = (turns - quad * quarter).astype(F32) * (2.0 * math.pi / IMAGE)
    z = t * t
    s = ((-1.9515295891e-4 * z + 8.3321608736e-3) * z - 1.6666654611e-1) * z * t + t
    c = ((2.443315711809948e-5 * z - 1.388731625493765e-3) * z + 4.166664568298827e-2) * z * z - 0.5 * z + 1.0
    odd = (quad & 1) == 1
    cos = jnp.where(odd, s, c)
    sin = jnp.where(odd, c, s)
    cos = jnp.where(((quad + 1) & 2) == 2, -cos, cos)
    sin = jnp.where((quad & 2) == 2, -sin, sin)
    return cos, sin


def grid_kernel(width, rows, cell_ref, value_ref, weight_ref, out_ref):
    @pl.when(pl.program_id(0) == 0)
    def _():
        out_ref[...] = jnp.zeros_like(out_ref)

    cell = cell_ref[...]
    weight = weight_ref[...]
    chunk = cell.shape[1]
    row = lax.shift_right_logical(cell, width.bit_length() - 1)
    col = cell & (width - 1)
    hot = jnp.where(lax.broadcasted_iota(jnp.int32, (width, chunk), 0) == col, 1.0, 0.0).astype(BF16)
    mine = lax.broadcasted_iota(jnp.int32, (rows, chunk), 0) == row
    terms = [weight * value_ref[0:1, :], weight * value_ref[1:2, :], weight]
    left = jnp.concatenate([jnp.where(mine, t, 0.0).astype(BF16) for t in terms], axis=0)
    out_ref[...] += lax.dot_general(left, hot, (((1,), (1,)), ((), ())), preferred_element_type=F32)


def grid_visibilities(cells, values, weights, owned, width):
    count = cells.shape[1]
    rows = -(-owned // 16) * 16
    chunk = min(count, 2048)
    out = pl.pallas_call(
        functools.partial(grid_kernel, width, rows),
        grid=(count // chunk,),
        in_specs=[
            pl.BlockSpec((1, chunk), lambda i: (0, i)),
            pl.BlockSpec((2, chunk), lambda i: (0, i)),
            pl.BlockSpec((1, chunk), lambda i: (0, i)),
        ],
        out_specs=pl.BlockSpec((3 * rows, width), lambda i: (0, 0)),
        out_shape=jax.ShapeDtypeStruct((3 * rows, width), F32),
        cost_estimate=pl.CostEstimate(flops=6 * rows * width * count, bytes_accessed=16 * count, transcendentals=0),
        name="gridding",
    )(cells, values, weights)
    return out.reshape(3, rows, width)[:, :owned]


def forward_kernel(first_ref, subs_ref, slab_ref, out_ref, cos_ref, sin_ref):
    s = pl.program_id(0)
    rows, local = cos_ref.shape
    first = first_ref[0]

    @pl.when(s == 0)
    def _():
        k = lax.broadcasted_iota(jnp.int32, (rows, local), 0)
        y = lax.broadcasted_iota(jnp.int32, (rows, local), 1) + first
        c, n = cis((UVSTEP * k) * y)
        cos_ref[...] = c
        sin_ref[...] = n

    y = lax.broadcasted_iota(jnp.int32, (8, local), 1) + first
    c1, s1 = cis(subs_ref[s] * y)
    c1, s1 = c1[0:1], s1[0:1]
    c2, s2 = cos_ref[...], sin_ref[...]
    tab_real = (c1 * c2 - s1 * s2).astype(BF16)
    tab_imag = (-(s1 * c2 + c1 * s2)).astype(BF16)
    re, im = slab_ref[0], slab_ref[1]
    dot = functools.partial(jnp.dot, preferred_element_type=F32)
    real = dot(tab_real, re) - dot(tab_imag, im)
    imag = dot(tab_real, im) + dot(tab_imag, re)
    slabs, band = out_ref.shape[1], out_ref.shape[3]
    for p in range(slabs):
        out_ref[0, p, 0] = real[p * band:(p + 1) * band].astype(out_ref.dtype)
        out_ref[1, p, 0] = imag[p * band:(p + 1) * band].astype(out_ref.dtype)


def forward(first, subs, slab, slabs):
    _, local, width = slab.shape
    count = subs.shape[0]
    band = SG // slabs
    return pl.pallas_call(
        forward_kernel,
        grid=(count,),
        in_specs=[
            pl.BlockSpec(memory_space=pltpu.SMEM),
            pl.BlockSpec(memory_space=pltpu.SMEM),
            pl.BlockSpec((2, local, width), lambda s: (0, 0, 0)),
        ],
        out_specs=pl.BlockSpec((2, slabs, 1, band, width), lambda s: (0, 0, s, 0, 0)),
        out_shape=jax.ShapeDtypeStruct((2, slabs, count, band, width), BF16),
        scratch_shapes=[pltpu.VMEM((SG, local), F32), pltpu.VMEM((SG, local), F32)],
        name="forward",
    )(first, subs, slab)


def adjoint_kernel(scale, slabs, first_ref, subs_ref, sent_ref, out_ref):
    tile = out_ref.shape[1]
    count = subs_ref.shape[1]
    band = SG // slabs
    start = first_ref[0] + pl.program_id(0) * tile
    yk = lax.broadcasted_iota(jnp.int32, (tile, SG), 0) + start
    c2, s2 = cis((UVSTEP * lax.broadcasted_iota(jnp.int32, (tile, SG), 1)) * yk)
    ys = lax.broadcasted_iota(jnp.int32, (tile, count), 0) + start
    c1, s1 = cis(ys * subs_ref[...])
    real = jnp.zeros(out_ref.shape[1:], F32)
    imag = jnp.zeros(out_ref.shape[1:], F32)
    dot = functools.partial(jnp.dot, preferred_element_type=F32)
    for s in range(count):
        a, b = c1[:, s:s + 1], s1[:, s:s + 1]
        tab_real = (a * c2 - b * s2).astype(BF16)
        tab_imag = (-(b * c2 + a * s2)).astype(BF16)
        re = jnp.concatenate([sent_ref[0, p, s] for p in range(slabs)], axis=0)
        im = jnp.concatenate([sent_ref[1, p, s] for p in range(slabs)], axis=0)
        real += dot(tab_real, re) + dot(tab_imag, im)
        imag += dot(tab_real, im) - dot(tab_imag, re)
    out_ref[0] = real * scale
    out_ref[1] = imag * scale


def adjoint(first, subs, sent, local):
    _, slabs, count, band, width = sent.shape
    tile = min(local, 256)
    return pl.pallas_call(
        functools.partial(adjoint_kernel, 1.0 / math.sqrt(count * SG), slabs),
        grid=(local // tile,),
        in_specs=[
            pl.BlockSpec(memory_space=pltpu.SMEM),
            pl.BlockSpec((1, count), lambda i: (0, 0)),
            pl.BlockSpec((2, slabs, count, band, width), lambda i: (0, 0, 0, 0, 0)),
        ],
        out_specs=pl.BlockSpec((2, tile, width), lambda i: (0, i, 0)),
        out_shape=jax.ShapeDtypeStruct((2, local, width), F32),
        name="adjoint",
    )(first, subs[None, :], sent)


def fused_kernel(
    scale, offset_ref, subs_hbm, slab_hbm, cell_hbm, value_hbm, weight_hbm,
    residual_ref, update_ref, last_ref, last_table,
    subs_ref, slab_ref, cell_ref, value_ref, weight_ref, low, high, acc, pb, rp, cb, rx, zf, zb, rz, sums, full,
    table, turn, load,
    p_send, p_recv, x_send, x_recv, z_send, z_recv, gz_send, gz_recv, gx_send, gx_recv, gc_send, gc_recv,
):
    facets, slabs = lax.axis_size("facet"), lax.axis_size("slab")
    q, z = lax.axis_index("facet"), lax.axis_index("slab")
    core, chip = q % 2, q // 2
    chips = facets // 2
    partner = q + 1 - 2 * core
    _, local, width = slab_ref.shape
    band = SG // slabs
    groups = band // 16
    dot = functools.partial(jnp.dot, preferred_element_type=F32)

    def at_chip(d):
        return 2 * (chip ^ d) + core

    def remote(src, dst, send, recv, **where):
        return pltpu.make_async_remote_copy(
            src_ref=src, dst_ref=dst, send_sem=send, recv_sem=recv,
            device_id=where, device_id_type=pl.DeviceIdType.MESH,
        )

    barrier = pltpu.get_barrier_semaphore()
    for e in range(1, slabs):
        pl.semaphore_signal(barrier, inc=1, device_id={"slab": z ^ e}, device_id_type=pl.DeviceIdType.MESH)
    for d in range(1, chips):
        pl.semaphore_signal(barrier, inc=1, device_id={"facet": at_chip(d)}, device_id_type=pl.DeviceIdType.MESH)
    pl.semaphore_signal(barrier, inc=1, device_id={"facet": partner}, device_id_type=pl.DeviceIdType.MESH)
    loads = [
        pltpu.make_async_copy(src, dst, load.at[i])
        for i, (src, dst) in enumerate(
            [
                (subs_hbm, subs_ref), (slab_hbm, slab_ref),
                (cell_hbm, cell_ref), (value_hbm, value_ref), (weight_hbm, weight_ref),
            ]
        )
    ]
    for copy in loads:
        copy.start()

    loads[0].wait()
    first = offset_ref[0] + z * local
    line = lax.broadcasted_iota(jnp.int32, (16, local), 1)

    places = line + first
    c, n = cis(UVSTEP * lax.broadcasted_iota(jnp.int32, (16, local), 0) * places)
    low[0] = c
    low[1] = n

    def partial_sum(i, other):
        row = lax.broadcasted_iota(jnp.int32, (chips * groups, local), 0)
        freq = UVSTEP * (band * (z ^ (slabs - 1 - i)) + 16 * (row % groups))
        for d in range(chips):
            freq += jnp.where(row // groups == d, subs_ref[at_chip(d) ^ other], 0)
        c, n = cis(freq * places[0:1])
        high[0] = c
        high[1] = n
        c2, s2 = low[0], low[1]
        cos, sin = [], []
        for g in range(chips * groups):
            c1, s1 = high[0, g:g + 1], high[1, g:g + 1]
            cos.append((c1 * c2 - s1 * s2).astype(BF16))
            sin.append((s1 * c2 + c1 * s2).astype(BF16))
        cos = jnp.concatenate(cos, axis=0)
        sin = jnp.concatenate(sin, axis=0)
        data = slab_ref[...].reshape(2 * local, width)
        real = dot(jnp.concatenate([cos, sin], axis=1), data)
        imag = dot(jnp.concatenate([-sin, cos], axis=1), data)
        return real, imag

    def compute_band(i, carry):
        real, imag = partial_sum(i, 1)
        pb[i, 0] = real.astype(BF16)
        pb[i, 1] = imag.astype(BF16)
        real, imag = partial_sum(i, 0)
        acc[i, 0] = real
        acc[i, 1] = imag
        return carry

    def pair_copy(i):
        return remote(pb.at[i], rp.at[i], p_send.at[i], p_recv.at[i], facet=partner)

    def x_copy(i, d):
        return remote(
            cb.at[i, d - 1], rx.at[i, d - 1], x_send.at[i, d - 1], x_recv.at[i, d - 1], facet=at_chip(d)
        )

    def pair_band(i, carry):
        pair_copy(i).wait_recv()
        for d in range(chips - 1, 0, -1):
            at = slice(d * band, (d + 1) * band)
            for c in range(2):
                cb[i, d - 1, c] = (acc[i, c, at] + rp[i, c, at].astype(F32)).astype(BF16)
            x_copy(i, d).start()
        for c in range(2):
            zf[i, c] = acc[i, c, 0:band] + rp[i, c, 0:band].astype(F32)
        return carry

    loads[1].wait()
    early = min(EARLY, slabs)
    lax.fori_loop(0, early, compute_band, 0)
    pl.semaphore_wait(barrier, chips + slabs - 1)
    for i in range(early):
        pair_copy(i).start()
    for i in range(slabs):
        if i + early < slabs:
            compute_band(i + early, 0)
            pair_copy(i + early).start()
        pair_band(i, 0)

    rows = sums.shape[0] // 3
    count = cell_ref.shape[1]
    chunk = min(count, 2048)
    for copy in loads[2:]:
        copy.wait()
    sums[...] = jnp.zeros_like(sums)

    def grid_step(i, carry):
        at = pl.ds(pl.multiple_of(i * chunk, chunk), chunk)
        cell = cell_ref[:, at]
        weight = weight_ref[:, at]
        row = lax.shift_right_logical(cell, width.bit_length() - 1).astype(F32)
        col = (cell & (width - 1)).astype(F32)
        lines = lax.broadcasted_iota(jnp.int32, (16, chunk), 0).astype(F32).astype(BF16)
        row = jnp.broadcast_to(row, (16, chunk)).astype(BF16)
        col = jnp.broadcast_to(col, (16, chunk)).astype(BF16)
        one, zero = jnp.ones((16, chunk), BF16), jnp.zeros((16, chunk), BF16)
        hot = jnp.concatenate(
            [jnp.where(col == lines + jnp.asarray(g, BF16), one, zero) for g in range(0, width, 16)], axis=0
        )
        terms = [weight * value_ref[0, :, at], weight * value_ref[1, :, at], weight]
        terms = [jnp.broadcast_to(t, (16, chunk)).astype(BF16) for t in terms]
        left = jnp.concatenate(
            [jnp.where(row == lines + jnp.asarray(g, BF16), t, zero) for t in terms for g in range(0, rows, 16)],
            axis=0,
        )
        sums[...] += lax.dot_general(left, hot, (((1,), (1,)), ((), ())), preferred_element_type=F32)
        return carry

    span = facets * band

    def table_band(e, carry):
        lane = lax.broadcasted_iota(jnp.int32, (16, span), 1)
        freq = UVSTEP * (band * (z ^ e) + lane % band)
        for s in range(facets):
            freq += jnp.where(lane // band == s, subs_ref[s], 0)
        c2, s2 = cis(freq * lax.broadcasted_iota(jnp.int32, (16, span), 0))
        far = first + 16 * lax.broadcasted_iota(jnp.int32, (local // 16, span), 0)
        c, n = cis(freq[0:1] * far)
        turn[0] = c
        turn[1] = n

        def step(g, inner):
            c1, s1 = turn[0, pl.ds(g, 1)], turn[1, pl.ds(g, 1)]
            sin = (s1 * c2 + c1 * s2).astype(BF16)
            at = pl.ds(pl.multiple_of(g * 16, 16), 16)
            into = last_table if isinstance(e, int) else table.at[e]
            into[at, 0:span] = sin
            into[at, span:2 * span] = (c1 * c2 - s1 * s2).astype(BF16)
            into[at, 2 * span:3 * span] = -sin
            return inner

        lax.fori_loop(0, local // 16, step, 0)
        return carry

    chunks = count // chunk
    cuts = [0, (6 * chunks) // 16, (9 * chunks) // 16, (13 * chunks) // 16, chunks]
    cuts = [cuts[min(i, 4)] for i in range(slabs)] + [chunks]

    def z_copy(i):
        return remote(zb.at[i], rz.at[i], z_send.at[i], z_recv.at[i], slab=z ^ (slabs - 1 - i))

    model = []
    for i in range(slabs):
        lax.fori_loop(cuts[i], cuts[i + 1], grid_step, 0)
        for d in range(chips - 1, 0, -1):
            x_copy(i, d).wait()
        for c in range(2):
            total = zf[i, c]
            for d in range(1, chips):
                total += rx[i, d - 1, c].astype(F32)
            if i < slabs - 1:
                zb[i, c] = total.astype(BF16)
            else:
                zf[i, c] = total
        if i < slabs - 1:
            z_copy(i).start()
    for i in range(slabs - 1):
        z_copy(i).wait()
    for c in range(2):
        model = zf[slabs - 1, c]
        for i in range(slabs - 1):
            model += rz[i, c].astype(F32)
        piece = sums[c * rows:c * rows + band] - sums[2 * rows:2 * rows + band] * (model * scale)
        residual_ref[c] = piece
        full[0, c, q] = piece.astype(BF16)

    def up_copy(e):
        ref = full.at[0, :, q]
        return remote(ref, full.at[e, :, q], gz_send.at[e - 1], gz_recv.at[e - 1], slab=z ^ e)

    def across_copy(e, d):
        ref = full.at[e, :, q]
        return remote(ref, ref, gx_send.at[e, d - 1], gx_recv.at[e, d - 1], facet=at_chip(d))

    def spread_copy(e, d):
        ref = full.at[e, :, at_chip(d)]
        return remote(ref, ref, gc_send.at[e, d], gc_recv.at[e, d], facet=partner)

    def hand_on(e):
        for d in range(chips - 1, 0, -1):
            across_copy(e, d).start()
        spread_copy(e, 0).start()

    def relay(e):
        for d in range(1, chips):
            across_copy(e, d).wait_recv()
            spread_copy(e, d).start()

    tile = min(local, 256)

    def gathered(e):
        for d in range(chips):
            spread_copy(e, d).wait_recv()

    def update_pass(e, begin):
        def step(i, carry):
            at = pl.ds(pl.multiple_of(i * tile, tile), tile)
            data = full[e].reshape(2 * span, width)
            imag = dot(table[e, at, 0:2 * span], data)
            real = dot(table[e, at, span:3 * span], data)
            if not begin:
                real += update_ref[0, at]
                imag += update_ref[1, at]
            update_ref[0, at] = real
            update_ref[1, at] = imag
            return carry

        lax.fori_loop(0, local // tile, step, 0)

    for e in range(1, slabs):
        up_copy(e).start()
    hand_on(0)
    order = [0] + sorted(range(1, slabs), key=lambda e: (e != 1, -e))
    last = order[-1]
    lax.fori_loop(0, last, table_band, 0)
    lax.fori_loop(last + 1, slabs, table_band, 0)
    table_band(last, 0)
    for k, e in enumerate(order[1:]):
        up_copy(e).wait_recv()
        hand_on(e)
        if k == 0:
            relay(0)
    for k, e in enumerate(order):
        if k + 1 < slabs:
            relay(order[k + 1])
        gathered(e)
        if e == last:
            last_ref[...] = full[e]
        else:
            update_pass(e, k == 0)
    for i in range(slabs):
        pair_copy(i).wait_send()
    for e in range(slabs):
        if e:
            up_copy(e).wait_send()
        for d in range(chips):
            if d:
                across_copy(e, d).wait_send()
            spread_copy(e, d).wait_send()


def finish_kernel(back, piece_ref, part_ref, last_ref, table_ref, residual_ref, update_ref, buffer, sent):
    dot = functools.partial(jnp.dot, preferred_element_type=F32)
    _, local, width = part_ref.shape
    span = table_ref.shape[1] // 3
    tiles, _, tile, _ = buffer.shape
    out = pltpu.make_async_copy(piece_ref, residual_ref, sent.at[tiles])
    out.start()

    def put(i):
        at = pl.ds(pl.multiple_of(i * tile, tile), tile)
        return pltpu.make_async_copy(buffer.at[i], update_ref.at[:, at], sent.at[i])

    def step(i, carry):
        at = pl.ds(pl.multiple_of(i * tile, tile), tile)
        data = last_ref[...].reshape(2 * span, width)
        imag = dot(table_ref[at, 0:2 * span], data)
        real = dot(table_ref[at, span:3 * span], data)
        buffer[i, 0] = (real + part_ref[0, at]) * back
        buffer[i, 1] = (imag + part_ref[1, at]) * back
        put(i).start()
        return carry

    lax.fori_loop(0, tiles, step, 0)
    for i in range(tiles):
        put(i).wait()
    out.wait()


def fused(offset, subs, slab, cells, values, weights, slabs, facets):
    _, local, width = slab.shape
    band = SG // slabs
    chips = facets // 2
    rows = -(-band // 16) * 16
    vmem = pl.BlockSpec(memory_space=pltpu.VMEM)
    dma = pltpu.SemaphoreType.DMA
    span = facets * band
    piece, part, last, last_table = pl.pallas_call(
        functools.partial(fused_kernel, 1.0 / math.sqrt(local * slabs * facets)),
        in_specs=[pl.BlockSpec(memory_space=pltpu.SMEM)] + [pl.BlockSpec(memory_space=pltpu.HBM)] * 5,
        out_specs=[vmem] * 4,
        out_shape=[
            jax.ShapeDtypeStruct((2, band, width), F32),
            jax.ShapeDtypeStruct((2, local, width), F32),
            jax.ShapeDtypeStruct((2, facets, band, width), BF16),
            jax.ShapeDtypeStruct((local, 3 * span), BF16),
        ],
        scratch_shapes=[
            pltpu.SMEM(subs.shape, jnp.int32),
            pltpu.VMEM((2, local, width), BF16),
            pltpu.VMEM(cells.shape, jnp.int32),
            pltpu.VMEM(values.shape, F32),
            pltpu.VMEM(weights.shape, F32),
            pltpu.VMEM((2, 16, local), F32),
            pltpu.VMEM((2, chips * (band // 16), local), F32),
            pltpu.VMEM((slabs, 2, chips * band, width), F32),
            pltpu.VMEM((slabs, 2, chips * band, width), BF16),
            pltpu.VMEM((slabs, 2, chips * band, width), BF16),
            pltpu.VMEM((slabs, chips - 1, 2, band, width), BF16),
            pltpu.VMEM((slabs, chips - 1, 2, band, width), BF16),
            pltpu.VMEM((slabs, 2, band, width), F32),
            pltpu.VMEM((slabs - 1, 2, band, width), BF16),
            pltpu.VMEM((slabs - 1, 2, band, width), BF16),
            pltpu.VMEM((3 * rows, width), F32),
            pltpu.VMEM((slabs, 2, facets, band, width), BF16),
            pltpu.VMEM((slabs, local, 3 * span), BF16),
            pltpu.VMEM((2, local // 16, span), F32),
            dma((5,)),
            dma((slabs,)), dma((slabs,)),
            dma((slabs, chips - 1)), dma((slabs, chips - 1)),
            dma((slabs - 1,)), dma((slabs - 1,)),
            dma((slabs - 1,)), dma((slabs - 1,)),
            dma((slabs, chips - 1)), dma((slabs, chips - 1)),
            dma((slabs, chips)), dma((slabs, chips)),
        ],
        compiler_params=pltpu.CompilerParams(collective_id=0, has_side_effects=True, vmem_limit_bytes=40 * 1024 * 1024),
        name="fused",
    )(offset, *[pltpu.with_memory_space_constraint(x, pltpu.HBM) for x in (subs, slab, cells, values, weights)])
    tiles = local // min(local, 256)
    return pl.pallas_call(
        functools.partial(finish_kernel, 1.0 / math.sqrt(subs.shape[0] * SG)),
        in_specs=[vmem] * 4,
        out_specs=[pl.BlockSpec(memory_space=pltpu.HBM)] * 2,
        out_shape=[
            jax.ShapeDtypeStruct((2, band, width), F32),
            jax.ShapeDtypeStruct((2, local, width), F32),
        ],
        scratch_shapes=[pltpu.VMEM((tiles, 2, local // tiles, width), F32), dma((tiles + 1,))],
        compiler_params=pltpu.CompilerParams(vmem_limit_bytes=8 * 1024 * 1024),
        name="finish",
    )(piece, part, last, last_table)


def body(slab, facet_offset, subgrid_offset, vis_cell, vis_value, vis_weight):
    slabs = lax.axis_size("slab")
    facets = lax.axis_size("facet")
    local_rows = slab.shape[2]
    width = slab.shape[3]
    count_sub = subgrid_offset.shape[0]
    band = SG // slabs
    owned = count_sub * band // facets
    first = (facet_offset + lax.axis_index("slab") * local_rows).astype(jnp.int32)
    chips = facets // 2
    paired = facets == 2 * chips and chips > 1 and chips & (chips - 1) == 0 and slabs > 1 and slabs & (slabs - 1) == 0
    if owned == band and count_sub == facets and paired and band % 16 == 0 and local_rows % 256 == 0:
        residual, update = fused(
            facet_offset, subgrid_offset, slab[:, 0], vis_cell[0], vis_value[:, 0], vis_weight[0], slabs, facets
        )
        return (residual.reshape(2, 1, owned, width), update.reshape(2, 1, local_rows, width))
    sums = grid_visibilities(vis_cell[0], vis_value[:, 0, 0], vis_weight[0], owned, width)
    contrib = forward(first, subgrid_offset, slab[:, 0], slabs)
    contrib = contrib.reshape(2, slabs, facets, owned, width)
    parts = lax.all_to_all(contrib, "facet", 2, 2, tiled=True)
    parts = jnp.sum(parts, axis=2, dtype=F32).astype(BF16)
    parts = lax.all_to_all(parts, "slab", 1, 1, tiled=True)
    scale = 1.0 / math.sqrt(local_rows * slabs * facets)
    model = jnp.sum(parts, axis=1, dtype=F32) * scale
    residual = sums[:2] - sums[2:] * model
    sent = residual.astype(BF16).reshape(2, 1, 1, owned, width)
    piece = lax.all_gather(sent, "slab", axis=1, tiled=True)
    piece = lax.all_gather(piece, "facet", axis=2, tiled=True)
    piece = piece.reshape(2, slabs, count_sub, band, width)
    update = adjoint(first, subgrid_offset, piece, local_rows)
    return (residual.reshape(2, 1, owned, width), update.reshape(2, 1, local_rows, width))


def solution(mesh):
    placed = (
        P(None, "facet", "slab", None),
        P("facet"),
        P(),
        P("slab", "facet", None),
        P(None, "slab", "facet", None),
        P("slab", "facet", None),
    )
    return jax.shard_map(
        body,
        mesh=mesh,
        in_specs=placed,
        out_specs=(P(None, "slab", "facet", None), P(None, "facet", "slab", None)),
        check_vma=False,
    )
```

```python
import functools
import math

import jax
import jax.numpy as jnp
from jax import lax
from jax.experimental import pallas as pl
from jax.experimental.pallas import tpu as pltpu
from jax.sharding import PartitionSpec as P

IMAGE = 32768
SG = 256
UVSTEP = 16
F32 = jnp.float32
BF16 = jnp.bfloat16


def cis(turns):
    turns = turns & (IMAGE - 1)
    quarter = IMAGE // 4
    quad = (turns + quarter // 2) // quarter if quarter & (quarter - 1) else lax.shift_right_logical(
        turns + quarter // 2, quarter.bit_length() - 1
    )
    t = (turns - quad * quarter).astype(F32) * (2.0 * math.pi / IMAGE)
    z = t * t
    s = ((-1.9515295891e-4 * z + 8.3321608736e-3) * z - 1.6666654611e-1) * z * t + t
    c = ((2.443315711809948e-5 * z - 1.388731625493765e-3) * z + 4.166664568298827e-2) * z * z - 0.5 * z + 1.0
    odd = (quad & 1) == 1
    cos = jnp.where(odd, s, c)
    sin = jnp.where(odd, c, s)
    cos = jnp.where(((quad + 1) & 2) == 2, -cos, cos)
    sin = jnp.where((quad & 2) == 2, -sin, sin)
    return cos, sin


def grid_kernel(width, rows, cell_ref, value_ref, weight_ref, out_ref):
    @pl.when(pl.program_id(0) == 0)
    def _():
        out_ref[...] = jnp.zeros_like(out_ref)

    cell = cell_ref[...]
    weight = weight_ref[...]
    chunk = cell.shape[1]
    row = lax.shift_right_logical(cell, width.bit_length() - 1)
    col = cell & (width - 1)
    hot = jnp.where(lax.broadcasted_iota(jnp.int32, (width, chunk), 0) == col, 1.0, 0.0).astype(BF16)
    mine = lax.broadcasted_iota(jnp.int32, (rows, chunk), 0) == row
    terms = [weight * value_ref[0:1, :], weight * value_ref[1:2, :], weight]
    left = jnp.concatenate([jnp.where(mine, t, 0.0).astype(BF16) for t in terms], axis=0)
    out_ref[...] += lax.dot_general(left, hot, (((1,), (1,)), ((), ())), preferred_element_type=F32)


def grid_visibilities(cells, values, weights, owned, width):
    count = cells.shape[1]
    rows = -(-owned // 16) * 16
    chunk = min(count, 2048)
    out = pl.pallas_call(
        functools.partial(grid_kernel, width, rows),
        grid=(count // chunk,),
        in_specs=[
            pl.BlockSpec((1, chunk), lambda i: (0, i)),
            pl.BlockSpec((2, chunk), lambda i: (0, i)),
            pl.BlockSpec((1, chunk), lambda i: (0, i)),
        ],
        out_specs=pl.BlockSpec((3 * rows, width), lambda i: (0, 0)),
        out_shape=jax.ShapeDtypeStruct((3 * rows, width), F32),
        cost_estimate=pl.CostEstimate(flops=6 * rows * width * count, bytes_accessed=16 * count, transcendentals=0),
        name="gridding",
    )(cells, values, weights)
    return out.reshape(3, rows, width)[:, :owned]


def forward_kernel(first_ref, subs_ref, slab_ref, out_ref, cos_ref, sin_ref):
    s = pl.program_id(0)
    rows, local = cos_ref.shape
    first = first_ref[0]

    @pl.when(s == 0)
    def _():
        k = lax.broadcasted_iota(jnp.int32, (rows, local), 0)
        y = lax.broadcasted_iota(jnp.int32, (rows, local), 1) + first
        c, n = cis((UVSTEP * k) * y)
        cos_ref[...] = c
        sin_ref[...] = n

    y = lax.broadcasted_iota(jnp.int32, (8, local), 1) + first
    c1, s1 = cis(subs_ref[s] * y)
    c1, s1 = c1[0:1], s1[0:1]
    c2, s2 = cos_ref[...], sin_ref[...]
    tab_real = (c1 * c2 - s1 * s2).astype(BF16)
    tab_imag = (-(s1 * c2 + c1 * s2)).astype(BF16)
    re, im = slab_ref[0], slab_ref[1]
    dot = functools.partial(jnp.dot, preferred_element_type=F32)
    real = dot(tab_real, re) - dot(tab_imag, im)
    imag = dot(tab_real, im) + dot(tab_imag, re)
    slabs, band = out_ref.shape[1], out_ref.shape[3]
    for p in range(slabs):
        out_ref[0, p, 0] = real[p * band:(p + 1) * band].astype(out_ref.dtype)
        out_ref[1, p, 0] = imag[p * band:(p + 1) * band].astype(out_ref.dtype)


def forward(first, subs, slab, slabs):
    _, local, width = slab.shape
    count = subs.shape[0]
    band = SG // slabs
    return pl.pallas_call(
        forward_kernel,
        grid=(count,),
        in_specs=[
            pl.BlockSpec(memory_space=pltpu.SMEM),
            pl.BlockSpec(memory_space=pltpu.SMEM),
            pl.BlockSpec((2, local, width), lambda s: (0, 0, 0)),
        ],
        out_specs=pl.BlockSpec((2, slabs, 1, band, width), lambda s: (0, 0, s, 0, 0)),
        out_shape=jax.ShapeDtypeStruct((2, slabs, count, band, width), BF16),
        scratch_shapes=[pltpu.VMEM((SG, local), F32), pltpu.VMEM((SG, local), F32)],
        name="forward",
    )(first, subs, slab)


def adjoint_kernel(scale, slabs, first_ref, subs_ref, sent_ref, out_ref):
    tile = out_ref.shape[1]
    count = subs_ref.shape[1]
    band = SG // slabs
    start = first_ref[0] + pl.program_id(0) * tile
    yk = lax.broadcasted_iota(jnp.int32, (tile, SG), 0) + start
    c2, s2 = cis((UVSTEP * lax.broadcasted_iota(jnp.int32, (tile, SG), 1)) * yk)
    ys = lax.broadcasted_iota(jnp.int32, (tile, count), 0) + start
    c1, s1 = cis(ys * subs_ref[...])
    real = jnp.zeros(out_ref.shape[1:], F32)
    imag = jnp.zeros(out_ref.shape[1:], F32)
    dot = functools.partial(jnp.dot, preferred_element_type=F32)
    for s in range(count):
        a, b = c1[:, s:s + 1], s1[:, s:s + 1]
        tab_real = (a * c2 - b * s2).astype(BF16)
        tab_imag = (-(b * c2 + a * s2)).astype(BF16)
        re = jnp.concatenate([sent_ref[0, p, s] for p in range(slabs)], axis=0)
        im = jnp.concatenate([sent_ref[1, p, s] for p in range(slabs)], axis=0)
        real += dot(tab_real, re) + dot(tab_imag, im)
        imag += dot(tab_real, im) - dot(tab_imag, re)
    out_ref[0] = real * scale
    out_ref[1] = imag * scale


def adjoint(first, subs, sent, local):
    _, slabs, count, band, width = sent.shape
    tile = min(local, 256)
    return pl.pallas_call(
        functools.partial(adjoint_kernel, 1.0 / math.sqrt(count * SG), slabs),
        grid=(local // tile,),
        in_specs=[
            pl.BlockSpec(memory_space=pltpu.SMEM),
            pl.BlockSpec((1, count), lambda i: (0, 0)),
            pl.BlockSpec((2, slabs, count, band, width), lambda i: (0, 0, 0, 0, 0)),
        ],
        out_specs=pl.BlockSpec((2, tile, width), lambda i: (0, i, 0)),
        out_shape=jax.ShapeDtypeStruct((2, local, width), F32),
        name="adjoint",
    )(first, subs[None, :], sent)


def fused_kernel(
    scale, offset_ref, subs_hbm, slab_hbm, cell_hbm, value_hbm, weight_hbm,
    residual_ref, update_ref, last_ref, last_table,
    subs_ref, slab_ref, cell_ref, value_ref, weight_ref, low, high, acc, pb, rp, cb, rx, dg, zd, zf, zb, rz, sums, flat, full,
    table, turn, load,
    p_send, p_recv, x_send, x_recv, d_send, d_recv, z_send, z_recv, gz_send, gz_recv, gx_send, gx_recv, gc_send, gc_recv,
):
    facets, slabs = lax.axis_size("facet"), lax.axis_size("slab")
    q, z = lax.axis_index("facet"), lax.axis_index("slab")
    core, chip = q % 2, q // 2
    chips = facets // 2
    partner = q + 1 - 2 * core
    _, local, width = slab_ref.shape
    band = SG // slabs
    groups = band // 16
    parts = x_send.shape[1]
    share = band // parts
    dot = functools.partial(jnp.dot, preferred_element_type=F32)

    def at_chip(d):
        return 2 * (chip ^ d) + core

    def remote(src, dst, send, recv, **where):
        return pltpu.make_async_remote_copy(
            src_ref=src, dst_ref=dst, send_sem=send, recv_sem=recv,
            device_id=where, device_id_type=pl.DeviceIdType.MESH,
        )

    barrier = pltpu.get_barrier_semaphore()
    for e in range(1, slabs):
        pl.semaphore_signal(barrier, inc=1, device_id={"slab": z ^ e}, device_id_type=pl.DeviceIdType.MESH)
    for d in range(1, chips):
        pl.semaphore_signal(barrier, inc=1, device_id={"facet": at_chip(d)}, device_id_type=pl.DeviceIdType.MESH)
    pl.semaphore_signal(barrier, inc=1, device_id={"facet": partner}, device_id_type=pl.DeviceIdType.MESH)
    loads = [
        pltpu.make_async_copy(src, dst, load.at[i])
        for i, (src, dst) in enumerate(
            [
                (subs_hbm, subs_ref), (slab_hbm, slab_ref),
                (cell_hbm, cell_ref), (value_hbm, value_ref), (weight_hbm, weight_ref),
            ]
        )
    ]
    for copy in loads:
        copy.start()

    loads[0].wait()
    first = offset_ref[0] + z * local
    line = lax.broadcasted_iota(jnp.int32, (16, local), 1)

    places = line + first
    c, n = cis(UVSTEP * lax.broadcasted_iota(jnp.int32, (16, local), 0) * places)
    low[0] = c
    low[1] = n

    def partial_sum(i, other):
        row = lax.broadcasted_iota(jnp.int32, (chips * groups, local), 0)
        freq = UVSTEP * (band * (z ^ (slabs - 1 - i)) + 16 * (row % groups))
        for d in range(chips):
            freq += jnp.where(row // groups == d, subs_ref[at_chip(d) ^ other], 0)
        c, n = cis(freq * places[0:1])
        high[0] = c
        high[1] = n
        c2, s2 = low[0], low[1]
        cos, sin = [], []
        for g in range(chips * groups):
            c1, s1 = high[0, g:g + 1], high[1, g:g + 1]
            cos.append((c1 * c2 - s1 * s2).astype(BF16))
            sin.append((s1 * c2 + c1 * s2).astype(BF16))
        cos = jnp.concatenate(cos, axis=0)
        sin = jnp.concatenate(sin, axis=0)
        data = slab_ref[...].reshape(2 * local, width)
        both = jnp.concatenate(
            [jnp.concatenate([cos, sin], axis=1), jnp.concatenate([-sin, cos], axis=1)], axis=0
        )
        return dot(both, data).reshape(2, chips * band, width)

    def compute_other(i):
        pb[i] = partial_sum(i, 1).astype(BF16)

    def compute_own(i):
        acc[i] = partial_sum(i, 0)

    def pair_copy(i):
        return remote(pb.at[i], rp.at[i], p_send.at[i], p_recv.at[i], facet=partner)

    def part(h):
        return slice(h * share, (h + 1) * share)

    def x_copy(i, h, d):
        return remote(
            cb.at[i, d - 1, :, part(h)], rx.at[i, d - 1, :, part(h)],
            x_send.at[i, h, d - 1], x_recv.at[i, h, d - 1], facet=at_chip(d),
        )

    own, far = slabs - 1, chips - 1
    routed = [i for i in range(own) if (own - i) % 2 == 1]

    def d_copy(i, h):
        k = routed.index(i)
        return remote(
            cb.at[i, far - 1, :, part(h)], zd.at[k, :, part(h)], d_send.at[k, h], d_recv.at[k, h], slab=z ^ (own - i)
        )

    def ways(i):
        return [d for d in range(far, 0, -1) if d != far or i not in routed]

    def x_send_part(i, h):
        for d in ways(i):
            if i != own or d != far:
                x_copy(i, h, d).start()

    def pair_band(i):
        pair_copy(i).wait_recv()
        for d in range(far, 0, -1):
            at = slice(d * band, (d + 1) * band)
            for c in range(2):
                total = acc[i, c, at] + rp[i, c, at].astype(F32)
                if i == own and d == far:
                    dg[c] = total
                else:
                    cb[i, d - 1, c] = total.astype(BF16)
        x_send_part(i, 0)
        if i in routed:
            for h in range(parts):
                d_copy(i, h).start()
        for c in range(2):
            zf[i, c] = acc[i, c, 0:band] + rp[i, c, 0:band].astype(F32)

    def send_far(h):
        for i in routed:
            d_copy(i, h).wait()
        for c in range(2):
            total = dg[c, part(h)]
            for k in range(len(routed)):
                total += zd[k, c, part(h)].astype(F32)
            cb[own, far - 1, c, part(h)] = total.astype(BF16)
        x_copy(own, h, far).start()

    loads[1].wait()
    compute_other(0)
    pl.semaphore_wait(barrier, chips + slabs - 1)
    pair_copy(0).start()
    compute_own(0)
    for i in range(slabs):
        if i + 1 < slabs:
            compute_other(i + 1)
            pair_copy(i + 1).start()
        pair_band(i)
        if i + 1 < slabs:
            compute_own(i + 1)
    if parts == 2:
        for i in range(own - 1):
            x_send_part(i, 1)

    rows = sums.shape[1] // 3
    count = cell_ref.shape[1]
    chunk = min(count, 8192)
    for copy in loads[2:]:
        copy.wait()
    sums[...] = jnp.zeros_like(sums)

    def grid_step(i, carry):
        at = pl.ds(pl.multiple_of(i * chunk, chunk), chunk)
        cell = cell_ref[:, at]
        weight = weight_ref[:, at]
        row = lax.shift_right_logical(cell, width.bit_length() - 1).astype(F32)
        col = (cell & (width - 1)).astype(F32)
        lines = lax.broadcasted_iota(jnp.int32, (16, chunk), 0).astype(F32).astype(BF16)
        row = jnp.broadcast_to(row, (16, chunk)).astype(BF16)
        col = jnp.broadcast_to(col, (16, chunk)).astype(BF16)
        one, zero = jnp.ones((16, chunk), BF16), jnp.zeros((16, chunk), BF16)
        hot = jnp.concatenate(
            [jnp.where(col == lines + jnp.asarray(g, BF16), one, zero) for g in range(0, width, 16)], axis=0
        )
        terms = [weight * value_ref[0, :, at], weight * value_ref[1, :, at], weight]
        terms = [jnp.broadcast_to(t, (16, chunk)).astype(BF16) for t in terms]
        left = jnp.concatenate(
            [jnp.where(row == lines + jnp.asarray(g, BF16), t, zero) for t in terms for g in range(0, rows, 16)],
            axis=0,
        )
        sums[...] += lax.dot_general(hot, left, (((1,), (1,)), ((), ())), preferred_element_type=F32)
        return carry

    span = facets * share

    def table_band(t, carry):
        e, h = t // parts, t % parts
        lane = lax.broadcasted_iota(jnp.int32, (16, span), 1)
        freq = UVSTEP * (band * (z ^ e) + share * h + lane % share)
        for s in range(facets):
            freq += jnp.where(lane // share == s, subs_ref[s], 0)
        c2, s2 = cis(freq * lax.broadcasted_iota(jnp.int32, (16, span), 0))
        far = first + 16 * lax.broadcasted_iota(jnp.int32, (local // 16, span), 0)
        c, n = cis(freq[0:1] * far)
        turn[0] = c
        turn[1] = n

        def step(g, inner):
            c1, s1 = turn[0, pl.ds(g, 1)], turn[1, pl.ds(g, 1)]
            sin = (s1 * c2 + c1 * s2).astype(BF16)
            at = pl.ds(pl.multiple_of(g * 16, 16), 16)
            into = last_table if isinstance(t, int) else table.at[e, h]
            into[at, 0:span] = sin
            into[at, span:2 * span] = (c1 * c2 - s1 * s2).astype(BF16)
            into[at, 2 * span:3 * span] = -sin
            return inner

        lax.fori_loop(0, local // 16, step, 0)
        return carry

    chunks = count // chunk

    def grid(i):
        lax.fori_loop((i * chunks) // slabs, ((i + 1) * chunks) // slabs, grid_step, 0)

    def z_copy(i, h):
        return remote(
            zb.at[i, :, part(h)], rz.at[i, :, part(h)], z_send.at[i, h], z_recv.at[i, h], slab=z ^ (slabs - 1 - i)
        )

    def reduce_part(i, h):
        for d in ways(i):
            x_copy(i, h, d).wait()
        for c in range(2):
            total = zf[i, c, part(h)]
            for d in ways(i):
                total += rx[i, d - 1, c, part(h)].astype(F32)
            if i < slabs - 1:
                zb[i, c, part(h)] = total.astype(BF16)
            else:
                zf[i, c, part(h)] = total
        if i < slabs - 1:
            z_copy(i, h).start()

    def residual_part(h):
        for i in range(slabs - 1):
            z_copy(i, h).wait()
        for c in range(2):
            model = zf[slabs - 1, c, part(h)]
            for i in range(slabs - 1):
                model += rz[i, c, part(h)].astype(F32)
            at = h * share
            piece = flat[c * rows + at:c * rows + at + share]
            piece -= flat[2 * rows + at:2 * rows + at + share] * (model * scale)
            residual_ref[c, part(h)] = piece
            full[0, h, c, q] = piece.astype(BF16)

    def up_copy(e, h):
        return remote(
            full.at[0, h, :, q], full.at[e, h, :, q], gz_send.at[e - 1, h], gz_recv.at[e - 1, h],
            slab=z ^ e,
        )

    def across_copy(e, h, d):
        ref = full.at[e, h, :, q]
        return remote(ref, ref, gx_send.at[e, h, d - 1], gx_recv.at[e, h, d - 1], facet=at_chip(d))

    def spread_copy(e, h, d):
        ref = full.at[e, h, :, at_chip(d)]
        return remote(ref, ref, gc_send.at[e, h, d], gc_recv.at[e, h, d], facet=partner)

    def hand_on(e, h):
        if e:
            up_copy(e, h).wait_recv()
        else:
            for away in order[1:]:
                up_copy(away, h).start()
        for d in range(chips - 1, 0, -1):
            across_copy(e, h, d).start()
        spread_copy(e, h, 0).start()

    def relay(e, h):
        for d in range(1, chips):
            across_copy(e, h, d).wait_recv()
            spread_copy(e, h, d).start()

    tile = min(local, 1024)

    def gathered(e, h):
        for d in range(chips):
            spread_copy(e, h, d).wait_recv()

    def update_pass(e, h, begin=False):
        gathered(e, h)

        def step(i, carry):
            at = pl.ds(pl.multiple_of(i * tile, tile), tile)
            data = full[e, h].reshape(2 * span, width)
            imag = dot(table[e, h, at, 0:2 * span], data)
            real = dot(table[e, h, at, span:3 * span], data)
            if not begin:
                real += update_ref[0, at]
                imag += update_ref[1, at]
            update_ref[0, at] = real
            update_ref[1, at] = imag
            return carry

        lax.fori_loop(0, local // tile, step, 0)

    def tables(begin, end):
        final = last * parts + parts - 1
        if begin <= final < end:
            lax.fori_loop(begin, final, table_band, 0)
            table_band(final, 0)
            begin = final + 1
        if begin < end:
            lax.fori_loop(begin, end, table_band, 0)

    order = [0] + sorted(range(1, slabs), key=lambda e: (e != 1, -e))
    last = order[-1]
    units = slabs * parts
    final = parts - 1

    reduce_part(0, 0)
    grid(0)
    for i in range(1, own):
        reduce_part(i, 0)
        if i == 1:
            send_far(0)
            if parts == 2:
                x_send_part(own - 1, 1)
                x_send_part(own, 1)
        grid(i)
    if parts == 2:
        send_far(1)
        reduce_part(0, 1)
    grid(own)
    flat[...] = sums[...].T
    if parts == 2:
        for i in range(1, own - 1):
            reduce_part(i, 1)
    reduce_part(own, 0)
    residual_part(0)
    hand_on(0, 0)
    if parts == 2:
        reduce_part(own - 1, 1)
        tables(0, 2)
        reduce_part(own, 1)
        tables(2, 3)
        hand_on(1, 0)
        residual_part(1)
        hand_on(0, 1)
        for e in order[2:-1]:
            hand_on(e, 0)
        relay(0, 0)
        tables(3, 5)
        hand_on(last, 0)
        tables(5, units)
        hand_on(1, 1)
        relay(1, 0)
        update_pass(0, 0, True)
        for k, e in enumerate(order[2:]):
            hand_on(e, 1)
            if e != last:
                relay(e, 0)
                update_pass(order[k + 1], 0)
        relay(last, 0)
        relay(0, 1)
        for e in order[2:]:
            update_pass(e, 0)
    else:
        tables(0, units)
        for e in order[1:]:
            hand_on(e, 0)
        relay(0, 0)
    for k, e in enumerate(order[1:]):
        relay(e, final)
        update_pass(order[k], final, parts == 1 and k == 0)
    gathered(last, final)
    last_ref[...] = full[last, final]
    for i in range(slabs):
        pair_copy(i).wait_send()
    for e in range(slabs):
        for h in range(parts):
            if e:
                up_copy(e, h).wait_send()
            for d in range(chips):
                if d:
                    across_copy(e, h, d).wait_send()
                spread_copy(e, h, d).wait_send()


def finish_kernel(back, piece_ref, part_ref, last_ref, table_ref, residual_ref, update_ref, buffer, sent):
    dot = functools.partial(jnp.dot, preferred_element_type=F32)
    _, local, width = part_ref.shape
    span = table_ref.shape[1] // 3
    tiles, _, tile, _ = buffer.shape
    out = pltpu.make_async_copy(piece_ref, residual_ref, sent.at[tiles])
    out.start()

    def put(i):
        at = pl.ds(pl.multiple_of(i * tile, tile), tile)
        return pltpu.make_async_copy(buffer.at[i], update_ref.at[:, at], sent.at[i])

    def step(i, carry):
        at = pl.ds(pl.multiple_of(i * tile, tile), tile)
        data = last_ref[...].reshape(2 * span, width)
        imag = dot(table_ref[at, 0:2 * span], data)
        real = dot(table_ref[at, span:3 * span], data)
        buffer[i, 0] = (real + part_ref[0, at]) * back
        buffer[i, 1] = (imag + part_ref[1, at]) * back
        put(i).start()
        return carry

    lax.fori_loop(0, tiles, step, 0)
    for i in range(tiles):
        put(i).wait()
    out.wait()


def fused(offset, subs, slab, cells, values, weights, slabs, facets):
    _, local, width = slab.shape
    band = SG // slabs
    chips = facets // 2
    rows = -(-band // 16) * 16
    vmem = pl.BlockSpec(memory_space=pltpu.VMEM)
    dma = pltpu.SemaphoreType.DMA
    parts = 2 if band % 32 == 0 else 1
    share = band // parts
    span = facets * share
    piece, part, last, last_table = pl.pallas_call(
        functools.partial(fused_kernel, 1.0 / math.sqrt(local * slabs * facets)),
        in_specs=[pl.BlockSpec(memory_space=pltpu.SMEM)] + [pl.BlockSpec(memory_space=pltpu.HBM)] * 5,
        out_specs=[vmem] * 4,
        out_shape=[
            jax.ShapeDtypeStruct((2, band, width), F32),
            jax.ShapeDtypeStruct((2, local, width), F32),
            jax.ShapeDtypeStruct((2, facets, share, width), BF16),
            jax.ShapeDtypeStruct((local, 3 * span), BF16),
        ],
        scratch_shapes=[
            pltpu.SMEM(subs.shape, jnp.int32),
            pltpu.VMEM((2, local, width), BF16),
            pltpu.VMEM(cells.shape, jnp.int32),
            pltpu.VMEM(values.shape, F32),
            pltpu.VMEM(weights.shape, F32),
            pltpu.VMEM((2, 16, local), F32),
            pltpu.VMEM((2, chips * (band // 16), local), F32),
            pltpu.VMEM((slabs, 2, chips * band, width), F32),
            pltpu.VMEM((slabs, 2, chips * band, width), BF16),
            pltpu.VMEM((slabs, 2, chips * band, width), BF16),
            pltpu.VMEM((slabs, chips - 1, 2, band, width), BF16),
            pltpu.VMEM((slabs, chips - 1, 2, band, width), BF16),
            pltpu.VMEM((2, band, width), F32),
            pltpu.VMEM((slabs // 2, 2, band, width), BF16),
            pltpu.VMEM((slabs, 2, band, width), F32),
            pltpu.VMEM((slabs - 1, 2, band, width), BF16),
            pltpu.VMEM((slabs - 1, 2, band, width), BF16),
            pltpu.VMEM((width, 3 * rows), F32),
            pltpu.VMEM((3 * rows, width), F32),
            pltpu.VMEM((slabs, parts, 2, facets, share, width), BF16),
            pltpu.VMEM((slabs, parts, local, 3 * span), BF16),
            pltpu.VMEM((2, local // 16, span), F32),
            dma((5,)),
            dma((slabs,)), dma((slabs,)),
            dma((slabs, parts, chips - 1)), dma((slabs, parts, chips - 1)),
            dma((slabs // 2, parts)), dma((slabs // 2, parts)),
            dma((slabs - 1, parts)), dma((slabs - 1, parts)),
            dma((slabs - 1, parts)), dma((slabs - 1, parts)),
            dma((slabs, parts, chips - 1)), dma((slabs, parts, chips - 1)),
            dma((slabs, parts, chips)), dma((slabs, parts, chips)),
        ],
        compiler_params=pltpu.CompilerParams(collective_id=0, has_side_effects=True, vmem_limit_bytes=40 * 1024 * 1024),
        name="fused",
    )(offset, *[pltpu.with_memory_space_constraint(x, pltpu.HBM) for x in (subs, slab, cells, values, weights)])
    tiles = local // min(local, 256)
    return pl.pallas_call(
        functools.partial(finish_kernel, 1.0 / math.sqrt(subs.shape[0] * SG)),
        in_specs=[vmem] * 4,
        out_specs=[pl.BlockSpec(memory_space=pltpu.HBM)] * 2,
        out_shape=[
            jax.ShapeDtypeStruct((2, band, width), F32),
            jax.ShapeDtypeStruct((2, local, width), F32),
        ],
        scratch_shapes=[pltpu.VMEM((tiles, 2, local // tiles, width), F32), dma((tiles + 1,))],
        compiler_params=pltpu.CompilerParams(vmem_limit_bytes=8 * 1024 * 1024),
        name="finish",
    )(piece, part, last, last_table)


def body(slab, facet_offset, subgrid_offset, vis_cell, vis_value, vis_weight):
    slabs = lax.axis_size("slab")
    facets = lax.axis_size("facet")
    local_rows = slab.shape[2]
    width = slab.shape[3]
    count_sub = subgrid_offset.shape[0]
    band = SG // slabs
    owned = count_sub * band // facets
    first = (facet_offset + lax.axis_index("slab") * local_rows).astype(jnp.int32)
    chips = facets // 2
    paired = facets == 2 * chips and chips == 4 and slabs > 2 and slabs & (slabs - 1) == 0
    if owned == band and count_sub == facets and paired and band % 16 == 0 and local_rows % 256 == 0:
        residual, update = fused(
            facet_offset, subgrid_offset, slab[:, 0], vis_cell[0], vis_value[:, 0], vis_weight[0], slabs, facets
        )
        return (residual.reshape(2, 1, owned, width), update.reshape(2, 1, local_rows, width))
    sums = grid_visibilities(vis_cell[0], vis_value[:, 0, 0], vis_weight[0], owned, width)
    contrib = forward(first, subgrid_offset, slab[:, 0], slabs)
    contrib = contrib.reshape(2, slabs, facets, owned, width)
    parts = lax.all_to_all(contrib, "facet", 2, 2, tiled=True)
    parts = jnp.sum(parts, axis=2, dtype=F32).astype(BF16)
    parts = lax.all_to_all(parts, "slab", 1, 1, tiled=True)
    scale = 1.0 / math.sqrt(local_rows * slabs * facets)
    model = jnp.sum(parts, axis=1, dtype=F32) * scale
    residual = sums[:2] - sums[2:] * model
    sent = residual.astype(BF16).reshape(2, 1, 1, owned, width)
    piece = lax.all_gather(sent, "slab", axis=1, tiled=True)
    piece = lax.all_gather(piece, "facet", axis=2, tiled=True)
    piece = piece.reshape(2, slabs, count_sub, band, width)
    update = adjoint(first, subgrid_offset, piece, local_rows)
    return (residual.reshape(2, 1, owned, width), update.reshape(2, 1, local_rows, width))


def solution(mesh):
    placed = (
        P(None, "facet", "slab", None),
        P("facet"),
        P(),
        P("slab", "facet", None),
        P(None, "slab", "facet", None),
        P("slab", "facet", None),
    )
    return jax.shard_map(
        body,
        mesh=mesh,
        in_specs=placed,
        out_specs=(P(None, "slab", "facet", None), P(None, "facet", "slab", None)),
        check_vma=False,
    )
```

```python
import functools
import math

import jax
import jax.numpy as jnp
from jax import lax
from jax.experimental import pallas as pl
from jax.experimental.pallas import tpu as pltpu
from jax.sharding import PartitionSpec as P

IMAGE = 32768
SG = 256
UVSTEP = 16
F32 = jnp.float32
BF16 = jnp.bfloat16


def cis(turns):
    turns = turns & (IMAGE - 1)
    quarter = IMAGE // 4
    quad = (turns + quarter // 2) // quarter if quarter & (quarter - 1) else lax.shift_right_logical(
        turns + quarter // 2, quarter.bit_length() - 1
    )
    t = (turns - quad * quarter).astype(F32) * (2.0 * math.pi / IMAGE)
    z = t * t
    s = ((-1.9515295891e-4 * z + 8.3321608736e-3) * z - 1.6666654611e-1) * z * t + t
    c = ((2.443315711809948e-5 * z - 1.388731625493765e-3) * z + 4.166664568298827e-2) * z * z - 0.5 * z + 1.0
    odd = (quad & 1) == 1
    cos = jnp.where(odd, s, c)
    sin = jnp.where(odd, c, s)
    cos = jnp.where(((quad + 1) & 2) == 2, -cos, cos)
    sin = jnp.where((quad & 2) == 2, -sin, sin)
    return cos, sin


def grid_kernel(width, rows, cell_ref, value_ref, weight_ref, out_ref):
    @pl.when(pl.program_id(0) == 0)
    def _():
        out_ref[...] = jnp.zeros_like(out_ref)

    cell = cell_ref[...]
    weight = weight_ref[...]
    chunk = cell.shape[1]
    row = lax.shift_right_logical(cell, width.bit_length() - 1)
    col = cell & (width - 1)
    hot = jnp.where(lax.broadcasted_iota(jnp.int32, (width, chunk), 0) == col, 1.0, 0.0).astype(BF16)
    mine = lax.broadcasted_iota(jnp.int32, (rows, chunk), 0) == row
    terms = [weight * value_ref[0:1, :], weight * value_ref[1:2, :], weight]
    left = jnp.concatenate([jnp.where(mine, t, 0.0).astype(BF16) for t in terms], axis=0)
    out_ref[...] += lax.dot_general(left, hot, (((1,), (1,)), ((), ())), preferred_element_type=F32)


def grid_visibilities(cells, values, weights, owned, width):
    count = cells.shape[1]
    rows = -(-owned // 16) * 16
    chunk = min(count, 2048)
    out = pl.pallas_call(
        functools.partial(grid_kernel, width, rows),
        grid=(count // chunk,),
        in_specs=[
            pl.BlockSpec((1, chunk), lambda i: (0, i)),
            pl.BlockSpec((2, chunk), lambda i: (0, i)),
            pl.BlockSpec((1, chunk), lambda i: (0, i)),
        ],
        out_specs=pl.BlockSpec((3 * rows, width), lambda i: (0, 0)),
        out_shape=jax.ShapeDtypeStruct((3 * rows, width), F32),
        cost_estimate=pl.CostEstimate(flops=6 * rows * width * count, bytes_accessed=16 * count, transcendentals=0),
        name="gridding",
    )(cells, values, weights)
    return out.reshape(3, rows, width)[:, :owned]


def forward_kernel(first_ref, subs_ref, slab_ref, out_ref, cos_ref, sin_ref):
    s = pl.program_id(0)
    rows, local = cos_ref.shape
    first = first_ref[0]

    @pl.when(s == 0)
    def _():
        k = lax.broadcasted_iota(jnp.int32, (rows, local), 0)
        y = lax.broadcasted_iota(jnp.int32, (rows, local), 1) + first
        c, n = cis((UVSTEP * k) * y)
        cos_ref[...] = c
        sin_ref[...] = n

    y = lax.broadcasted_iota(jnp.int32, (8, local), 1) + first
    c1, s1 = cis(subs_ref[s] * y)
    c1, s1 = c1[0:1], s1[0:1]
    c2, s2 = cos_ref[...], sin_ref[...]
    tab_real = (c1 * c2 - s1 * s2).astype(BF16)
    tab_imag = (-(s1 * c2 + c1 * s2)).astype(BF16)
    re, im = slab_ref[0], slab_ref[1]
    dot = functools.partial(jnp.dot, preferred_element_type=F32)
    real = dot(tab_real, re) - dot(tab_imag, im)
    imag = dot(tab_real, im) + dot(tab_imag, re)
    slabs, band = out_ref.shape[1], out_ref.shape[3]
    for p in range(slabs):
        out_ref[0, p, 0] = real[p * band:(p + 1) * band].astype(out_ref.dtype)
        out_ref[1, p, 0] = imag[p * band:(p + 1) * band].astype(out_ref.dtype)


def forward(first, subs, slab, slabs):
    _, local, width = slab.shape
    count = subs.shape[0]
    band = SG // slabs
    return pl.pallas_call(
        forward_kernel,
        grid=(count,),
        in_specs=[
            pl.BlockSpec(memory_space=pltpu.SMEM),
            pl.BlockSpec(memory_space=pltpu.SMEM),
            pl.BlockSpec((2, local, width), lambda s: (0, 0, 0)),
        ],
        out_specs=pl.BlockSpec((2, slabs, 1, band, width), lambda s: (0, 0, s, 0, 0)),
        out_shape=jax.ShapeDtypeStruct((2, slabs, count, band, width), BF16),
        scratch_shapes=[pltpu.VMEM((SG, local), F32), pltpu.VMEM((SG, local), F32)],
        name="forward",
    )(first, subs, slab)


def adjoint_kernel(scale, slabs, first_ref, subs_ref, sent_ref, out_ref):
    tile = out_ref.shape[1]
    count = subs_ref.shape[1]
    band = SG // slabs
    start = first_ref[0] + pl.program_id(0) * tile
    yk = lax.broadcasted_iota(jnp.int32, (tile, SG), 0) + start
    c2, s2 = cis((UVSTEP * lax.broadcasted_iota(jnp.int32, (tile, SG), 1)) * yk)
    ys = lax.broadcasted_iota(jnp.int32, (tile, count), 0) + start
    c1, s1 = cis(ys * subs_ref[...])
    real = jnp.zeros(out_ref.shape[1:], F32)
    imag = jnp.zeros(out_ref.shape[1:], F32)
    dot = functools.partial(jnp.dot, preferred_element_type=F32)
    for s in range(count):
        a, b = c1[:, s:s + 1], s1[:, s:s + 1]
        tab_real = (a * c2 - b * s2).astype(BF16)
        tab_imag = (-(b * c2 + a * s2)).astype(BF16)
        re = jnp.concatenate([sent_ref[0, p, s] for p in range(slabs)], axis=0)
        im = jnp.concatenate([sent_ref[1, p, s] for p in range(slabs)], axis=0)
        real += dot(tab_real, re) + dot(tab_imag, im)
        imag += dot(tab_real, im) - dot(tab_imag, re)
    out_ref[0] = real * scale
    out_ref[1] = imag * scale


def adjoint(first, subs, sent, local):
    _, slabs, count, band, width = sent.shape
    tile = min(local, 256)
    return pl.pallas_call(
        functools.partial(adjoint_kernel, 1.0 / math.sqrt(count * SG), slabs),
        grid=(local // tile,),
        in_specs=[
            pl.BlockSpec(memory_space=pltpu.SMEM),
            pl.BlockSpec((1, count), lambda i: (0, 0)),
            pl.BlockSpec((2, slabs, count, band, width), lambda i: (0, 0, 0, 0, 0)),
        ],
        out_specs=pl.BlockSpec((2, tile, width), lambda i: (0, i, 0)),
        out_shape=jax.ShapeDtypeStruct((2, local, width), F32),
        name="adjoint",
    )(first, subs[None, :], sent)


def fused_kernel(
    scale, offset_ref, subs_hbm, slab_hbm, cell_hbm, value_hbm, weight_hbm,
    residual_ref, update_ref, last_ref, last_table,
    subs_ref, slab_ref, cell_ref, value_ref, weight_ref, low, high, acc, pb, rp, cb, rx, dg, zd, zf, zb, rz, sums, flat, full,
    table, turn, load,
    p_send, p_recv, x_send, x_recv, d_send, d_recv, z_send, z_recv, gz_send, gz_recv, gx_send, gx_recv, gc_send, gc_recv,
):
    facets, slabs = lax.axis_size("facet"), lax.axis_size("slab")
    q, z = lax.axis_index("facet"), lax.axis_index("slab")
    core, chip = q % 2, q // 2
    chips = facets // 2
    partner = q + 1 - 2 * core
    _, local, width = slab_ref.shape
    band = SG // slabs
    groups = band // 16
    parts = x_send.shape[1]
    share = band // parts
    dot = functools.partial(jnp.dot, preferred_element_type=F32)

    def at_chip(d):
        return 2 * (chip ^ d) + core

    def remote(src, dst, send, recv, **where):
        return pltpu.make_async_remote_copy(
            src_ref=src, dst_ref=dst, send_sem=send, recv_sem=recv,
            device_id=where, device_id_type=pl.DeviceIdType.MESH,
        )

    barrier = pltpu.get_barrier_semaphore()
    for e in range(1, slabs):
        pl.semaphore_signal(barrier, inc=1, device_id={"slab": z ^ e}, device_id_type=pl.DeviceIdType.MESH)
    for d in range(1, chips):
        pl.semaphore_signal(barrier, inc=1, device_id={"facet": at_chip(d)}, device_id_type=pl.DeviceIdType.MESH)
    pl.semaphore_signal(barrier, inc=1, device_id={"facet": partner}, device_id_type=pl.DeviceIdType.MESH)
    loads = [
        pltpu.make_async_copy(src, dst, load.at[i])
        for i, (src, dst) in enumerate(
            [
                (subs_hbm, subs_ref), (slab_hbm, slab_ref),
                (cell_hbm, cell_ref), (value_hbm, value_ref), (weight_hbm, weight_ref),
            ]
        )
    ]
    for copy in loads:
        copy.start()

    loads[0].wait()
    first = offset_ref[0] + z * local
    line = lax.broadcasted_iota(jnp.int32, (16, local), 1)

    places = line + first
    c, n = cis(UVSTEP * lax.broadcasted_iota(jnp.int32, (16, local), 0) * places)
    low[0] = c
    low[1] = n

    def partial_sum(i, other):
        row = lax.broadcasted_iota(jnp.int32, (chips * groups, local), 0)
        freq = UVSTEP * (band * (z ^ (slabs - 1 - i)) + 16 * (row % groups))
        for d in range(chips):
            freq += jnp.where(row // groups == d, subs_ref[at_chip(d) ^ other], 0)
        c, n = cis(freq * places[0:1])
        high[0] = c
        high[1] = n
        c2, s2 = low[0], low[1]
        cos, sin = [], []
        for g in range(chips * groups):
            c1, s1 = high[0, g:g + 1], high[1, g:g + 1]
            cos.append((c1 * c2 - s1 * s2).astype(BF16))
            sin.append((s1 * c2 + c1 * s2).astype(BF16))
        cos = jnp.concatenate(cos, axis=0)
        sin = jnp.concatenate(sin, axis=0)
        data = slab_ref[...].reshape(2 * local, width)
        both = jnp.concatenate(
            [jnp.concatenate([cos, sin], axis=1), jnp.concatenate([-sin, cos], axis=1)], axis=0
        )
        return dot(both, data).reshape(2, chips * band, width)

    def compute_other(i):
        pb[i] = partial_sum(i, 1).astype(BF16)

    def compute_own(i):
        acc[i] = partial_sum(i, 0)

    def pair_copy(i):
        return remote(pb.at[i], rp.at[i], p_send.at[i], p_recv.at[i], facet=partner)

    def part(h):
        return slice(h * share, (h + 1) * share)

    def x_copy(i, h, d):
        return remote(
            cb.at[i, d - 1, :, part(h)], rx.at[i, d - 1, :, part(h)],
            x_send.at[i, h, d - 1], x_recv.at[i, h, d - 1], facet=at_chip(d),
        )

    own, far = slabs - 1, chips - 1
    routed = [i for i in range(own) if (own - i) % 2 == 1]

    def d_copy(i, h):
        k = routed.index(i)
        return remote(
            cb.at[i, far - 1, :, part(h)], zd.at[k, :, part(h)], d_send.at[k, h], d_recv.at[k, h], slab=z ^ (own - i)
        )

    def ways(i):
        return [d for d in range(far, 0, -1) if d != far or i not in routed]

    def x_send_part(i, h):
        for d in ways(i):
            if i != own or d != far:
                x_copy(i, h, d).start()

    def pair_band(i):
        pair_copy(i).wait_recv()
        for d in range(far, 0, -1):
            at = slice(d * band, (d + 1) * band)
            for c in range(2):
                total = acc[i, c, at] + rp[i, c, at].astype(F32)
                if i == own and d == far:
                    dg[c] = total
                else:
                    cb[i, d - 1, c] = total.astype(BF16)
        x_send_part(i, 0)
        if i in routed:
            for h in range(parts):
                d_copy(i, h).start()
        for c in range(2):
            zf[i, c] = acc[i, c, 0:band] + rp[i, c, 0:band].astype(F32)

    def send_far(h):
        for i in routed:
            d_copy(i, h).wait()
        for c in range(2):
            total = dg[c, part(h)]
            for k in range(len(routed)):
                total += zd[k, c, part(h)].astype(F32)
            cb[own, far - 1, c, part(h)] = total.astype(BF16)
        x_copy(own, h, far).start()

    loads[1].wait()
    compute_other(0)
    pl.semaphore_wait(barrier, chips + slabs - 1)
    pair_copy(0).start()
    compute_own(0)
    for i in range(slabs):
        if i + 1 < slabs:
            compute_other(i + 1)
            pair_copy(i + 1).start()
        pair_band(i)
        if i + 1 < slabs:
            compute_own(i + 1)
    if parts == 2:
        for i in range(own - 1):
            x_send_part(i, 1)

    rows = sums.shape[1] // 3
    count = cell_ref.shape[1]
    chunk = min(count, 4096)
    for copy in loads[2:]:
        copy.wait()
    sums[...] = jnp.zeros_like(sums)

    def grid_step(i, carry):
        at = pl.ds(pl.multiple_of(i * chunk, chunk), chunk)
        cell = cell_ref[:, at]
        weight = weight_ref[:, at]
        row = lax.shift_right_logical(cell, width.bit_length() - 1).astype(F32)
        col = (cell & (width - 1)).astype(F32)
        lines = lax.broadcasted_iota(jnp.int32, (16, chunk), 0).astype(F32).astype(BF16)
        row = jnp.broadcast_to(row, (16, chunk)).astype(BF16)
        col = jnp.broadcast_to(col, (16, chunk)).astype(BF16)
        one, zero = jnp.ones((16, chunk), BF16), jnp.zeros((16, chunk), BF16)
        hot = jnp.concatenate(
            [jnp.where(col == lines + jnp.asarray(g, BF16), one, zero) for g in range(0, width, 16)], axis=0
        )
        terms = [weight * value_ref[0, :, at], weight * value_ref[1, :, at], weight]
        terms = [jnp.broadcast_to(t, (16, chunk)).astype(BF16) for t in terms]
        left = jnp.concatenate(
            [jnp.where(row == lines + jnp.asarray(g, BF16), t, zero) for t in terms for g in range(0, rows, 16)],
            axis=0,
        )
        sums[...] += lax.dot_general(hot, left, (((1,), (1,)), ((), ())), preferred_element_type=F32)
        return carry

    span = facets * share

    def table_band(t, carry):
        e, h = t // parts, t % parts
        lane = lax.broadcasted_iota(jnp.int32, (16, span), 1)
        freq = UVSTEP * (band * (z ^ e) + share * h + lane % share)
        for s in range(facets):
            freq += jnp.where(lane // share == s, subs_ref[s], 0)
        c2, s2 = cis(freq * lax.broadcasted_iota(jnp.int32, (16, span), 0))
        far = first + 16 * lax.broadcasted_iota(jnp.int32, (local // 16, span), 0)
        c, n = cis(freq[0:1] * far)
        turn[0] = c
        turn[1] = n

        def step(g, inner):
            c1, s1 = turn[0, pl.ds(g, 1)], turn[1, pl.ds(g, 1)]
            sin = (s1 * c2 + c1 * s2).astype(BF16)
            at = pl.ds(pl.multiple_of(g * 16, 16), 16)
            into = last_table if isinstance(t, int) else table.at[e, h]
            into[at, 0:span] = sin
            into[at, span:2 * span] = (c1 * c2 - s1 * s2).astype(BF16)
            into[at, 2 * span:3 * span] = -sin
            return inner

        lax.fori_loop(0, local // 16, step, 0)
        return carry

    chunks = count // chunk

    def grid(i):
        lax.fori_loop((i * chunks) // slabs, ((i + 1) * chunks) // slabs, grid_step, 0)

    def z_copy(i, h):
        return remote(
            zb.at[i, :, part(h)], rz.at[i, :, part(h)], z_send.at[i, h], z_recv.at[i, h], slab=z ^ (slabs - 1 - i)
        )

    def reduce_part(i, h):
        for d in ways(i):
            x_copy(i, h, d).wait()
        for c in range(2):
            total = zf[i, c, part(h)]
            for d in ways(i):
                total += rx[i, d - 1, c, part(h)].astype(F32)
            if i < slabs - 1:
                zb[i, c, part(h)] = total.astype(BF16)
            else:
                zf[i, c, part(h)] = total
        if i < slabs - 1:
            z_copy(i, h).start()

    def residual_part(h):
        for i in range(slabs - 1):
            z_copy(i, h).wait()
        for c in range(2):
            model = zf[slabs - 1, c, part(h)]
            for i in range(slabs - 1):
                model += rz[i, c, part(h)].astype(F32)
            at = h * share
            piece = flat[c * rows + at:c * rows + at + share]
            piece -= flat[2 * rows + at:2 * rows + at + share] * (model * scale)
            residual_ref[c, part(h)] = piece
            full[0, h, c, q] = piece.astype(BF16)

    def up_copy(e, h):
        return remote(
            full.at[0, h, :, q], full.at[e, h, :, q], gz_send.at[e - 1, h], gz_recv.at[e - 1, h],
            slab=z ^ e,
        )

    def across_copy(e, h, d):
        ref = full.at[e, h, :, q]
        return remote(ref, ref, gx_send.at[e, h, d - 1], gx_recv.at[e, h, d - 1], facet=at_chip(d))

    def spread_copy(e, h, d):
        ref = full.at[e, h, :, at_chip(d)]
        return remote(ref, ref, gc_send.at[e, h, d], gc_recv.at[e, h, d], facet=partner)

    def hand_on(e, h):
        if e:
            up_copy(e, h).wait_recv()
        else:
            for away in order[1:]:
                up_copy(away, h).start()
        for d in range(chips - 1, 0, -1):
            across_copy(e, h, d).start()
        spread_copy(e, h, 0).start()

    def relay(e, h):
        for d in range(1, chips):
            across_copy(e, h, d).wait_recv()
            spread_copy(e, h, d).start()

    tile = min(local, 1024)

    def gathered(e, h):
        for d in range(chips):
            spread_copy(e, h, d).wait_recv()

    def update_pass(e, h, begin=False):
        gathered(e, h)

        def step(i, carry):
            at = pl.ds(pl.multiple_of(i * tile, tile), tile)
            data = full[e, h].reshape(2 * span, width)
            imag = dot(table[e, h, at, 0:2 * span], data)
            real = dot(table[e, h, at, span:3 * span], data)
            if not begin:
                real += update_ref[0, at]
                imag += update_ref[1, at]
            update_ref[0, at] = real
            update_ref[1, at] = imag
            return carry

        lax.fori_loop(0, local // tile, step, 0)

    def tables(begin, end):
        final = last * parts + parts - 1
        if begin <= final < end:
            lax.fori_loop(begin, final, table_band, 0)
            table_band(final, 0)
            begin = final + 1
        if begin < end:
            lax.fori_loop(begin, end, table_band, 0)

    order = [0] + sorted(range(1, slabs), key=lambda e: (e != 1, -e))
    last = order[-1]
    units = slabs * parts
    final = parts - 1

    reduce_part(0, 0)
    grid(0)
    for i in range(1, own):
        reduce_part(i, 0)
        if i == 1:
            send_far(0)
            if parts == 2:
                x_send_part(own - 1, 1)
                x_send_part(own, 1)
        grid(i)
    if parts == 2:
        send_far(1)
        reduce_part(0, 1)
    grid(own)
    flat[...] = sums[...].T
    if parts == 2:
        for i in range(1, own - 1):
            reduce_part(i, 1)
    reduce_part(own, 0)
    residual_part(0)
    hand_on(0, 0)
    if parts == 2:
        reduce_part(own - 1, 1)
        tables(0, 2)
        reduce_part(own, 1)
        tables(2, 3)
        hand_on(1, 0)
        residual_part(1)
        hand_on(0, 1)
        for e in order[2:-1]:
            hand_on(e, 0)
        relay(0, 0)
        tables(3, 5)
        hand_on(last, 0)
        tables(5, units)
        hand_on(1, 1)
        relay(1, 0)
        update_pass(0, 0, True)
        for k, e in enumerate(order[2:]):
            hand_on(e, 1)
            if e != last:
                relay(e, 0)
                update_pass(order[k + 1], 0)
        relay(last, 0)
        relay(0, 1)
        for e in order[2:]:
            update_pass(e, 0)
    else:
        tables(0, units)
        for e in order[1:]:
            hand_on(e, 0)
        relay(0, 0)
    for k, e in enumerate(order[1:]):
        relay(e, final)
        update_pass(order[k], final, parts == 1 and k == 0)
    gathered(last, final)
    last_ref[...] = full[last, final]
    for i in range(slabs):
        pair_copy(i).wait_send()
    for e in range(slabs):
        for h in range(parts):
            if e:
                up_copy(e, h).wait_send()
            for d in range(chips):
                if d:
                    across_copy(e, h, d).wait_send()
                spread_copy(e, h, d).wait_send()


def finish_kernel(back, piece_ref, part_ref, last_ref, table_ref, residual_ref, update_ref, buffer, sent):
    dot = functools.partial(jnp.dot, preferred_element_type=F32)
    _, local, width = part_ref.shape
    span = table_ref.shape[1] // 3
    tiles, _, tile, _ = buffer.shape
    out = pltpu.make_async_copy(piece_ref, residual_ref, sent.at[tiles])
    out.start()

    def put(i):
        at = pl.ds(pl.multiple_of(i * tile, tile), tile)
        return pltpu.make_async_copy(buffer.at[i], update_ref.at[:, at], sent.at[i])

    def step(i, carry):
        at = pl.ds(pl.multiple_of(i * tile, tile), tile)
        data = last_ref[...].reshape(2 * span, width)
        imag = dot(table_ref[at, 0:2 * span], data)
        real = dot(table_ref[at, span:3 * span], data)
        buffer[i, 0] = (real + part_ref[0, at]) * back
        buffer[i, 1] = (imag + part_ref[1, at]) * back
        put(i).start()
        return carry

    lax.fori_loop(0, tiles, step, 0)
    for i in range(tiles):
        put(i).wait()
    out.wait()


def fused(offset, subs, slab, cells, values, weights, slabs, facets):
    _, local, width = slab.shape
    band = SG // slabs
    chips = facets // 2
    rows = -(-band // 16) * 16
    vmem = pl.BlockSpec(memory_space=pltpu.VMEM)
    dma = pltpu.SemaphoreType.DMA
    parts = 2 if band % 32 == 0 else 1
    share = band // parts
    span = facets * share
    piece, part, last, last_table = pl.pallas_call(
        functools.partial(fused_kernel, 1.0 / math.sqrt(local * slabs * facets)),
        in_specs=[pl.BlockSpec(memory_space=pltpu.SMEM)] + [pl.BlockSpec(memory_space=pltpu.HBM)] * 5,
        out_specs=[vmem] * 4,
        out_shape=[
            jax.ShapeDtypeStruct((2, band, width), F32),
            jax.ShapeDtypeStruct((2, local, width), F32),
            jax.ShapeDtypeStruct((2, facets, share, width), BF16),
            jax.ShapeDtypeStruct((local, 3 * span), BF16),
        ],
        scratch_shapes=[
            pltpu.SMEM(subs.shape, jnp.int32),
            pltpu.VMEM((2, local, width), BF16),
            pltpu.VMEM(cells.shape, jnp.int32),
            pltpu.VMEM(values.shape, F32),
            pltpu.VMEM(weights.shape, F32),
            pltpu.VMEM((2, 16, local), F32),
            pltpu.VMEM((2, chips * (band // 16), local), F32),
            pltpu.VMEM((slabs, 2, chips * band, width), F32),
            pltpu.VMEM((slabs, 2, chips * band, width), BF16),
            pltpu.VMEM((slabs, 2, chips * band, width), BF16),
            pltpu.VMEM((slabs, chips - 1, 2, band, width), BF16),
            pltpu.VMEM((slabs, chips - 1, 2, band, width), BF16),
            pltpu.VMEM((2, band, width), F32),
            pltpu.VMEM((slabs // 2, 2, band, width), BF16),
            pltpu.VMEM((slabs, 2, band, width), F32),
            pltpu.VMEM((slabs - 1, 2, band, width), BF16),
            pltpu.VMEM((slabs - 1, 2, band, width), BF16),
            pltpu.VMEM((width, 3 * rows), F32),
            pltpu.VMEM((3 * rows, width), F32),
            pltpu.VMEM((slabs, parts, 2, facets, share, width), BF16),
            pltpu.VMEM((slabs, parts, local, 3 * span), BF16),
            pltpu.VMEM((2, local // 16, span), F32),
            dma((5,)),
            dma((slabs,)), dma((slabs,)),
            dma((slabs, parts, chips - 1)), dma((slabs, parts, chips - 1)),
            dma((slabs // 2, parts)), dma((slabs // 2, parts)),
            dma((slabs - 1, parts)), dma((slabs - 1, parts)),
            dma((slabs - 1, parts)), dma((slabs - 1, parts)),
            dma((slabs, parts, chips - 1)), dma((slabs, parts, chips - 1)),
            dma((slabs, parts, chips)), dma((slabs, parts, chips)),
        ],
        compiler_params=pltpu.CompilerParams(collective_id=0, has_side_effects=True, vmem_limit_bytes=40 * 1024 * 1024),
        name="fused",
    )(offset, *[pltpu.with_memory_space_constraint(x, pltpu.HBM) for x in (subs, slab, cells, values, weights)])
    tiles = local // min(local, 256)
    return pl.pallas_call(
        functools.partial(finish_kernel, 1.0 / math.sqrt(subs.shape[0] * SG)),
        in_specs=[vmem] * 4,
        out_specs=[pl.BlockSpec(memory_space=pltpu.HBM)] * 2,
        out_shape=[
            jax.ShapeDtypeStruct((2, band, width), F32),
            jax.ShapeDtypeStruct((2, local, width), F32),
        ],
        scratch_shapes=[pltpu.VMEM((tiles, 2, local // tiles, width), F32), dma((tiles + 1,))],
        compiler_params=pltpu.CompilerParams(vmem_limit_bytes=8 * 1024 * 1024),
        name="finish",
    )(piece, part, last, last_table)


def body(slab, facet_offset, subgrid_offset, vis_cell, vis_value, vis_weight):
    slabs = lax.axis_size("slab")
    facets = lax.axis_size("facet")
    local_rows = slab.shape[2]
    width = slab.shape[3]
    count_sub = subgrid_offset.shape[0]
    band = SG // slabs
    owned = count_sub * band // facets
    first = (facet_offset + lax.axis_index("slab") * local_rows).astype(jnp.int32)
    chips = facets // 2
    paired = facets == 2 * chips and chips == 4 and slabs > 2 and slabs & (slabs - 1) == 0
    if owned == band and count_sub == facets and paired and band % 16 == 0 and local_rows % 256 == 0:
        residual, update = fused(
            facet_offset, subgrid_offset, slab[:, 0], vis_cell[0], vis_value[:, 0], vis_weight[0], slabs, facets
        )
        return (residual.reshape(2, 1, owned, width), update.reshape(2, 1, local_rows, width))
    sums = grid_visibilities(vis_cell[0], vis_value[:, 0, 0], vis_weight[0], owned, width)
    contrib = forward(first, subgrid_offset, slab[:, 0], slabs)
    contrib = contrib.reshape(2, slabs, facets, owned, width)
    parts = lax.all_to_all(contrib, "facet", 2, 2, tiled=True)
    parts = jnp.sum(parts, axis=2, dtype=F32).astype(BF16)
    parts = lax.all_to_all(parts, "slab", 1, 1, tiled=True)
    scale = 1.0 / math.sqrt(local_rows * slabs * facets)
    model = jnp.sum(parts, axis=1, dtype=F32) * scale
    residual = sums[:2] - sums[2:] * model
    sent = residual.astype(BF16).reshape(2, 1, 1, owned, width)
    piece = lax.all_gather(sent, "slab", axis=1, tiled=True)
    piece = lax.all_gather(piece, "facet", axis=2, tiled=True)
    piece = piece.reshape(2, slabs, count_sub, band, width)
    update = adjoint(first, subgrid_offset, piece, local_rows)
    return (residual.reshape(2, 1, owned, width), update.reshape(2, 1, local_rows, width))


def solution(mesh):
    placed = (
        P(None, "facet", "slab", None),
        P("facet"),
        P(),
        P("slab", "facet", None),
        P(None, "slab", "facet", None),
        P("slab", "facet", None),
    )
    return jax.shard_map(
        body,
        mesh=mesh,
        in_specs=placed,
        out_specs=(P(None, "slab", "facet", None), P(None, "facet", "slab", None)),
        check_vma=False,
    )
```

```python
import functools
import math

import jax
import jax.numpy as jnp
from jax import lax
from jax.experimental import pallas as pl
from jax.experimental.pallas import tpu as pltpu
from jax.sharding import PartitionSpec as P

IMAGE = 32768
SG = 256
UVSTEP = 16
F32 = jnp.float32
BF16 = jnp.bfloat16
GRID = 8192
GRID_LATE = 0
TILE = 1024


def cis(turns):
    turns = turns & (IMAGE - 1)
    quarter = IMAGE // 4
    quad = (turns + quarter // 2) // quarter if quarter & (quarter - 1) else lax.shift_right_logical(
        turns + quarter // 2, quarter.bit_length() - 1
    )
    t = (turns - quad * quarter).astype(F32) * (2.0 * math.pi / IMAGE)
    z = t * t
    s = ((-1.9515295891e-4 * z + 8.3321608736e-3) * z - 1.6666654611e-1) * z * t + t
    c = ((2.443315711809948e-5 * z - 1.388731625493765e-3) * z + 4.166664568298827e-2) * z * z - 0.5 * z + 1.0
    odd = (quad & 1) == 1
    cos = jnp.where(odd, s, c)
    sin = jnp.where(odd, c, s)
    cos = jnp.where(((quad + 1) & 2) == 2, -cos, cos)
    sin = jnp.where((quad & 2) == 2, -sin, sin)
    return cos, sin


def grid_kernel(width, rows, cell_ref, value_ref, weight_ref, out_ref):
    @pl.when(pl.program_id(0) == 0)
    def _():
        out_ref[...] = jnp.zeros_like(out_ref)

    cell = cell_ref[...]
    weight = weight_ref[...]
    chunk = cell.shape[1]
    row = lax.shift_right_logical(cell, width.bit_length() - 1)
    col = cell & (width - 1)
    hot = jnp.where(lax.broadcasted_iota(jnp.int32, (width, chunk), 0) == col, 1.0, 0.0).astype(BF16)
    mine = lax.broadcasted_iota(jnp.int32, (rows, chunk), 0) == row
    terms = [weight * value_ref[0:1, :], weight * value_ref[1:2, :], weight]
    left = jnp.concatenate([jnp.where(mine, t, 0.0).astype(BF16) for t in terms], axis=0)
    out_ref[...] += lax.dot_general(left, hot, (((1,), (1,)), ((), ())), preferred_element_type=F32)


def grid_visibilities(cells, values, weights, owned, width):
    count = cells.shape[1]
    rows = -(-owned // 16) * 16
    chunk = min(count, 2048)
    out = pl.pallas_call(
        functools.partial(grid_kernel, width, rows),
        grid=(count // chunk,),
        in_specs=[
            pl.BlockSpec((1, chunk), lambda i: (0, i)),
            pl.BlockSpec((2, chunk), lambda i: (0, i)),
            pl.BlockSpec((1, chunk), lambda i: (0, i)),
        ],
        out_specs=pl.BlockSpec((3 * rows, width), lambda i: (0, 0)),
        out_shape=jax.ShapeDtypeStruct((3 * rows, width), F32),
        cost_estimate=pl.CostEstimate(flops=6 * rows * width * count, bytes_accessed=16 * count, transcendentals=0),
        name="gridding",
    )(cells, values, weights)
    return out.reshape(3, rows, width)[:, :owned]


def forward_kernel(first_ref, subs_ref, slab_ref, out_ref, cos_ref, sin_ref):
    s = pl.program_id(0)
    rows, local = cos_ref.shape
    first = first_ref[0]

    @pl.when(s == 0)
    def _():
        k = lax.broadcasted_iota(jnp.int32, (rows, local), 0)
        y = lax.broadcasted_iota(jnp.int32, (rows, local), 1) + first
        c, n = cis((UVSTEP * k) * y)
        cos_ref[...] = c
        sin_ref[...] = n

    y = lax.broadcasted_iota(jnp.int32, (8, local), 1) + first
    c1, s1 = cis(subs_ref[s] * y)
    c1, s1 = c1[0:1], s1[0:1]
    c2, s2 = cos_ref[...], sin_ref[...]
    tab_real = (c1 * c2 - s1 * s2).astype(BF16)
    tab_imag = (-(s1 * c2 + c1 * s2)).astype(BF16)
    re, im = slab_ref[0], slab_ref[1]
    dot = functools.partial(jnp.dot, preferred_element_type=F32)
    real = dot(tab_real, re) - dot(tab_imag, im)
    imag = dot(tab_real, im) + dot(tab_imag, re)
    slabs, band = out_ref.shape[1], out_ref.shape[3]
    for p in range(slabs):
        out_ref[0, p, 0] = real[p * band:(p + 1) * band].astype(out_ref.dtype)
        out_ref[1, p, 0] = imag[p * band:(p + 1) * band].astype(out_ref.dtype)


def forward(first, subs, slab, slabs):
    _, local, width = slab.shape
    count = subs.shape[0]
    band = SG // slabs
    return pl.pallas_call(
        forward_kernel,
        grid=(count,),
        in_specs=[
            pl.BlockSpec(memory_space=pltpu.SMEM),
            pl.BlockSpec(memory_space=pltpu.SMEM),
            pl.BlockSpec((2, local, width), lambda s: (0, 0, 0)),
        ],
        out_specs=pl.BlockSpec((2, slabs, 1, band, width), lambda s: (0, 0, s, 0, 0)),
        out_shape=jax.ShapeDtypeStruct((2, slabs, count, band, width), BF16),
        scratch_shapes=[pltpu.VMEM((SG, local), F32), pltpu.VMEM((SG, local), F32)],
        name="forward",
    )(first, subs, slab)


def adjoint_kernel(scale, slabs, first_ref, subs_ref, sent_ref, out_ref):
    tile = out_ref.shape[1]
    count = subs_ref.shape[1]
    band = SG // slabs
    start = first_ref[0] + pl.program_id(0) * tile
    yk = lax.broadcasted_iota(jnp.int32, (tile, SG), 0) + start
    c2, s2 = cis((UVSTEP * lax.broadcasted_iota(jnp.int32, (tile, SG), 1)) * yk)
    ys = lax.broadcasted_iota(jnp.int32, (tile, count), 0) + start
    c1, s1 = cis(ys * subs_ref[...])
    real = jnp.zeros(out_ref.shape[1:], F32)
    imag = jnp.zeros(out_ref.shape[1:], F32)
    dot = functools.partial(jnp.dot, preferred_element_type=F32)
    for s in range(count):
        a, b = c1[:, s:s + 1], s1[:, s:s + 1]
        tab_real = (a * c2 - b * s2).astype(BF16)
        tab_imag = (-(b * c2 + a * s2)).astype(BF16)
        re = jnp.concatenate([sent_ref[0, p, s] for p in range(slabs)], axis=0)
        im = jnp.concatenate([sent_ref[1, p, s] for p in range(slabs)], axis=0)
        real += dot(tab_real, re) + dot(tab_imag, im)
        imag += dot(tab_real, im) - dot(tab_imag, re)
    out_ref[0] = real * scale
    out_ref[1] = imag * scale


def adjoint(first, subs, sent, local):
    _, slabs, count, band, width = sent.shape
    tile = min(local, 256)
    return pl.pallas_call(
        functools.partial(adjoint_kernel, 1.0 / math.sqrt(count * SG), slabs),
        grid=(local // tile,),
        in_specs=[
            pl.BlockSpec(memory_space=pltpu.SMEM),
            pl.BlockSpec((1, count), lambda i: (0, 0)),
            pl.BlockSpec((2, slabs, count, band, width), lambda i: (0, 0, 0, 0, 0)),
        ],
        out_specs=pl.BlockSpec((2, tile, width), lambda i: (0, i, 0)),
        out_shape=jax.ShapeDtypeStruct((2, local, width), F32),
        name="adjoint",
    )(first, subs[None, :], sent)


def fused_kernel(
    scale, offset_ref, subs_hbm, slab_hbm, cell_hbm, value_hbm, weight_hbm,
    residual_ref, update_ref, last_ref, table,
    subs_ref, slab_ref, cell_ref, value_ref, weight_ref, low, high, acc, pb, rp, cb, rx, dg, zd, zf, zb, rz, sums, flat, full,
    turn, load,
    p_send, p_recv, x_send, x_recv, d_send, d_recv, z_send, z_recv, gz_send, gz_recv, gx_send, gx_recv, gc_send, gc_recv,
):
    facets, slabs = lax.axis_size("facet"), lax.axis_size("slab")
    q, z = lax.axis_index("facet"), lax.axis_index("slab")
    core, chip = q % 2, q // 2
    chips = facets // 2
    partner = q + 1 - 2 * core
    _, local, width = slab_ref.shape
    band = SG // slabs
    groups = band // 16
    parts = x_send.shape[1]
    share = band // parts
    dot = functools.partial(jnp.dot, preferred_element_type=F32)

    def at_chip(d):
        return 2 * (chip ^ d) + core

    def remote(src, dst, send, recv, **where):
        return pltpu.make_async_remote_copy(
            src_ref=src, dst_ref=dst, send_sem=send, recv_sem=recv,
            device_id=where, device_id_type=pl.DeviceIdType.MESH,
        )

    barrier = pltpu.get_barrier_semaphore()
    for e in range(1, slabs):
        pl.semaphore_signal(barrier, inc=1, device_id={"slab": z ^ e}, device_id_type=pl.DeviceIdType.MESH)
    for d in range(1, chips):
        pl.semaphore_signal(barrier, inc=1, device_id={"facet": at_chip(d)}, device_id_type=pl.DeviceIdType.MESH)
    pl.semaphore_signal(barrier, inc=1, device_id={"facet": partner}, device_id_type=pl.DeviceIdType.MESH)
    loads = [
        pltpu.make_async_copy(src, dst, load.at[i])
        for i, (src, dst) in enumerate(
            [
                (subs_hbm, subs_ref), (slab_hbm, slab_ref),
                (cell_hbm, cell_ref), (value_hbm, value_ref), (weight_hbm, weight_ref),
            ]
        )
    ]
    for copy in loads:
        copy.start()

    loads[0].wait()
    first = offset_ref[0] + z * local
    line = lax.broadcasted_iota(jnp.int32, (16, local), 1)

    places = line + first
    c, n = cis(UVSTEP * lax.broadcasted_iota(jnp.int32, (16, local), 0) * places)
    low[0] = c
    low[1] = n

    def partial_sum(i, other):
        row = lax.broadcasted_iota(jnp.int32, (chips * groups, local), 0)
        freq = UVSTEP * (band * (z ^ (slabs - 1 - i)) + 16 * (row % groups))
        for d in range(chips):
            freq += jnp.where(row // groups == d, subs_ref[at_chip(d) ^ other], 0)
        c, n = cis(freq * places[0:1])
        high[0] = c
        high[1] = n
        c2, s2 = low[0], low[1]
        cos, sin = [], []
        for g in range(chips * groups):
            c1, s1 = high[0, g:g + 1], high[1, g:g + 1]
            cos.append((c1 * c2 - s1 * s2).astype(BF16))
            sin.append((s1 * c2 + c1 * s2).astype(BF16))
        cos = jnp.concatenate(cos, axis=0)
        sin = jnp.concatenate(sin, axis=0)
        data = slab_ref[...].reshape(2 * local, width)
        both = jnp.concatenate(
            [jnp.concatenate([cos, sin], axis=1), jnp.concatenate([-sin, cos], axis=1)], axis=0
        )
        return dot(both, data).reshape(2, chips * band, width)

    def pair_copy(i):
        return remote(pb.at[i], rp.at[i], p_send.at[i], p_recv.at[i], facet=partner)

    def part(h):
        return slice(h * share, (h + 1) * share)

    def x_copy(i, h, d):
        return remote(
            cb.at[i, d - 1, :, part(h)], rx.at[i, d - 1, :, part(h)],
            x_send.at[i, h, d - 1], x_recv.at[i, h, d - 1], facet=at_chip(d),
        )

    own, far = slabs - 1, chips - 1

    def routed(i):
        return i % 2 == 0

    def d_copy(i, h):
        return remote(
            cb.at[i, far - 1, :, part(h)], zd.at[i // 2, :, part(h)], d_send.at[i // 2, h], d_recv.at[i // 2, h],
            slab=z ^ (own - i),
        )

    def ways(i):
        return [d for d in range(far, 0, -1) if d != far or not routed(i)]

    def x_send_part(i, h):
        for d in ways(i):
            if i != own or d != far:
                x_copy(i, h, d).start()

    def pair_band(i, mine):
        pair_copy(i).wait_recv()
        for d in range(far, 0, -1):
            at = slice(d * band, (d + 1) * band)
            for c in range(2):
                total = acc[i, c, at] + rp[i, c, at].astype(F32)
                if mine and d == far:
                    dg[c] = total
                else:
                    cb[i, d - 1, c] = total.astype(BF16)
        if not mine and routed(i):
            for h in range(parts):
                d_copy(i, h).start()
        elif not mine:
            x_copy(i, 0, far).start()
        for d in range(far - 1, 0, -1):
            x_copy(i, 0, d).start()
        for c in range(2):
            zf[i, c] = acc[i, c, 0:band] + rp[i, c, 0:band].astype(F32)

    def send_far(h):
        for i in range(0, own, 2):
            d_copy(i, h).wait()
        for c in range(2):
            total = dg[c, part(h)]
            for k in range(slabs // 2):
                total += zd[k, c, part(h)].astype(F32)
            cb[own, far - 1, c, part(h)] = total.astype(BF16)
        x_copy(own, h, far).start()

    loads[1].wait()
    for i in range(slabs):
        pb[i] = partial_sum(i, 1).astype(BF16)
        if i == 0:
            pl.semaphore_wait(barrier, chips + slabs - 1)
        pair_copy(i).start()
        if i > 0:
            pair_band(i - 1, False)
        acc[i] = partial_sum(i, 0)
    pair_band(own, True)
    for i in range(own - 1):
        x_send_part(i, 1)

    rows = sums.shape[1] // 3
    count = cell_ref.shape[1]
    chunk = min(count, GRID)
    for copy in loads[2:]:
        copy.wait()
    sums[...] = jnp.zeros_like(sums)

    def grid_step(i, carry):
        at = pl.ds(pl.multiple_of(i * chunk, chunk), chunk)
        cell = cell_ref[:, at]
        weight = weight_ref[:, at]
        row = lax.shift_right_logical(cell, width.bit_length() - 1).astype(F32)
        col = (cell & (width - 1)).astype(F32)
        lines = lax.broadcasted_iota(jnp.int32, (16, chunk), 0).astype(F32).astype(BF16)
        row = jnp.broadcast_to(row, (16, chunk)).astype(BF16)
        col = jnp.broadcast_to(col, (16, chunk)).astype(BF16)
        one, zero = jnp.ones((16, chunk), BF16), jnp.zeros((16, chunk), BF16)
        hot = jnp.concatenate(
            [jnp.where(col == lines + jnp.asarray(g, BF16), one, zero) for g in range(0, width, 16)], axis=0
        )
        terms = [weight * value_ref[0, :, at], weight * value_ref[1, :, at], weight]
        terms = [jnp.broadcast_to(t, (16, chunk)).astype(BF16) for t in terms]
        left = jnp.concatenate(
            [jnp.where(row == lines + jnp.asarray(g, BF16), t, zero) for t in terms for g in range(0, rows, 16)],
            axis=0,
        )
        sums[...] += lax.dot_general(hot, left, (((1,), (1,)), ((), ())), preferred_element_type=F32)
        return carry

    span = facets * share

    def table_band(t, carry):
        e, h = t // parts, t % parts
        lane = lax.broadcasted_iota(jnp.int32, (16, span), 1)
        freq = UVSTEP * (band * (z ^ e) + share * h + lane % share)
        for s in range(facets):
            freq += jnp.where(lane // share == s, subs_ref[s], 0)
        c2, s2 = cis(freq * lax.broadcasted_iota(jnp.int32, (16, span), 0))
        far = first + 16 * lax.broadcasted_iota(jnp.int32, (local // 16, span), 0)
        c, n = cis(freq[0:1] * far)
        turn[0] = c
        turn[1] = n

        def step(g, inner):
            c1, s1 = turn[0, pl.ds(g, 1)], turn[1, pl.ds(g, 1)]
            sin = (s1 * c2 + c1 * s2).astype(BF16)
            at = pl.ds(pl.multiple_of(g * 16, 16), 16)
            into = table.at[e, h]
            into[at, 0:span] = sin
            into[at, span:2 * span] = (c1 * c2 - s1 * s2).astype(BF16)
            into[at, 2 * span:3 * span] = -sin
            return inner

        lax.fori_loop(0, local // 16, step, 0)
        return carry

    chunks = count // chunk

    def z_copy(i, h):
        return remote(
            zb.at[i, :, part(h)], rz.at[i, :, part(h)], z_send.at[i, h], z_recv.at[i, h], slab=z ^ (slabs - 1 - i)
        )

    def reduce_part(i, h):
        for d in ways(i):
            x_copy(i, h, d).wait()
        for c in range(2):
            total = zf[i, c, part(h)]
            for d in ways(i):
                total += rx[i, d - 1, c, part(h)].astype(F32)
            if i < slabs - 1:
                zb[i, c, part(h)] = total.astype(BF16)
            else:
                zf[i, c, part(h)] = total
        if i < slabs - 1:
            z_copy(i, h).start()

    def residual_part(h):
        for i in range(slabs - 1):
            z_copy(i, h).wait()
        for c in range(2):
            model = zf[slabs - 1, c, part(h)]
            for i in range(slabs - 1):
                model += rz[i, c, part(h)].astype(F32)
            at = h * share
            piece = flat[c * rows + at:c * rows + at + share]
            piece -= flat[2 * rows + at:2 * rows + at + share] * (model * scale)
            residual_ref[c, part(h)] = piece
            full[0, h, c, q] = piece.astype(BF16)

    def up_copy(e, h):
        return remote(
            full.at[0, h, :, q], full.at[e, h, :, q], gz_send.at[e - 1, h], gz_recv.at[e - 1, h],
            slab=z ^ e,
        )

    def across_copy(e, h, d):
        ref = full.at[e, h, :, q]
        return remote(ref, ref, gx_send.at[e, h, d - 1], gx_recv.at[e, h, d - 1], facet=at_chip(d))

    def spread_copy(e, h, d):
        ref = full.at[e, h, :, at_chip(d)]
        return remote(ref, ref, gc_send.at[e, h, d], gc_recv.at[e, h, d], facet=partner)

    def hand_on(e, h):
        if e:
            up_copy(e, h).wait_recv()
        else:
            for away in order[1:]:
                up_copy(away, h).start()
        for d in range(chips - 1, 0, -1):
            across_copy(e, h, d).start()
        spread_copy(e, h, 0).start()

    def relay(e, h):
        for d in range(1, chips):
            across_copy(e, h, d).wait_recv()
            spread_copy(e, h, d).start()

    tile = min(local, TILE)

    def gathered(e, h):
        for d in range(chips):
            spread_copy(e, h, d).wait_recv()

    order = [k ^ (k >> 1) for k in range(slabs)]
    last = order[-1]
    units = slabs * parts

    def looped(count, work, before, after):
        def step(k, carry):
            for at, events in before.items():
                @pl.when(k == at)
                def _():
                    for event in events:
                        event()
            work(k)
            for at, events in after.items():
                @pl.when(k == at)
                def _():
                    for event in events:
                        event()
            return carry

        lax.fori_loop(0, count, step, 0)

    def update_pass(k):
        j, h = k % slabs, k // slabs
        e = j ^ lax.shift_right_logical(j, 1)
        gathered(e, h)

        def step(i, carry):
            at = pl.ds(pl.multiple_of(i * tile, tile), tile)
            data = full[e, h].reshape(2 * span, width)
            update_ref[1, at] += dot(table[e, h, at, 0:2 * span], data)
            update_ref[0, at] += dot(table[e, h, at, span:3 * span], data)
            return carry

        lax.fori_loop(0, local // tile, step, 0)

    def call(f, *args):
        return functools.partial(f, *args)

    reduce_part(0, 0)
    after = {}
    for i in range(1, own):
        after.setdefault(min(chunks - 1, i + GRID_LATE), []).append(call(reduce_part, i, 0))
        if i == 1:
            after[min(chunks - 1, i + GRID_LATE)] += [
                call(send_far, 0), call(x_send_part, own - 1, 1), call(x_send_part, own, 1)
            ]
    after.setdefault(max(chunks - 2, 0), []).extend([call(send_far, 1), call(reduce_part, 0, 1)])
    looped(chunks, lambda k: grid_step(k, 0), {}, after)
    flat[...] = sums[...].T
    update_ref[...] = jnp.zeros_like(update_ref)
    for i in range(1, own - 1):
        reduce_part(i, 1)
    reduce_part(own, 0)
    residual_part(0)
    hand_on(0, 0)
    reduce_part(own - 1, 1)
    middle = [call(hand_on, 1, 0), call(residual_part, 1), call(hand_on, 0, 1)]
    middle += [call(hand_on, e, 0) for e in order[2:-1]] + [call(relay, 0, 0)]
    looped(
        units, lambda t: table_band(t, 0), {},
        {1: [call(reduce_part, own, 1)], 2: middle, 4: [call(hand_on, last, 0)]},
    )
    hand_on(1, 1)
    relay(1, 0)
    before = {}
    for k, e in enumerate(order[2:]):
        before[k + 1] = [call(hand_on, e, 1), call(relay, e, 0)]
    before[slabs - 2] += [call(relay, 0, 1)]
    for k, e in enumerate(order[1:]):
        before[slabs + k] = [call(relay, e, 1)]
    looped(units - 1, update_pass, before, {})
    gathered(last, parts - 1)
    last_ref[...] = full[last, parts - 1]
    for i in range(slabs):
        pair_copy(i).wait_send()
    for e in range(slabs):
        for h in range(parts):
            if e:
                up_copy(e, h).wait_send()
            for d in range(chips):
                if d:
                    across_copy(e, h, d).wait_send()
                spread_copy(e, h, d).wait_send()


def finish_kernel(back, piece_ref, part_ref, last_ref, table_ref, residual_ref, update_ref, buffer, sent):
    dot = functools.partial(jnp.dot, preferred_element_type=F32)
    _, local, width = part_ref.shape
    slabs, parts, _, span = table_ref.shape
    span //= 3
    last = (slabs - 1) ^ ((slabs - 1) >> 1)
    tiles, _, tile, _ = buffer.shape
    out = pltpu.make_async_copy(piece_ref, residual_ref, sent.at[tiles])
    out.start()

    def put(i):
        at = pl.ds(i * tile, tile)
        return pltpu.make_async_copy(buffer.at[i], update_ref.at[:, at], sent.at[i])

    def step(i, carry):
        at = pl.ds(i * tile, tile)
        data = last_ref[...].reshape(2 * span, width)
        imag = dot(table_ref[last, parts - 1, at, 0:2 * span], data)
        real = dot(table_ref[last, parts - 1, at, span:3 * span], data)
        buffer[i, 0] = (real + part_ref[0, at]) * back
        buffer[i, 1] = (imag + part_ref[1, at]) * back
        put(i).start()
        return carry

    for i in range(tiles):
        step(i, 0)
    for i in range(tiles):
        put(i).wait()
    out.wait()


def fused(offset, subs, slab, cells, values, weights, slabs, facets):
    _, local, width = slab.shape
    band = SG // slabs
    chips = facets // 2
    rows = -(-band // 16) * 16
    vmem = pl.BlockSpec(memory_space=pltpu.VMEM)
    dma = pltpu.SemaphoreType.DMA
    parts = 2
    share = band // parts
    span = facets * share
    piece, part, last, last_table = pl.pallas_call(
        functools.partial(fused_kernel, 1.0 / math.sqrt(local * slabs * facets)),
        in_specs=[pl.BlockSpec(memory_space=pltpu.SMEM)] + [pl.BlockSpec(memory_space=pltpu.HBM)] * 5,
        out_specs=[vmem] * 4,
        out_shape=[
            jax.ShapeDtypeStruct((2, band, width), F32),
            jax.ShapeDtypeStruct((2, local, width), F32),
            jax.ShapeDtypeStruct((2, facets, share, width), BF16),
            jax.ShapeDtypeStruct((slabs, parts, local, 3 * span), BF16),
        ],
        scratch_shapes=[
            pltpu.SMEM(subs.shape, jnp.int32),
            pltpu.VMEM((2, local, width), BF16),
            pltpu.VMEM(cells.shape, jnp.int32),
            pltpu.VMEM(values.shape, F32),
            pltpu.VMEM(weights.shape, F32),
            pltpu.VMEM((2, 16, local), F32),
            pltpu.VMEM((2, chips * (band // 16), local), F32),
            pltpu.VMEM((slabs, 2, chips * band, width), F32),
            pltpu.VMEM((slabs, 2, chips * band, width), BF16),
            pltpu.VMEM((slabs, 2, chips * band, width), BF16),
            pltpu.VMEM((slabs, chips - 1, 2, band, width), BF16),
            pltpu.VMEM((slabs, chips - 1, 2, band, width), BF16),
            pltpu.VMEM((2, band, width), F32),
            pltpu.VMEM((slabs // 2, 2, band, width), BF16),
            pltpu.VMEM((slabs, 2, band, width), F32),
            pltpu.VMEM((slabs - 1, 2, band, width), BF16),
            pltpu.VMEM((slabs - 1, 2, band, width), BF16),
            pltpu.VMEM((width, 3 * rows), F32),
            pltpu.VMEM((3 * rows, width), F32),
            pltpu.VMEM((slabs, parts, 2, facets, share, width), BF16),
            pltpu.VMEM((2, local // 16, span), F32),
            dma((5,)),
            dma((slabs,)), dma((slabs,)),
            dma((slabs, parts, chips - 1)), dma((slabs, parts, chips - 1)),
            dma((slabs // 2, parts)), dma((slabs // 2, parts)),
            dma((slabs - 1, parts)), dma((slabs - 1, parts)),
            dma((slabs - 1, parts)), dma((slabs - 1, parts)),
            dma((slabs, parts, chips - 1)), dma((slabs, parts, chips - 1)),
            dma((slabs, parts, chips)), dma((slabs, parts, chips)),
        ],
        compiler_params=pltpu.CompilerParams(collective_id=0, has_side_effects=True, vmem_limit_bytes=36 * 1024 * 1024),
        name="fused",
    )(offset, *[pltpu.with_memory_space_constraint(x, pltpu.HBM) for x in (subs, slab, cells, values, weights)])
    tiles = local // min(local, 256)
    return pl.pallas_call(
        functools.partial(finish_kernel, 1.0 / math.sqrt(subs.shape[0] * SG)),
        in_specs=[vmem] * 4,
        out_specs=[pl.BlockSpec(memory_space=pltpu.HBM)] * 2,
        out_shape=[
            jax.ShapeDtypeStruct((2, band, width), F32),
            jax.ShapeDtypeStruct((2, local, width), F32),
        ],
        scratch_shapes=[pltpu.VMEM((tiles, 2, local // tiles, width), F32), dma((tiles + 1,))],
        compiler_params=pltpu.CompilerParams(vmem_limit_bytes=8 * 1024 * 1024),
        name="finish",
    )(piece, part, last, last_table)


def body(slab, facet_offset, subgrid_offset, vis_cell, vis_value, vis_weight):
    slabs = lax.axis_size("slab")
    facets = lax.axis_size("facet")
    local_rows = slab.shape[2]
    width = slab.shape[3]
    count_sub = subgrid_offset.shape[0]
    band = SG // slabs
    owned = count_sub * band // facets
    first = (facet_offset + lax.axis_index("slab") * local_rows).astype(jnp.int32)
    chips = facets // 2
    paired = facets == 2 * chips and chips == 4 and slabs > 2 and slabs & (slabs - 1) == 0
    if owned == band and count_sub == facets and paired and band % 32 == 0 and local_rows % 256 == 0:
        residual, update = fused(
            facet_offset, subgrid_offset, slab[:, 0], vis_cell[0], vis_value[:, 0], vis_weight[0], slabs, facets
        )
        return (residual.reshape(2, 1, owned, width), update.reshape(2, 1, local_rows, width))
    sums = grid_visibilities(vis_cell[0], vis_value[:, 0, 0], vis_weight[0], owned, width)
    contrib = forward(first, subgrid_offset, slab[:, 0], slabs)
    contrib = contrib.reshape(2, slabs, facets, owned, width)
    parts = lax.all_to_all(contrib, "facet", 2, 2, tiled=True)
    parts = jnp.sum(parts, axis=2, dtype=F32).astype(BF16)
    parts = lax.all_to_all(parts, "slab", 1, 1, tiled=True)
    scale = 1.0 / math.sqrt(local_rows * slabs * facets)
    model = jnp.sum(parts, axis=1, dtype=F32) * scale
    residual = sums[:2] - sums[2:] * model
    sent = residual.astype(BF16).reshape(2, 1, 1, owned, width)
    piece = lax.all_gather(sent, "slab", axis=1, tiled=True)
    piece = lax.all_gather(piece, "facet", axis=2, tiled=True)
    piece = piece.reshape(2, slabs, count_sub, band, width)
    update = adjoint(first, subgrid_offset, piece, local_rows)
    return (residual.reshape(2, 1, owned, width), update.reshape(2, 1, local_rows, width))


def solution(mesh):
    placed = (
        P(None, "facet", "slab", None),
        P("facet"),
        P(),
        P("slab", "facet", None),
        P(None, "slab", "facet", None),
        P("slab", "facet", None),
    )
    return jax.shard_map(
        body,
        mesh=mesh,
        in_specs=placed,
        out_specs=(P(None, "slab", "facet", None), P(None, "facet", "slab", None)),
        check_vma=False,
    )
```

```python
import functools
import math

import jax
import jax.numpy as jnp
from jax import lax
from jax.experimental import pallas as pl
from jax.experimental.pallas import tpu as pltpu
from jax.sharding import PartitionSpec as P

IMAGE = 32768
SG = 256
UVSTEP = 16
F32 = jnp.float32
BF16 = jnp.bfloat16
GRID = 8192
GRID_LATE = 0
TILE = 1024


def cis(turns):
    turns = turns & (IMAGE - 1)
    quarter = IMAGE // 4
    quad = (turns + quarter // 2) // quarter if quarter & (quarter - 1) else lax.shift_right_logical(
        turns + quarter // 2, quarter.bit_length() - 1
    )
    t = (turns - quad * quarter).astype(F32) * (2.0 * math.pi / IMAGE)
    z = t * t
    s = ((-1.9515295891e-4 * z + 8.3321608736e-3) * z - 1.6666654611e-1) * z * t + t
    c = ((2.443315711809948e-5 * z - 1.388731625493765e-3) * z + 4.166664568298827e-2) * z * z - 0.5 * z + 1.0
    odd = (quad & 1) == 1
    cos = jnp.where(odd, s, c)
    sin = jnp.where(odd, c, s)
    cos = jnp.where(((quad + 1) & 2) == 2, -cos, cos)
    sin = jnp.where((quad & 2) == 2, -sin, sin)
    return cos, sin


def grid_kernel(width, rows, cell_ref, value_ref, weight_ref, out_ref):
    @pl.when(pl.program_id(0) == 0)
    def _():
        out_ref[...] = jnp.zeros_like(out_ref)

    cell = cell_ref[...]
    weight = weight_ref[...]
    chunk = cell.shape[1]
    row = lax.shift_right_logical(cell, width.bit_length() - 1)
    col = cell & (width - 1)
    hot = jnp.where(lax.broadcasted_iota(jnp.int32, (width, chunk), 0) == col, 1.0, 0.0).astype(BF16)
    mine = lax.broadcasted_iota(jnp.int32, (rows, chunk), 0) == row
    terms = [weight * value_ref[0:1, :], weight * value_ref[1:2, :], weight]
    left = jnp.concatenate([jnp.where(mine, t, 0.0).astype(BF16) for t in terms], axis=0)
    out_ref[...] += lax.dot_general(left, hot, (((1,), (1,)), ((), ())), preferred_element_type=F32)


def grid_visibilities(cells, values, weights, owned, width):
    count = cells.shape[1]
    rows = -(-owned // 16) * 16
    chunk = min(count, 2048)
    out = pl.pallas_call(
        functools.partial(grid_kernel, width, rows),
        grid=(count // chunk,),
        in_specs=[
            pl.BlockSpec((1, chunk), lambda i: (0, i)),
            pl.BlockSpec((2, chunk), lambda i: (0, i)),
            pl.BlockSpec((1, chunk), lambda i: (0, i)),
        ],
        out_specs=pl.BlockSpec((3 * rows, width), lambda i: (0, 0)),
        out_shape=jax.ShapeDtypeStruct((3 * rows, width), F32),
        cost_estimate=pl.CostEstimate(flops=6 * rows * width * count, bytes_accessed=16 * count, transcendentals=0),
        name="gridding",
    )(cells, values, weights)
    return out.reshape(3, rows, width)[:, :owned]


def forward_kernel(first_ref, subs_ref, slab_ref, out_ref, cos_ref, sin_ref):
    s = pl.program_id(0)
    rows, local = cos_ref.shape
    first = first_ref[0]

    @pl.when(s == 0)
    def _():
        k = lax.broadcasted_iota(jnp.int32, (rows, local), 0)
        y = lax.broadcasted_iota(jnp.int32, (rows, local), 1) + first
        c, n = cis((UVSTEP * k) * y)
        cos_ref[...] = c
        sin_ref[...] = n

    y = lax.broadcasted_iota(jnp.int32, (8, local), 1) + first
    c1, s1 = cis(subs_ref[s] * y)
    c1, s1 = c1[0:1], s1[0:1]
    c2, s2 = cos_ref[...], sin_ref[...]
    tab_real = (c1 * c2 - s1 * s2).astype(BF16)
    tab_imag = (-(s1 * c2 + c1 * s2)).astype(BF16)
    re, im = slab_ref[0], slab_ref[1]
    dot = functools.partial(jnp.dot, preferred_element_type=F32)
    real = dot(tab_real, re) - dot(tab_imag, im)
    imag = dot(tab_real, im) + dot(tab_imag, re)
    slabs, band = out_ref.shape[1], out_ref.shape[3]
    for p in range(slabs):
        out_ref[0, p, 0] = real[p * band:(p + 1) * band].astype(out_ref.dtype)
        out_ref[1, p, 0] = imag[p * band:(p + 1) * band].astype(out_ref.dtype)


def forward(first, subs, slab, slabs):
    _, local, width = slab.shape
    count = subs.shape[0]
    band = SG // slabs
    return pl.pallas_call(
        forward_kernel,
        grid=(count,),
        in_specs=[
            pl.BlockSpec(memory_space=pltpu.SMEM),
            pl.BlockSpec(memory_space=pltpu.SMEM),
            pl.BlockSpec((2, local, width), lambda s: (0, 0, 0)),
        ],
        out_specs=pl.BlockSpec((2, slabs, 1, band, width), lambda s: (0, 0, s, 0, 0)),
        out_shape=jax.ShapeDtypeStruct((2, slabs, count, band, width), BF16),
        scratch_shapes=[pltpu.VMEM((SG, local), F32), pltpu.VMEM((SG, local), F32)],
        name="forward",
    )(first, subs, slab)


def adjoint_kernel(scale, slabs, first_ref, subs_ref, sent_ref, out_ref):
    tile = out_ref.shape[1]
    count = subs_ref.shape[1]
    band = SG // slabs
    start = first_ref[0] + pl.program_id(0) * tile
    yk = lax.broadcasted_iota(jnp.int32, (tile, SG), 0) + start
    c2, s2 = cis((UVSTEP * lax.broadcasted_iota(jnp.int32, (tile, SG), 1)) * yk)
    ys = lax.broadcasted_iota(jnp.int32, (tile, count), 0) + start
    c1, s1 = cis(ys * subs_ref[...])
    real = jnp.zeros(out_ref.shape[1:], F32)
    imag = jnp.zeros(out_ref.shape[1:], F32)
    dot = functools.partial(jnp.dot, preferred_element_type=F32)
    for s in range(count):
        a, b = c1[:, s:s + 1], s1[:, s:s + 1]
        tab_real = (a * c2 - b * s2).astype(BF16)
        tab_imag = (-(b * c2 + a * s2)).astype(BF16)
        re = jnp.concatenate([sent_ref[0, p, s] for p in range(slabs)], axis=0)
        im = jnp.concatenate([sent_ref[1, p, s] for p in range(slabs)], axis=0)
        real += dot(tab_real, re) + dot(tab_imag, im)
        imag += dot(tab_real, im) - dot(tab_imag, re)
    out_ref[0] = real * scale
    out_ref[1] = imag * scale


def adjoint(first, subs, sent, local):
    _, slabs, count, band, width = sent.shape
    tile = min(local, 256)
    return pl.pallas_call(
        functools.partial(adjoint_kernel, 1.0 / math.sqrt(count * SG), slabs),
        grid=(local // tile,),
        in_specs=[
            pl.BlockSpec(memory_space=pltpu.SMEM),
            pl.BlockSpec((1, count), lambda i: (0, 0)),
            pl.BlockSpec((2, slabs, count, band, width), lambda i: (0, 0, 0, 0, 0)),
        ],
        out_specs=pl.BlockSpec((2, tile, width), lambda i: (0, i, 0)),
        out_shape=jax.ShapeDtypeStruct((2, local, width), F32),
        name="adjoint",
    )(first, subs[None, :], sent)


def fused_kernel(
    scale, offset_ref, subs_hbm, slab_hbm, cell_hbm, value_hbm, weight_hbm,
    residual_ref, update_ref, last_ref, table,
    subs_ref, slab_ref, cell_ref, value_ref, weight_ref, low, high, acc, pb, rp, cb, rx, dg, zd, zf, zb, rz, sums, flat, full,
    turn, load,
    p_send, p_recv, x_send, x_recv, d_send, d_recv, z_send, z_recv, gz_send, gz_recv, gx_send, gx_recv, gc_send, gc_recv,
):
    facets, slabs = lax.axis_size("facet"), lax.axis_size("slab")
    q, z = lax.axis_index("facet"), lax.axis_index("slab")
    core, chip = q % 2, q // 2
    chips = facets // 2
    partner = q + 1 - 2 * core
    _, local, width = slab_ref.shape
    band = SG // slabs
    groups = band // 16
    parts = x_send.shape[1]
    share = band // parts
    dot = functools.partial(jnp.dot, preferred_element_type=F32)

    def at_chip(d):
        return 2 * (chip ^ d) + core

    def remote(src, dst, send, recv, **where):
        return pltpu.make_async_remote_copy(
            src_ref=src, dst_ref=dst, send_sem=send, recv_sem=recv,
            device_id=where, device_id_type=pl.DeviceIdType.MESH,
        )

    barrier = pltpu.get_barrier_semaphore()
    for e in range(1, slabs):
        pl.semaphore_signal(barrier, inc=1, device_id={"slab": z ^ e}, device_id_type=pl.DeviceIdType.MESH)
    for d in range(1, chips):
        pl.semaphore_signal(barrier, inc=1, device_id={"facet": at_chip(d)}, device_id_type=pl.DeviceIdType.MESH)
    pl.semaphore_signal(barrier, inc=1, device_id={"facet": partner}, device_id_type=pl.DeviceIdType.MESH)
    loads = [
        pltpu.make_async_copy(src, dst, load.at[i])
        for i, (src, dst) in enumerate(
            [
                (subs_hbm, subs_ref), (slab_hbm, slab_ref),
                (cell_hbm, cell_ref), (value_hbm, value_ref), (weight_hbm, weight_ref),
            ]
        )
    ]
    for copy in loads:
        copy.start()

    loads[0].wait()
    first = offset_ref[0] + z * local
    line = lax.broadcasted_iota(jnp.int32, (16, local), 1)

    places = line + first
    c, n = cis(UVSTEP * lax.broadcasted_iota(jnp.int32, (16, local), 0) * places)
    low[0] = c
    low[1] = n

    def partial_sum(i, other):
        row = lax.broadcasted_iota(jnp.int32, (chips * groups, local), 0)
        freq = UVSTEP * (band * (z ^ (slabs - 1 - i)) + 16 * (row % groups))
        for d in range(chips):
            freq += jnp.where(row // groups == d, subs_ref[at_chip(d) ^ other], 0)
        c, n = cis(freq * places[0:1])
        high[0] = c
        high[1] = n
        c2, s2 = low[0], low[1]
        cos, sin = [], []
        for g in range(chips * groups):
            c1, s1 = high[0, g:g + 1], high[1, g:g + 1]
            cos.append((c1 * c2 - s1 * s2).astype(BF16))
            sin.append((s1 * c2 + c1 * s2).astype(BF16))
        cos = jnp.concatenate(cos, axis=0)
        sin = jnp.concatenate(sin, axis=0)
        data = slab_ref[...].reshape(2 * local, width)
        real = dot(jnp.concatenate([cos, sin], axis=1), data)
        imag = dot(jnp.concatenate([-sin, cos], axis=1), data)
        return real, imag

    def pair_copy(i):
        return remote(pb.at[i], rp.at[i], p_send.at[i], p_recv.at[i], facet=partner)

    def part(h):
        return slice(h * share, (h + 1) * share)

    def x_copy(i, h, d):
        return remote(
            cb.at[i, d - 1, :, part(h)], rx.at[i, d - 1, :, part(h)],
            x_send.at[i, h, d - 1], x_recv.at[i, h, d - 1], facet=at_chip(d),
        )

    own, far = slabs - 1, chips - 1

    def routed(i):
        return i % 2 == 0

    def d_copy(i, h):
        return remote(
            cb.at[i, far - 1, :, part(h)], zd.at[i // 2, :, part(h)], d_send.at[i // 2, h], d_recv.at[i // 2, h],
            slab=z ^ (own - i),
        )

    def ways(i):
        return [d for d in range(far, 0, -1) if d != far or not routed(i)]

    def x_send_part(i, h):
        for d in ways(i):
            if i != own or d != far:
                x_copy(i, h, d).start()

    def pair_band(i, mine):
        pair_copy(i).wait_recv()
        for d in range(far, 0, -1):
            at = slice(d * band, (d + 1) * band)
            for c in range(2):
                total = acc[i, c, at] + rp[i, c, at].astype(F32)
                if mine and d == far:
                    dg[c] = total
                else:
                    cb[i, d - 1, c] = total.astype(BF16)
        if not mine and routed(i):
            for h in range(parts):
                d_copy(i, h).start()
        elif not mine:
            x_copy(i, 0, far).start()
        for d in range(far - 1, 0, -1):
            x_copy(i, 0, d).start()
        for c in range(2):
            zf[i, c] = acc[i, c, 0:band] + rp[i, c, 0:band].astype(F32)

    def send_far(h):
        for i in range(0, own, 2):
            d_copy(i, h).wait()
        for c in range(2):
            total = dg[c, part(h)]
            for k in range(slabs // 2):
                total += zd[k, c, part(h)].astype(F32)
            cb[own, far - 1, c, part(h)] = total.astype(BF16)
        x_copy(own, h, far).start()

    loads[1].wait()
    for i in range(slabs):
        for c, half in enumerate(partial_sum(i, 1)):
            pb[i, c] = half.astype(BF16)
        if i == 0:
            pl.semaphore_wait(barrier, chips + slabs - 1)
        pair_copy(i).start()
        if i > 0:
            pair_band(i - 1, False)
        for c, half in enumerate(partial_sum(i, 0)):
            acc[i, c] = half
    pair_band(own, True)
    for i in range(own - 1):
        x_send_part(i, 1)

    rows = sums.shape[1] // 3
    count = cell_ref.shape[1]
    chunk = min(count, GRID)
    for copy in loads[2:]:
        copy.wait()
    sums[...] = jnp.zeros_like(sums)

    def grid_step(i, carry):
        at = pl.ds(pl.multiple_of(i * chunk, chunk), chunk)
        cell = cell_ref[:, at]
        weight = weight_ref[:, at]
        row = lax.shift_right_logical(cell, width.bit_length() - 1).astype(F32)
        col = (cell & (width - 1)).astype(F32)
        lines = lax.broadcasted_iota(jnp.int32, (16, chunk), 0).astype(F32).astype(BF16)
        row = jnp.broadcast_to(row, (16, chunk)).astype(BF16)
        col = jnp.broadcast_to(col, (16, chunk)).astype(BF16)
        one, zero = jnp.ones((16, chunk), BF16), jnp.zeros((16, chunk), BF16)
        hot = jnp.concatenate(
            [jnp.where(col == lines + jnp.asarray(g, BF16), one, zero) for g in range(0, width, 16)], axis=0
        )
        terms = [weight * value_ref[0, :, at], weight * value_ref[1, :, at], weight]
        terms = [jnp.broadcast_to(t, (16, chunk)).astype(BF16) for t in terms]
        left = jnp.concatenate(
            [jnp.where(row == lines + jnp.asarray(g, BF16), t, zero) for t in terms for g in range(0, rows, 16)],
            axis=0,
        )
        sums[...] += lax.dot_general(hot, left, (((1,), (1,)), ((), ())), preferred_element_type=F32)
        return carry

    span = facets * share

    def table_band(t, carry):
        e, h = t // parts, t % parts
        lane = lax.broadcasted_iota(jnp.int32, (16, span), 1)
        freq = UVSTEP * (band * (z ^ e) + share * h + lane % share)
        for s in range(facets):
            freq += jnp.where(lane // share == s, subs_ref[s], 0)
        c2, s2 = cis(freq * lax.broadcasted_iota(jnp.int32, (16, span), 0))
        far = first + 16 * lax.broadcasted_iota(jnp.int32, (local // 16, span), 0)
        c, n = cis(freq[0:1] * far)
        turn[0] = c
        turn[1] = n

        def step(g, inner):
            c1, s1 = turn[0, pl.ds(g, 1)], turn[1, pl.ds(g, 1)]
            sin = (s1 * c2 + c1 * s2).astype(BF16)
            at = pl.ds(pl.multiple_of(g * 16, 16), 16)
            into = table.at[e, h]
            into[at, 0:span] = sin
            into[at, span:2 * span] = (c1 * c2 - s1 * s2).astype(BF16)
            into[at, 2 * span:3 * span] = -sin
            return inner

        lax.fori_loop(0, local // 16, step, 0)
        return carry

    chunks = count // chunk

    def z_copy(i, h):
        return remote(
            zb.at[i, :, part(h)], rz.at[i, :, part(h)], z_send.at[i, h], z_recv.at[i, h], slab=z ^ (slabs - 1 - i)
        )

    def reduce_part(i, h):
        for d in ways(i):
            x_copy(i, h, d).wait()
        for c in range(2):
            total = zf[i, c, part(h)]
            for d in ways(i):
                total += rx[i, d - 1, c, part(h)].astype(F32)
            if i < slabs - 1:
                zb[i, c, part(h)] = total.astype(BF16)
            else:
                zf[i, c, part(h)] = total
        if i < slabs - 1:
            z_copy(i, h).start()

    def residual_part(h):
        for i in range(slabs - 1):
            z_copy(i, h).wait()
        for c in range(2):
            model = zf[slabs - 1, c, part(h)]
            for i in range(slabs - 1):
                model += rz[i, c, part(h)].astype(F32)
            at = h * share
            piece = flat[c * rows + at:c * rows + at + share]
            piece -= flat[2 * rows + at:2 * rows + at + share] * (model * scale)
            residual_ref[c, part(h)] = piece
            full[0, h, c, q] = piece.astype(BF16)

    def up_copy(e, h):
        return remote(
            full.at[0, h, :, q], full.at[e, h, :, q], gz_send.at[e - 1, h], gz_recv.at[e - 1, h],
            slab=z ^ e,
        )

    def across_copy(e, h, d):
        ref = full.at[e, h, :, q]
        return remote(ref, ref, gx_send.at[e, h, d - 1], gx_recv.at[e, h, d - 1], facet=at_chip(d))

    def spread_copy(e, h, d):
        ref = full.at[e, h, :, at_chip(d)]
        return remote(ref, ref, gc_send.at[e, h, d], gc_recv.at[e, h, d], facet=partner)

    def hand_on(e, h):
        if e:
            up_copy(e, h).wait_recv()
        else:
            for away in order[1:]:
                up_copy(away, h).start()
        for d in range(chips - 1, 0, -1):
            across_copy(e, h, d).start()
        spread_copy(e, h, 0).start()

    def relay(e, h):
        for d in range(1, chips):
            across_copy(e, h, d).wait_recv()
            spread_copy(e, h, d).start()

    tile = min(local, TILE)

    def gathered(e, h):
        for d in range(chips):
            spread_copy(e, h, d).wait_recv()

    order = [k ^ (k >> 1) for k in range(slabs)]
    last = order[-1]
    units = slabs * parts

    def looped(count, work, before, after):
        def step(k, carry):
            for at, events in before.items():
                @pl.when(k == at)
                def _():
                    for event in events:
                        event()
            work(k)
            for at, events in after.items():
                @pl.when(k == at)
                def _():
                    for event in events:
                        event()
            return carry

        lax.fori_loop(0, count, step, 0)

    def update_pass(k):
        j, h = k % slabs, k // slabs
        e = j ^ lax.shift_right_logical(j, 1)
        gathered(e, h)

        def step(i, carry):
            at = pl.ds(pl.multiple_of(i * tile, tile), tile)
            data = full[e, h].reshape(2 * span, width)
            update_ref[1, at] += dot(table[e, h, at, 0:2 * span], data)
            update_ref[0, at] += dot(table[e, h, at, span:3 * span], data)
            return carry

        lax.fori_loop(0, local // tile, step, 0)

    def call(f, *args):
        return functools.partial(f, *args)

    reduce_part(0, 0)
    after = {}
    for i in range(1, own):
        after.setdefault(min(chunks - 1, i + GRID_LATE), []).append(call(reduce_part, i, 0))
        if i == 1:
            after[min(chunks - 1, i + GRID_LATE)] += [
                call(send_far, 0), call(x_send_part, own - 1, 1), call(x_send_part, own, 1)
            ]
    after.setdefault(max(chunks - 2, 0), []).extend([call(send_far, 1), call(reduce_part, 0, 1)])
    looped(chunks, lambda k: grid_step(k, 0), {}, after)
    flat[...] = sums[...].T
    update_ref[...] = jnp.zeros_like(update_ref)
    for i in range(1, own - 1):
        reduce_part(i, 1)
    reduce_part(own, 0)
    residual_part(0)
    hand_on(0, 0)
    reduce_part(own - 1, 1)
    middle = [call(hand_on, 1, 0), call(residual_part, 1), call(hand_on, 0, 1)]
    middle += [call(hand_on, e, 0) for e in order[2:-1]] + [call(relay, 0, 0)]
    looped(
        units, lambda t: table_band(t, 0), {},
        {1: [call(reduce_part, own, 1)], 2: middle, 4: [call(hand_on, last, 0)]},
    )
    hand_on(1, 1)
    relay(1, 0)
    before = {}
    for k, e in enumerate(order[2:]):
        before[k + 1] = [call(hand_on, e, 1), call(relay, e, 0)]
    before[slabs - 2] += [call(relay, 0, 1)]
    for k, e in enumerate(order[1:]):
        before[slabs + k] = [call(relay, e, 1)]
    looped(units - 1, update_pass, before, {})
    gathered(last, parts - 1)
    last_ref[...] = full[last, parts - 1]
    for i in range(slabs):
        pair_copy(i).wait_send()
    for e in range(slabs):
        for h in range(parts):
            if e:
                up_copy(e, h).wait_send()
            for d in range(chips):
                if d:
                    across_copy(e, h, d).wait_send()
                spread_copy(e, h, d).wait_send()


def finish_kernel(back, piece_ref, part_ref, last_ref, table_ref, residual_ref, update_ref, buffer, sent):
    dot = functools.partial(jnp.dot, preferred_element_type=F32)
    _, local, width = part_ref.shape
    slabs, parts, _, span = table_ref.shape
    span //= 3
    last = (slabs - 1) ^ ((slabs - 1) >> 1)
    tiles, _, tile, _ = buffer.shape
    out = pltpu.make_async_copy(piece_ref, residual_ref, sent.at[tiles])
    out.start()

    def put(i):
        at = pl.ds(i * tile, tile)
        return pltpu.make_async_copy(buffer.at[i], update_ref.at[:, at], sent.at[i])

    def step(i, carry):
        at = pl.ds(i * tile, tile)
        data = last_ref[...].reshape(2 * span, width)
        imag = dot(table_ref[last, parts - 1, at, 0:2 * span], data)
        real = dot(table_ref[last, parts - 1, at, span:3 * span], data)
        buffer[i, 0] = (real + part_ref[0, at]) * back
        buffer[i, 1] = (imag + part_ref[1, at]) * back
        put(i).start()
        return carry

    for i in range(tiles):
        step(i, 0)
    for i in range(tiles):
        put(i).wait()
    out.wait()


def fused(offset, subs, slab, cells, values, weights, slabs, facets):
    _, local, width = slab.shape
    band = SG // slabs
    chips = facets // 2
    rows = -(-band // 16) * 16
    vmem = pl.BlockSpec(memory_space=pltpu.VMEM)
    dma = pltpu.SemaphoreType.DMA
    parts = 2
    share = band // parts
    span = facets * share
    piece, part, last, last_table = pl.pallas_call(
        functools.partial(fused_kernel, 1.0 / math.sqrt(local * slabs * facets)),
        in_specs=[pl.BlockSpec(memory_space=pltpu.SMEM)] + [pl.BlockSpec(memory_space=pltpu.HBM)] * 5,
        out_specs=[vmem] * 4,
        out_shape=[
            jax.ShapeDtypeStruct((2, band, width), F32),
            jax.ShapeDtypeStruct((2, local, width), F32),
            jax.ShapeDtypeStruct((2, facets, share, width), BF16),
            jax.ShapeDtypeStruct((slabs, parts, local, 3 * span), BF16),
        ],
        scratch_shapes=[
            pltpu.SMEM(subs.shape, jnp.int32),
            pltpu.VMEM((2, local, width), BF16),
            pltpu.VMEM(cells.shape, jnp.int32),
            pltpu.VMEM(values.shape, F32),
            pltpu.VMEM(weights.shape, F32),
            pltpu.VMEM((2, 16, local), F32),
            pltpu.VMEM((2, chips * (band // 16), local), F32),
            pltpu.VMEM((slabs, 2, chips * band, width), F32),
            pltpu.VMEM((slabs, 2, chips * band, width), BF16),
            pltpu.VMEM((slabs, 2, chips * band, width), BF16),
            pltpu.VMEM((slabs, chips - 1, 2, band, width), BF16),
            pltpu.VMEM((slabs, chips - 1, 2, band, width), BF16),
            pltpu.VMEM((2, band, width), F32),
            pltpu.VMEM((slabs // 2, 2, band, width), BF16),
            pltpu.VMEM((slabs, 2, band, width), F32),
            pltpu.VMEM((slabs - 1, 2, band, width), BF16),
            pltpu.VMEM((slabs - 1, 2, band, width), BF16),
            pltpu.VMEM((width, 3 * rows), F32),
            pltpu.VMEM((3 * rows, width), F32),
            pltpu.VMEM((slabs, parts, 2, facets, share, width), BF16),
            pltpu.VMEM((2, local // 16, span), F32),
            dma((5,)),
            dma((slabs,)), dma((slabs,)),
            dma((slabs, parts, chips - 1)), dma((slabs, parts, chips - 1)),
            dma((slabs // 2, parts)), dma((slabs // 2, parts)),
            dma((slabs - 1, parts)), dma((slabs - 1, parts)),
            dma((slabs - 1, parts)), dma((slabs - 1, parts)),
            dma((slabs, parts, chips - 1)), dma((slabs, parts, chips - 1)),
            dma((slabs, parts, chips)), dma((slabs, parts, chips)),
        ],
        compiler_params=pltpu.CompilerParams(collective_id=0, has_side_effects=True, vmem_limit_bytes=36 * 1024 * 1024),
        name="fused",
    )(offset, *[pltpu.with_memory_space_constraint(x, pltpu.HBM) for x in (subs, slab, cells, values, weights)])
    tiles = local // min(local, 256)
    return pl.pallas_call(
        functools.partial(finish_kernel, 1.0 / math.sqrt(subs.shape[0] * SG)),
        in_specs=[vmem] * 4,
        out_specs=[pl.BlockSpec(memory_space=pltpu.HBM)] * 2,
        out_shape=[
            jax.ShapeDtypeStruct((2, band, width), F32),
            jax.ShapeDtypeStruct((2, local, width), F32),
        ],
        scratch_shapes=[pltpu.VMEM((tiles, 2, local // tiles, width), F32), dma((tiles + 1,))],
        compiler_params=pltpu.CompilerParams(vmem_limit_bytes=8 * 1024 * 1024),
        name="finish",
    )(piece, part, last, last_table)


def body(slab, facet_offset, subgrid_offset, vis_cell, vis_value, vis_weight):
    slabs = lax.axis_size("slab")
    facets = lax.axis_size("facet")
    local_rows = slab.shape[2]
    width = slab.shape[3]
    count_sub = subgrid_offset.shape[0]
    band = SG // slabs
    owned = count_sub * band // facets
    first = (facet_offset + lax.axis_index("slab") * local_rows).astype(jnp.int32)
    chips = facets // 2
    paired = facets == 2 * chips and chips == 4 and slabs > 2 and slabs & (slabs - 1) == 0
    if owned == band and count_sub == facets and paired and band % 32 == 0 and local_rows % 256 == 0:
        residual, update = fused(
            facet_offset, subgrid_offset, slab[:, 0], vis_cell[0], vis_value[:, 0], vis_weight[0], slabs, facets
        )
        return (residual.reshape(2, 1, owned, width), update.reshape(2, 1, local_rows, width))
    sums = grid_visibilities(vis_cell[0], vis_value[:, 0, 0], vis_weight[0], owned, width)
    contrib = forward(first, subgrid_offset, slab[:, 0], slabs)
    contrib = contrib.reshape(2, slabs, facets, owned, width)
    parts = lax.all_to_all(contrib, "facet", 2, 2, tiled=True)
    parts = jnp.sum(parts, axis=2, dtype=F32).astype(BF16)
    parts = lax.all_to_all(parts, "slab", 1, 1, tiled=True)
    scale = 1.0 / math.sqrt(local_rows * slabs * facets)
    model = jnp.sum(parts, axis=1, dtype=F32) * scale
    residual = sums[:2] - sums[2:] * model
    sent = residual.astype(BF16).reshape(2, 1, 1, owned, width)
    piece = lax.all_gather(sent, "slab", axis=1, tiled=True)
    piece = lax.all_gather(piece, "facet", axis=2, tiled=True)
    piece = piece.reshape(2, slabs, count_sub, band, width)
    update = adjoint(first, subgrid_offset, piece, local_rows)
    return (residual.reshape(2, 1, owned, width), update.reshape(2, 1, local_rows, width))


def solution(mesh):
    placed = (
        P(None, "facet", "slab", None),
        P("facet"),
        P(),
        P("slab", "facet", None),
        P(None, "slab", "facet", None),
        P("slab", "facet", None),
    )
    return jax.shard_map(
        body,
        mesh=mesh,
        in_specs=placed,
        out_specs=(P(None, "slab", "facet", None), P(None, "facet", "slab", None)),
        check_vma=False,
    )
```

```python
import functools
import math

import jax
import jax.numpy as jnp
from jax import lax
from jax.experimental import pallas as pl
from jax.experimental.pallas import tpu as pltpu
from jax.sharding import PartitionSpec as P

IMAGE = 32768
SG = 256
UVSTEP = 16
F32 = jnp.float32
BF16 = jnp.bfloat16
GRID = 8192
GRID_LATE = 0
TILE = 1024


def cis(turns):
    turns = turns & (IMAGE - 1)
    quarter = IMAGE // 4
    quad = (turns + quarter // 2) // quarter if quarter & (quarter - 1) else lax.shift_right_logical(
        turns + quarter // 2, quarter.bit_length() - 1
    )
    t = (turns - quad * quarter).astype(F32) * (2.0 * math.pi / IMAGE)
    z = t * t
    s = ((-1.9515295891e-4 * z + 8.3321608736e-3) * z - 1.6666654611e-1) * z * t + t
    c = ((2.443315711809948e-5 * z - 1.388731625493765e-3) * z + 4.166664568298827e-2) * z * z - 0.5 * z + 1.0
    odd = (quad & 1) == 1
    cos = jnp.where(odd, s, c)
    sin = jnp.where(odd, c, s)
    cos = jnp.where(((quad + 1) & 2) == 2, -cos, cos)
    sin = jnp.where((quad & 2) == 2, -sin, sin)
    return cos, sin


def grid_kernel(width, rows, cell_ref, value_ref, weight_ref, out_ref):
    @pl.when(pl.program_id(0) == 0)
    def _():
        out_ref[...] = jnp.zeros_like(out_ref)

    cell = cell_ref[...]
    weight = weight_ref[...]
    chunk = cell.shape[1]
    row = lax.shift_right_logical(cell, width.bit_length() - 1)
    col = cell & (width - 1)
    hot = jnp.where(lax.broadcasted_iota(jnp.int32, (width, chunk), 0) == col, 1.0, 0.0).astype(BF16)
    mine = lax.broadcasted_iota(jnp.int32, (rows, chunk), 0) == row
    terms = [weight * value_ref[0:1, :], weight * value_ref[1:2, :], weight]
    left = jnp.concatenate([jnp.where(mine, t, 0.0).astype(BF16) for t in terms], axis=0)
    out_ref[...] += lax.dot_general(left, hot, (((1,), (1,)), ((), ())), preferred_element_type=F32)


def grid_visibilities(cells, values, weights, owned, width):
    count = cells.shape[1]
    rows = -(-owned // 16) * 16
    chunk = min(count, 2048)
    out = pl.pallas_call(
        functools.partial(grid_kernel, width, rows),
        grid=(count // chunk,),
        in_specs=[
            pl.BlockSpec((1, chunk), lambda i: (0, i)),
            pl.BlockSpec((2, chunk), lambda i: (0, i)),
            pl.BlockSpec((1, chunk), lambda i: (0, i)),
        ],
        out_specs=pl.BlockSpec((3 * rows, width), lambda i: (0, 0)),
        out_shape=jax.ShapeDtypeStruct((3 * rows, width), F32),
        cost_estimate=pl.CostEstimate(flops=6 * rows * width * count, bytes_accessed=16 * count, transcendentals=0),
        name="gridding",
    )(cells, values, weights)
    return out.reshape(3, rows, width)[:, :owned]


def forward_kernel(first_ref, subs_ref, slab_ref, out_ref, cos_ref, sin_ref):
    s = pl.program_id(0)
    rows, local = cos_ref.shape
    first = first_ref[0]

    @pl.when(s == 0)
    def _():
        k = lax.broadcasted_iota(jnp.int32, (rows, local), 0)
        y = lax.broadcasted_iota(jnp.int32, (rows, local), 1) + first
        c, n = cis((UVSTEP * k) * y)
        cos_ref[...] = c
        sin_ref[...] = n

    y = lax.broadcasted_iota(jnp.int32, (8, local), 1) + first
    c1, s1 = cis(subs_ref[s] * y)
    c1, s1 = c1[0:1], s1[0:1]
    c2, s2 = cos_ref[...], sin_ref[...]
    tab_real = (c1 * c2 - s1 * s2).astype(BF16)
    tab_imag = (-(s1 * c2 + c1 * s2)).astype(BF16)
    re, im = slab_ref[0], slab_ref[1]
    dot = functools.partial(jnp.dot, preferred_element_type=F32)
    real = dot(tab_real, re) - dot(tab_imag, im)
    imag = dot(tab_real, im) + dot(tab_imag, re)
    slabs, band = out_ref.shape[1], out_ref.shape[3]
    for p in range(slabs):
        out_ref[0, p, 0] = real[p * band:(p + 1) * band].astype(out_ref.dtype)
        out_ref[1, p, 0] = imag[p * band:(p + 1) * band].astype(out_ref.dtype)


def forward(first, subs, slab, slabs):
    _, local, width = slab.shape
    count = subs.shape[0]
    band = SG // slabs
    return pl.pallas_call(
        forward_kernel,
        grid=(count,),
        in_specs=[
            pl.BlockSpec(memory_space=pltpu.SMEM),
            pl.BlockSpec(memory_space=pltpu.SMEM),
            pl.BlockSpec((2, local, width), lambda s: (0, 0, 0)),
        ],
        out_specs=pl.BlockSpec((2, slabs, 1, band, width), lambda s: (0, 0, s, 0, 0)),
        out_shape=jax.ShapeDtypeStruct((2, slabs, count, band, width), BF16),
        scratch_shapes=[pltpu.VMEM((SG, local), F32), pltpu.VMEM((SG, local), F32)],
        name="forward",
    )(first, subs, slab)


def adjoint_kernel(scale, slabs, first_ref, subs_ref, sent_ref, out_ref):
    tile = out_ref.shape[1]
    count = subs_ref.shape[1]
    band = SG // slabs
    start = first_ref[0] + pl.program_id(0) * tile
    yk = lax.broadcasted_iota(jnp.int32, (tile, SG), 0) + start
    c2, s2 = cis((UVSTEP * lax.broadcasted_iota(jnp.int32, (tile, SG), 1)) * yk)
    ys = lax.broadcasted_iota(jnp.int32, (tile, count), 0) + start
    c1, s1 = cis(ys * subs_ref[...])
    real = jnp.zeros(out_ref.shape[1:], F32)
    imag = jnp.zeros(out_ref.shape[1:], F32)
    dot = functools.partial(jnp.dot, preferred_element_type=F32)
    for s in range(count):
        a, b = c1[:, s:s + 1], s1[:, s:s + 1]
        tab_real = (a * c2 - b * s2).astype(BF16)
        tab_imag = (-(b * c2 + a * s2)).astype(BF16)
        re = jnp.concatenate([sent_ref[0, p, s] for p in range(slabs)], axis=0)
        im = jnp.concatenate([sent_ref[1, p, s] for p in range(slabs)], axis=0)
        real += dot(tab_real, re) + dot(tab_imag, im)
        imag += dot(tab_real, im) - dot(tab_imag, re)
    out_ref[0] = real * scale
    out_ref[1] = imag * scale


def adjoint(first, subs, sent, local):
    _, slabs, count, band, width = sent.shape
    tile = min(local, 256)
    return pl.pallas_call(
        functools.partial(adjoint_kernel, 1.0 / math.sqrt(count * SG), slabs),
        grid=(local // tile,),
        in_specs=[
            pl.BlockSpec(memory_space=pltpu.SMEM),
            pl.BlockSpec((1, count), lambda i: (0, 0)),
            pl.BlockSpec((2, slabs, count, band, width), lambda i: (0, 0, 0, 0, 0)),
        ],
        out_specs=pl.BlockSpec((2, tile, width), lambda i: (0, i, 0)),
        out_shape=jax.ShapeDtypeStruct((2, local, width), F32),
        name="adjoint",
    )(first, subs[None, :], sent)


def fused_kernel(
    scale, offset_ref, subs_hbm, slab_hbm, cell_hbm, value_hbm, weight_hbm,
    residual_ref, update_ref, last_ref, table,
    subs_ref, slab_ref, cell_ref, value_ref, weight_ref, low, high, acc, pb, rp, cb, rx, dg, zd, zf, zb, rz, sums, flat, full,
    turn, load,
    p_send, p_recv, x_send, x_recv, d_send, d_recv, z_send, z_recv, gz_send, gz_recv, gx_send, gx_recv, gc_send, gc_recv,
):
    facets, slabs = lax.axis_size("facet"), lax.axis_size("slab")
    q, z = lax.axis_index("facet"), lax.axis_index("slab")
    core, chip = q % 2, q // 2
    chips = facets // 2
    partner = q + 1 - 2 * core
    _, local, width = slab_ref.shape
    band = SG // slabs
    groups = band // 16
    parts = x_send.shape[1]
    share = band // parts
    dot = functools.partial(jnp.dot, preferred_element_type=F32)

    def at_chip(d):
        return 2 * (chip ^ d) + core

    def remote(src, dst, send, recv, **where):
        return pltpu.make_async_remote_copy(
            src_ref=src, dst_ref=dst, send_sem=send, recv_sem=recv,
            device_id=where, device_id_type=pl.DeviceIdType.MESH,
        )

    barrier = pltpu.get_barrier_semaphore()
    for e in range(1, slabs):
        pl.semaphore_signal(barrier, inc=1, device_id={"slab": z ^ e}, device_id_type=pl.DeviceIdType.MESH)
    for d in range(1, chips):
        pl.semaphore_signal(barrier, inc=1, device_id={"facet": at_chip(d)}, device_id_type=pl.DeviceIdType.MESH)
    pl.semaphore_signal(barrier, inc=1, device_id={"facet": partner}, device_id_type=pl.DeviceIdType.MESH)
    loads = [
        pltpu.make_async_copy(src, dst, load.at[i])
        for i, (src, dst) in enumerate(
            [
                (subs_hbm, subs_ref), (slab_hbm, slab_ref),
                (cell_hbm, cell_ref), (value_hbm, value_ref), (weight_hbm, weight_ref),
            ]
        )
    ]
    for copy in loads:
        copy.start()

    loads[0].wait()
    first = offset_ref[0] + z * local
    line = lax.broadcasted_iota(jnp.int32, (16, local), 1)

    places = line + first
    c, n = cis(UVSTEP * lax.broadcasted_iota(jnp.int32, (16, local), 0) * places)
    low[0] = c
    low[1] = n

    def partial_sum(i, other):
        row = lax.broadcasted_iota(jnp.int32, (chips * groups, local), 0)
        freq = UVSTEP * (band * (z ^ (slabs - 1 - i)) + 16 * (row % groups))
        for d in range(chips):
            freq += jnp.where(row // groups == d, subs_ref[at_chip(d) ^ other], 0)
        c, n = cis(freq * places[0:1])
        high[0] = c
        high[1] = n
        c2, s2 = low[0], low[1]
        cos, sin = [], []
        for g in range(chips * groups):
            c1, s1 = high[0, g:g + 1], high[1, g:g + 1]
            cos.append((c1 * c2 - s1 * s2).astype(BF16))
            sin.append((s1 * c2 + c1 * s2).astype(BF16))
        cos = jnp.concatenate(cos, axis=0)
        sin = jnp.concatenate(sin, axis=0)
        data = slab_ref[...].reshape(2 * local, width)
        real = dot(jnp.concatenate([cos, sin], axis=1), data)
        imag = dot(jnp.concatenate([-sin, cos], axis=1), data)
        return real, imag

    def pair_copy(i):
        return remote(pb.at[i], rp.at[i], p_send.at[i], p_recv.at[i], facet=partner)

    def part(h):
        return slice(h * share, (h + 1) * share)

    def x_copy(i, h, d):
        return remote(
            cb.at[i, d - 1, :, part(h)], rx.at[i, d - 1, :, part(h)],
            x_send.at[i, h, d - 1], x_recv.at[i, h, d - 1], facet=at_chip(d),
        )

    own, far = slabs - 1, chips - 1

    def routed(i):
        return i % 2 == 0

    def d_copy(i, h):
        return remote(
            cb.at[i, far - 1, :, part(h)], zd.at[i // 2, :, part(h)], d_send.at[i // 2, h], d_recv.at[i // 2, h],
            slab=z ^ (own - i),
        )

    def ways(i):
        return [d for d in range(far, 0, -1) if d != far or not routed(i)]

    def x_send_part(i, h):
        for d in ways(i):
            if i != own or d != far:
                x_copy(i, h, d).start()

    def pair_band(i, mine):
        pair_copy(i).wait_recv()
        for d in range(far, 0, -1):
            at = slice(d * band, (d + 1) * band)
            for c in range(2):
                total = acc[i, c, at] + rp[i, c, at].astype(F32)
                if mine and d == far:
                    dg[c] = total
                else:
                    cb[i, d - 1, c] = total.astype(BF16)
        if not mine and routed(i):
            for h in range(parts):
                d_copy(i, h).start()
        elif not mine:
            x_copy(i, 0, far).start()
        for d in range(far - 1, 0, -1):
            x_copy(i, 0, d).start()
        for c in range(2):
            zf[i, c] = acc[i, c, 0:band] + rp[i, c, 0:band].astype(F32)

    def send_far(h):
        for i in range(0, own, 2):
            d_copy(i, h).wait()
        for c in range(2):
            total = dg[c, part(h)]
            for k in range(slabs // 2):
                total += zd[k, c, part(h)].astype(F32)
            cb[own, far - 1, c, part(h)] = total.astype(BF16)
        x_copy(own, h, far).start()

    loads[1].wait()
    for i in range(slabs):
        for c, half in enumerate(partial_sum(i, 1)):
            pb[i, c] = half.astype(BF16)
        if i == 0:
            pl.semaphore_wait(barrier, chips + slabs - 1)
        pair_copy(i).start()
        if i > 0:
            pair_band(i - 1, False)
        for c, half in enumerate(partial_sum(i, 0)):
            acc[i, c] = half
    pair_band(own, True)
    for i in range(own - 1):
        x_send_part(i, 1)

    rows = sums.shape[1] // 3
    count = cell_ref.shape[1]
    chunk = min(count, GRID)
    for copy in loads[2:]:
        copy.wait()
    sums[...] = jnp.zeros_like(sums)

    def grid_step(i, carry):
        at = pl.ds(pl.multiple_of(i * chunk, chunk), chunk)
        cell = cell_ref[:, at]
        weight = weight_ref[:, at]
        row = lax.shift_right_logical(cell, width.bit_length() - 1).astype(F32)
        col = (cell & (width - 1)).astype(F32)
        lines = lax.broadcasted_iota(jnp.int32, (16, chunk), 0).astype(F32).astype(BF16)
        row = jnp.broadcast_to(row, (16, chunk)).astype(BF16)
        col = jnp.broadcast_to(col, (16, chunk)).astype(BF16)
        one, zero = jnp.ones((16, chunk), BF16), jnp.zeros((16, chunk), BF16)
        hot = jnp.concatenate(
            [jnp.where(col == lines + jnp.asarray(g, BF16), one, zero) for g in range(0, width, 16)], axis=0
        )
        terms = [weight * value_ref[0, :, at], weight * value_ref[1, :, at], weight]
        terms = [jnp.broadcast_to(t, (16, chunk)).astype(BF16) for t in terms]
        left = jnp.concatenate(
            [jnp.where(row == lines + jnp.asarray(g, BF16), t, zero) for t in terms for g in range(0, rows, 16)],
            axis=0,
        )
        sums[...] += lax.dot_general(hot, left, (((1,), (1,)), ((), ())), preferred_element_type=F32)
        return carry

    span = facets * share

    def table_band(t, carry):
        e, h = t // parts, t % parts
        lane = lax.broadcasted_iota(jnp.int32, (16, span), 1)
        freq = UVSTEP * (band * (z ^ e) + share * h + lane % share)
        for s in range(facets):
            freq += jnp.where(lane // share == s, subs_ref[s], 0)
        c2, s2 = cis(freq * lax.broadcasted_iota(jnp.int32, (16, span), 0))
        far = first + 16 * lax.broadcasted_iota(jnp.int32, (local // 16, span), 0)
        c, n = cis(freq[0:1] * far)
        turn[0] = c
        turn[1] = n

        def step(g, inner):
            c1, s1 = turn[0, pl.ds(g, 1)], turn[1, pl.ds(g, 1)]
            sin = (s1 * c2 + c1 * s2).astype(BF16)
            at = pl.ds(pl.multiple_of(g * 16, 16), 16)
            into = table.at[e, h]
            into[at, 0:span] = sin
            into[at, span:2 * span] = (c1 * c2 - s1 * s2).astype(BF16)
            into[at, 2 * span:3 * span] = -sin
            return inner

        lax.fori_loop(0, local // 16, step, 0)
        return carry

    chunks = count // chunk

    def z_copy(i, h):
        return remote(
            zb.at[i, :, part(h)], rz.at[i, :, part(h)], z_send.at[i, h], z_recv.at[i, h], slab=z ^ (slabs - 1 - i)
        )

    def reduce_part(i, h):
        for d in ways(i):
            x_copy(i, h, d).wait()
        for c in range(2):
            total = zf[i, c, part(h)]
            for d in ways(i):
                total += rx[i, d - 1, c, part(h)].astype(F32)
            if i < slabs - 1:
                zb[i, c, part(h)] = total.astype(BF16)
            else:
                zf[i, c, part(h)] = total
        if i < slabs - 1:
            z_copy(i, h).start()

    def residual_part(h):
        for i in range(slabs - 1):
            z_copy(i, h).wait()
        for c in range(2):
            model = zf[slabs - 1, c, part(h)]
            for i in range(slabs - 1):
                model += rz[i, c, part(h)].astype(F32)
            at = h * share
            piece = flat[c * rows + at:c * rows + at + share]
            piece -= flat[2 * rows + at:2 * rows + at + share] * (model * scale)
            residual_ref[c, part(h)] = piece
            full[0, h, c, q] = piece.astype(BF16)

    def up_copy(e, h):
        return remote(
            full.at[0, h, :, q], full.at[e, h, :, q], gz_send.at[e - 1, h], gz_recv.at[e - 1, h],
            slab=z ^ e,
        )

    def across_copy(e, h, d):
        ref = full.at[e, h, :, q]
        return remote(ref, ref, gx_send.at[e, h, d - 1], gx_recv.at[e, h, d - 1], facet=at_chip(d))

    def spread_copy(e, h, d):
        ref = full.at[e, h, :, at_chip(d)]
        return remote(ref, ref, gc_send.at[e, h, d], gc_recv.at[e, h, d], facet=partner)

    def hand_on(e, h):
        if e:
            up_copy(e, h).wait_recv()
        else:
            for away in order[1:]:
                up_copy(away, h).start()
        for d in range(chips - 1, 0, -1):
            across_copy(e, h, d).start()
        spread_copy(e, h, 0).start()

    def relay(e, h):
        for d in range(1, chips):
            across_copy(e, h, d).wait_recv()
            spread_copy(e, h, d).start()

    tile = min(local, TILE)

    def gathered(e, h):
        for d in range(chips):
            spread_copy(e, h, d).wait_recv()

    order = [k ^ (k >> 1) for k in range(slabs)]
    last = order[-1]
    units = slabs * parts

    def looped(count, work, before, after):
        def step(k, carry):
            for at, events in before.items():
                @pl.when(k == at)
                def _():
                    for event in events:
                        event()
            work(k)
            for at, events in after.items():
                @pl.when(k == at)
                def _():
                    for event in events:
                        event()
            return carry

        lax.fori_loop(0, count, step, 0)

    def update_pass(k):
        j, h = k % slabs, k // slabs
        e = j ^ lax.shift_right_logical(j, 1)
        gathered(e, h)

        def step(i, carry):
            at = pl.ds(pl.multiple_of(i * tile, tile), tile)
            data = full[e, h].reshape(2 * span, width)
            update_ref[1, at] += dot(table[e, h, at, 0:2 * span], data)
            update_ref[0, at] += dot(table[e, h, at, span:3 * span], data)
            return carry

        lax.fori_loop(0, local // tile, step, 0)

    def call(f, *args):
        return functools.partial(f, *args)

    reduce_part(0, 0)
    after = {}
    for i in range(1, own):
        after.setdefault(min(chunks - 1, i + GRID_LATE), []).append(call(reduce_part, i, 0))
        if i == 1:
            after[min(chunks - 1, i + GRID_LATE)] += [
                call(send_far, 0), call(x_send_part, own - 1, 1), call(x_send_part, own, 1)
            ]
    after.setdefault(max(chunks - 2, 0), []).extend([call(send_far, 1), call(reduce_part, 0, 1)])
    looped(chunks, lambda k: grid_step(k, 0), {}, after)
    flat[...] = sums[...].T
    update_ref[...] = jnp.zeros_like(update_ref)
    for i in range(1, own - 1):
        reduce_part(i, 1)
    reduce_part(own, 0)
    residual_part(0)
    hand_on(0, 0)
    reduce_part(own - 1, 1)
    middle = [call(hand_on, 1, 0), call(residual_part, 1), call(hand_on, 0, 1)]
    middle += [call(hand_on, e, 0) for e in order[2:-1]] + [call(relay, 0, 0)]
    looped(
        units, lambda t: table_band(t, 0), {},
        {1: [call(reduce_part, own, 1)], 2: middle, 4: [call(hand_on, last, 0)]},
    )
    hand_on(1, 1)
    relay(1, 0)
    before = {}
    for k, e in enumerate(order[2:]):
        before[k + 1] = [call(hand_on, e, 1), call(relay, e, 0)]
    before[slabs - 2] += [call(relay, 0, 1)]
    for k, e in enumerate(order[1:]):
        before[slabs + k] = [call(relay, e, 1)]
    looped(units - 1, update_pass, before, {})
    gathered(last, parts - 1)
    last_ref[...] = full[last, parts - 1]
    for i in range(slabs):
        pair_copy(i).wait_send()
    for e in range(slabs):
        for h in range(parts):
            if e:
                up_copy(e, h).wait_send()
            for d in range(chips):
                if d:
                    across_copy(e, h, d).wait_send()
                spread_copy(e, h, d).wait_send()


def finish_kernel(back, piece_ref, part_ref, last_ref, table_ref, residual_ref, update_ref, buffer, sent):
    dot = functools.partial(jnp.dot, preferred_element_type=F32)
    _, local, width = part_ref.shape
    slabs, parts, _, span = table_ref.shape
    span //= 3
    last = (slabs - 1) ^ ((slabs - 1) >> 1)
    tiles, _, tile, _ = buffer.shape
    out = pltpu.make_async_copy(piece_ref, residual_ref, sent.at[2 * tiles])
    out.start()

    def put(i, c):
        at = pl.ds(i * tile, tile)
        return pltpu.make_async_copy(buffer.at[i, c], update_ref.at[c, at], sent.at[2 * i + c])

    def step(i, carry):
        at = pl.ds(i * tile, tile)
        data = last_ref[...].reshape(2 * span, width)
        real = dot(table_ref[last, parts - 1, at, span:3 * span], data)
        buffer[i, 0] = (real + part_ref[0, at]) * back
        put(i, 0).start()
        imag = dot(table_ref[last, parts - 1, at, 0:2 * span], data)
        buffer[i, 1] = (imag + part_ref[1, at]) * back
        put(i, 1).start()
        return carry

    for i in range(tiles):
        step(i, 0)
    for i in range(tiles):
        for c in range(2):
            put(i, c).wait()
    out.wait()


def fused(offset, subs, slab, cells, values, weights, slabs, facets):
    _, local, width = slab.shape
    band = SG // slabs
    chips = facets // 2
    rows = -(-band // 16) * 16
    vmem = pl.BlockSpec(memory_space=pltpu.VMEM)
    dma = pltpu.SemaphoreType.DMA
    parts = 2
    share = band // parts
    span = facets * share
    piece, part, last, last_table = pl.pallas_call(
        functools.partial(fused_kernel, 1.0 / math.sqrt(local * slabs * facets)),
        in_specs=[pl.BlockSpec(memory_space=pltpu.SMEM)] + [pl.BlockSpec(memory_space=pltpu.HBM)] * 5,
        out_specs=[vmem] * 4,
        out_shape=[
            jax.ShapeDtypeStruct((2, band, width), F32),
            jax.ShapeDtypeStruct((2, local, width), F32),
            jax.ShapeDtypeStruct((2, facets, share, width), BF16),
            jax.ShapeDtypeStruct((slabs, parts, local, 3 * span), BF16),
        ],
        scratch_shapes=[
            pltpu.SMEM(subs.shape, jnp.int32),
            pltpu.VMEM((2, local, width), BF16),
            pltpu.VMEM(cells.shape, jnp.int32),
            pltpu.VMEM(values.shape, F32),
            pltpu.VMEM(weights.shape, F32),
            pltpu.VMEM((2, 16, local), F32),
            pltpu.VMEM((2, chips * (band // 16), local), F32),
            pltpu.VMEM((slabs, 2, chips * band, width), F32),
            pltpu.VMEM((slabs, 2, chips * band, width), BF16),
            pltpu.VMEM((slabs, 2, chips * band, width), BF16),
            pltpu.VMEM((slabs, chips - 1, 2, band, width), BF16),
            pltpu.VMEM((slabs, chips - 1, 2, band, width), BF16),
            pltpu.VMEM((2, band, width), F32),
            pltpu.VMEM((slabs // 2, 2, band, width), BF16),
            pltpu.VMEM((slabs, 2, band, width), F32),
            pltpu.VMEM((slabs - 1, 2, band, width), BF16),
            pltpu.VMEM((slabs - 1, 2, band, width), BF16),
            pltpu.VMEM((width, 3 * rows), F32),
            pltpu.VMEM((3 * rows, width), F32),
            pltpu.VMEM((slabs, parts, 2, facets, share, width), BF16),
            pltpu.VMEM((2, local // 16, span), F32),
            dma((5,)),
            dma((slabs,)), dma((slabs,)),
            dma((slabs, parts, chips - 1)), dma((slabs, parts, chips - 1)),
            dma((slabs // 2, parts)), dma((slabs // 2, parts)),
            dma((slabs - 1, parts)), dma((slabs - 1, parts)),
            dma((slabs - 1, parts)), dma((slabs - 1, parts)),
            dma((slabs, parts, chips - 1)), dma((slabs, parts, chips - 1)),
            dma((slabs, parts, chips)), dma((slabs, parts, chips)),
        ],
        compiler_params=pltpu.CompilerParams(collective_id=0, has_side_effects=True, vmem_limit_bytes=36 * 1024 * 1024),
        name="fused",
    )(offset, *[pltpu.with_memory_space_constraint(x, pltpu.HBM) for x in (subs, slab, cells, values, weights)])
    tiles = local // min(local, 256)
    return pl.pallas_call(
        functools.partial(finish_kernel, 1.0 / math.sqrt(subs.shape[0] * SG)),
        in_specs=[vmem] * 4,
        out_specs=[pl.BlockSpec(memory_space=pltpu.HBM)] * 2,
        out_shape=[
            jax.ShapeDtypeStruct((2, band, width), F32),
            jax.ShapeDtypeStruct((2, local, width), F32),
        ],
        scratch_shapes=[pltpu.VMEM((tiles, 2, local // tiles, width), F32), dma((2 * tiles + 1,))],
        compiler_params=pltpu.CompilerParams(vmem_limit_bytes=8 * 1024 * 1024),
        name="finish",
    )(piece, part, last, last_table)


def body(slab, facet_offset, subgrid_offset, vis_cell, vis_value, vis_weight):
    slabs = lax.axis_size("slab")
    facets = lax.axis_size("facet")
    local_rows = slab.shape[2]
    width = slab.shape[3]
    count_sub = subgrid_offset.shape[0]
    band = SG // slabs
    owned = count_sub * band // facets
    first = (facet_offset + lax.axis_index("slab") * local_rows).astype(jnp.int32)
    chips = facets // 2
    paired = facets == 2 * chips and chips == 4 and slabs > 2 and slabs & (slabs - 1) == 0
    if owned == band and count_sub == facets and paired and band % 32 == 0 and local_rows % 256 == 0:
        residual, update = fused(
            facet_offset, subgrid_offset, slab[:, 0], vis_cell[0], vis_value[:, 0], vis_weight[0], slabs, facets
        )
        return (residual.reshape(2, 1, owned, width), update.reshape(2, 1, local_rows, width))
    sums = grid_visibilities(vis_cell[0], vis_value[:, 0, 0], vis_weight[0], owned, width)
    contrib = forward(first, subgrid_offset, slab[:, 0], slabs)
    contrib = contrib.reshape(2, slabs, facets, owned, width)
    parts = lax.all_to_all(contrib, "facet", 2, 2, tiled=True)
    parts = jnp.sum(parts, axis=2, dtype=F32).astype(BF16)
    parts = lax.all_to_all(parts, "slab", 1, 1, tiled=True)
    scale = 1.0 / math.sqrt(local_rows * slabs * facets)
    model = jnp.sum(parts, axis=1, dtype=F32) * scale
    residual = sums[:2] - sums[2:] * model
    sent = residual.astype(BF16).reshape(2, 1, 1, owned, width)
    piece = lax.all_gather(sent, "slab", axis=1, tiled=True)
    piece = lax.all_gather(piece, "facet", axis=2, tiled=True)
    piece = piece.reshape(2, slabs, count_sub, band, width)
    update = adjoint(first, subgrid_offset, piece, local_rows)
    return (residual.reshape(2, 1, owned, width), update.reshape(2, 1, local_rows, width))


def solution(mesh):
    placed = (
        P(None, "facet", "slab", None),
        P("facet"),
        P(),
        P("slab", "facet", None),
        P(None, "slab", "facet", None),
        P("slab", "facet", None),
    )
    return jax.shard_map(
        body,
        mesh=mesh,
        in_specs=placed,
        out_specs=(P(None, "slab", "facet", None), P(None, "facet", "slab", None)),
        check_vma=False,
    )
```
